32 devices in a mesh: groups: 2 (over y), bricks: 4 (over z), chan: 2 (over x), rep: 2 (over core).
Axes of the slice: x: 2, y: 2, z: 4, core: 2. Of those that a mesh axis runs over, the one named last changes fastest.
Arguments:
- features: bfloat16 [16, 64, 8, 24, 128], P(('groups', 'bricks', 'rep')), parts along dimension 0, may hold values from -6 to 6
- w_first: bfloat16 [27, 64, 64], P(None, None, 'chan'), may hold values from -0.15625 to 0.15625
- w_second: bfloat16 [27, 64, 64], P(None, None, 'chan'), may hold values from -0.15625 to 0.15625
- w_down: bfloat16 [8, 64, 64], P(None, 'chan'), may hold values from -0.25 to 0.25
- w_head: float32 [64], replicated, may hold values from -0.75 to 0.75
- footprint: int32 [2, 16], P(None, 'groups'), parts along dimension 1, may hold values from 0 to 3, as said below
- labels: int32 [16, 4, 768], P(('groups', 'bricks', 'rep')), parts along dimension 0, may hold values 0 or 1
Outputs:
- grad_second: float32 [54, 64, 64], P('groups', None, 'chan'), parts along dimension 0
- grad_down: float32 [16, 64, 64], P('groups', 'chan'), parts along dimension 0
- grad_head: float32 [128], P('groups'), parts along dimension 0
- loss: float32 [2], P('groups'), parts along dimension 0
The draws below stay inside these ranges and needn't reach their ends.
There are 2 independent parts, one for each index of `groups`. The reference program is written for one: setup_inputs(seed, part) draws one part's arguments, and reference() takes and returns one part's arrays. A program takes and returns all parts, laid end to end along the dimension named above; an argument that names none is the same for every part. Nothing has to cross between parts.
Inputs may be any that keep to these rules, and one draw needn't show every extreme that they name: `footprint`: row 0 gives each column's first live brick row, 0 or 1; row 1 its number of live bricks. Columns 2k and 2k + 1 hold 2 to 4 live bricks together, and some column holds 3.
All inputs are finite; a program needn't handle non-finite values. No bound on the sum of `labels` on one device may be relied on, other than what follows from the above.
Results may differ from the reference program's by a relative error of at most 0.0035.
Values may be sent and summed in bfloat16 or wider, within the bound.
No kernel may reach another device: no remote copies, remote signals or barrier semaphores. Data moves between devices by JAX's collectives and lax.ppermute only.
A program may use at most 128 MiB of HBM per device.

```python
import jax
import jax.numpy as jnp
from jax import lax

CHANNELS = 64
BRICK = 8
DEPTH = 128
SLOTS = 3
COLUMNS = 8
ROWS = 4
COARSE = 1024


def draw_footprint(key, part):
    pair_count = COLUMNS // 2
    subkeys = jax.random.split(jax.random.fold_in(key, 17), 5)
    totals = jax.random.randint(subkeys[0], (pair_count,), 2, 2 * SLOTS - 1)
    lowest = jnp.maximum(totals - SLOTS, 0)
    highest = jnp.minimum(totals, SLOTS)
    picks = jax.random.randint(subkeys[1], (pair_count,), 0, 1 << 20)
    firsts = lowest + picks % (highest - lowest + 1)
    chosen = jax.random.randint(subkeys[2], (), 0, pair_count)
    heavy_side = jax.random.randint(subkeys[3], (), 0, 2)
    marked = jnp.arange(pair_count) == chosen
    totals = jnp.where(marked, 2 * SLOTS - 2, totals)
    firsts = jnp.where(marked, jnp.where(heavy_side == 0, SLOTS, SLOTS - 2), firsts)
    heights = jnp.stack([firsts, totals - firsts], axis=1).reshape(COLUMNS)
    starts = jax.random.randint(subkeys[4], (COLUMNS,), 0, 2)
    return jnp.stack([starts, heights]).astype(jnp.int32)


def plant(values, rng, least, largest):
    spot = [jax.random.randint(jax.random.fold_in(rng, axis), (), 0, length) for axis, length in enumerate(values.shape)]
    widest = values.shape.index(max(values.shape))
    next_to = spot[:widest] + [(spot[widest] + 1) % values.shape[widest]] + spot[widest + 1:]
    return values.at[tuple(spot)].set(least).at[tuple(next_to)].set(largest)


def block_scale(key, shape, pieces, least, high):
    def one(position, parts):
        steps = jax.random.uniform(jax.random.fold_in(jax.random.fold_in(key, 6), position), (parts,), jnp.float32, least / len(pieces), high / len(pieces))
        return jnp.repeat(jnp.exp(steps), shape[position] // parts).reshape((-1,) + (1,) * (len(shape) - position - 1))

    loudness = one(*pieces[0])
    for cut in pieces[1:]:
        loudness = loudness * one(*cut)
    return loudness


def gaussian(own_key, shape, width, bound, cuts=(), held_as=jnp.bfloat16):
    entries = width * jax.random.normal(own_key, shape, jnp.float32)
    if cuts:
        entries = entries * block_scale(own_key, shape, cuts, -0.22, 0.18)
    return jnp.clip(entries, -bound, bound).astype(held_as)


def setup_inputs(seed: int = 0, part: int = 0) -> dict:
    keys = jax.random.split(jax.random.key(seed), 8)
    part_splits = jax.random.split(jax.random.fold_in(keys[7], part), 8)
    features = gaussian(part_splits[0], (COLUMNS, CHANNELS, BRICK, SLOTS * BRICK, DEPTH), 1.0, 6.0, ((0, 8),))
    w_first = gaussian(keys[1], (27, CHANNELS, CHANNELS), (27 * CHANNELS) ** -0.5, 0.15625, ((2, 2),))
    w_second = gaussian(keys[2], (27, CHANNELS, CHANNELS), (27 * CHANNELS) ** -0.5, 0.15625, ((2, 2),))
    w_down = gaussian(keys[3], (8, CHANNELS, CHANNELS), (8 * CHANNELS) ** -0.5, 0.25, ((1, 2),))
    w_head = gaussian(keys[4], (CHANNELS,), CHANNELS ** -0.5, 0.75, (), jnp.float32)
    footprint = draw_footprint(jax.random.fold_in(jax.random.fold_in(keys[7], part), 71), part)
    labels = plant((jax.random.randint(part_splits[6], (COLUMNS, BRICK // 2, SLOTS * (BRICK // 2) * (DEPTH // 2)), 0, 8) < 1).astype(jnp.int32), jax.random.fold_in(part_splits[6], 1), 0, 1)
    return dict(features=features, w_first=w_first, w_second=w_second, w_down=w_down, w_head=w_head, footprint=footprint, labels=labels)


def conv_ref(window, weight, dilation):
    kernel = weight.astype(jnp.float32).reshape(3, 3, 3, weight.shape[1], weight.shape[2])
    return lax.conv_general_dilated(window.astype(jnp.float32), kernel, (1, 1, 1), ((0, 0), (0, 0), (dilation, dilation)), rhs_dilation=(dilation, dilation, dilation), dimension_numbers=("NCDHW", "DHWIO", "NCDHW"), precision=lax.Precision.HIGHEST)


def kernel_grad_ref(window, delta_bf, dilation):
    raw_grad = lax.conv_general_dilated(window.astype(jnp.float32), delta_bf.astype(jnp.float32), (dilation, dilation, dilation), ((0, 0), (0, 0), (dilation, dilation)), dimension_numbers=("CNDHW", "IODHW", "NCDHW"), precision=lax.Precision.HIGHEST)
    return raw_grad.transpose(2, 3, 4, 0, 1).reshape(27, raw_grad.shape[0], raw_grad.shape[1])


def down_ref(fine_out, weight):
    kernel = weight.astype(jnp.float32).reshape(2, 2, 2, weight.shape[1], weight.shape[2])
    return lax.conv_general_dilated(fine_out.astype(jnp.float32), kernel, (2, 2, 2), "VALID", dimension_numbers=("NCDHW", "DHWIO", "NCDHW"), precision=lax.Precision.HIGHEST)


def down_grad_ref(fine_out, delta_bf):
    raw_grad = lax.conv_general_dilated(fine_out.astype(jnp.float32), delta_bf.astype(jnp.float32), (1, 1, 1), "VALID", rhs_dilation=(2, 2, 2), dimension_numbers=("CNDHW", "IODHW", "NCDHW"), precision=lax.Precision.HIGHEST)
    return raw_grad.transpose(2, 3, 4, 0, 1).reshape(8, raw_grad.shape[0], raw_grad.shape[1])


def down_back_ref(delta_bf, weight):
    kernel = weight.astype(jnp.float32).reshape(2, 2, 2, weight.shape[1], weight.shape[2])[::-1, ::-1, ::-1]
    return lax.conv_general_dilated(delta_bf.astype(jnp.float32), kernel, (1, 1, 1), ((1, 1), (1, 1), (1, 1)), lhs_dilation=(2, 2, 2), dimension_numbers=("NCDHW", "DHWOI", "NCDHW"), precision=lax.Precision.HIGHEST)


def brick_terms(window, margin_mask, target, w_first, w_second, w_down, w_head):
    first_out = conv_ref(window[None], w_first, 2)
    hidden = lax.optimization_barrier((jnp.maximum(first_out, 0.0) * margin_mask[None, None, :, :, None]).astype(jnp.bfloat16))
    second = conv_ref(hidden, w_second, 2)
    fine_out = lax.optimization_barrier(jnp.maximum(second, 0.0).astype(jnp.bfloat16))
    coarse_five = down_ref(fine_out, w_down)
    five_shape = coarse_five.shape
    coarse = coarse_five.reshape(five_shape[0], five_shape[1], five_shape[2], -1)
    rectified = jnp.maximum(coarse, 0.0)
    head_weights = w_head.astype(jnp.float32)
    logits = jnp.einsum("c,ncxw->nxw", head_weights, rectified)
    targets = target[None]
    loss_part = jnp.sum(jax.nn.softplus(logits) - targets * logits)
    slope_map = (jax.nn.sigmoid(logits) - targets) / COARSE
    head_part = jnp.einsum("nxw,ncxw->c", slope_map, rectified)
    delta_bf = lax.optimization_barrier((slope_map[:, None] * head_weights[None, :, None, None] * (coarse > 0.0)).astype(jnp.bfloat16))
    delta_bf = delta_bf.reshape(five_shape)
    down_part = down_grad_ref(fine_out, delta_bf)
    error_bf = lax.optimization_barrier((down_back_ref(delta_bf, w_down) * (second > 0.0)).astype(jnp.bfloat16))
    second_part = kernel_grad_ref(hidden, error_bf, 2)
    return second_part, down_part, head_part, loss_part


def reference(features, w_first, w_second, w_down, w_head, footprint, labels):
    starts = footprint[0].astype(jnp.int32)
    heights = footprint[1].astype(jnp.int32)
    col_count = features.shape[0]
    channels = features.shape[1]
    frame_rows = ROWS * BRICK
    padded = jnp.pad(features, ((0, 0), (0, 0), (0, 0), (BRICK, BRICK), (0, 0)))
    zero = jnp.zeros((), jnp.int32)

    def place(column_slab, first_row):
        return lax.dynamic_slice_in_dim(column_slab, ((1 - first_row) * BRICK).astype(jnp.int32), frame_rows, 2)

    placed = jax.vmap(place)(padded, starts)
    row_ids = jnp.arange(frame_rows, dtype=jnp.int32) // BRICK
    alive = (row_ids[None, :] >= starts[:, None]) & (row_ids[None, :] < (starts + heights)[:, None])
    placed = placed * alive[:, None, None, :, None].astype(placed.dtype)
    volume = placed.transpose(1, 0, 2, 3, 4).reshape(channels, col_count * BRICK, frame_rows, DEPTH)
    volume = jnp.pad(volume, ((0, 0), (4, 4), (4, 4), (0, 0)))
    livemap = jnp.pad(jnp.repeat(alive.astype(jnp.float32), BRICK, axis=0), 4)
    slot_cells = labels.shape[2] // SLOTS

    def visit(carry, item):
        column = (item // SLOTS).astype(jnp.int32)
        slot_index = (item % SLOTS).astype(jnp.int32)
        brick_row = (starts[column] + slot_index).astype(jnp.int32)
        col_cell = (column * BRICK).astype(jnp.int32)
        row_cell = (brick_row * BRICK).astype(jnp.int32)
        window = lax.dynamic_slice(volume, (zero, col_cell, row_cell, zero), (channels, BRICK + 8, BRICK + 8, DEPTH))
        margin_mask = lax.dynamic_slice(livemap, ((col_cell + 2).astype(jnp.int32), (row_cell + 2).astype(jnp.int32)), (BRICK + 4, BRICK + 4))
        target = lax.dynamic_slice_in_dim(labels[column], (slot_index * slot_cells).astype(jnp.int32), slot_cells, 1).astype(jnp.float32)

        def compute():
            return brick_terms(window, margin_mask, target, w_first, w_second, w_down, w_head)

        def nothing():
            return (jnp.zeros((27, channels, channels), jnp.float32), jnp.zeros((8, channels, channels), jnp.float32), jnp.zeros((channels,), jnp.float32), jnp.zeros((), jnp.float32))

        terms = lax.cond(slot_index < heights[column], compute, nothing)
        return tuple(total + term for total, term in zip(carry, terms)), None

    initial = (jnp.zeros((27, channels, channels), jnp.float32), jnp.zeros((8, channels, channels), jnp.float32), jnp.zeros((channels,), jnp.float32), jnp.zeros((), jnp.float32))
    totals, unused = lax.scan(visit, initial, jnp.arange(col_count * SLOTS, dtype=jnp.int32))
    live_count = jnp.sum(heights).astype(jnp.float32)
    loss = (totals[3] / (COARSE * live_count)).reshape(1)
    return totals[0], totals[1], totals[2], loss
```

```python
import functools

import jax
import jax.numpy as jnp
from jax import lax
from jax.experimental import pallas as pl
from jax.experimental.pallas import tpu as pltpu
from jax.sharding import PartitionSpec as P

BRICK = 8
COARSE = 1024
ROWS = 256
F32 = jnp.float32
BF16 = jnp.bfloat16


def lanes_low(shape):
    return lax.broadcasted_iota(jnp.int32, shape, len(shape) - 1) % 128 < 64


def merge_half(low, high):
    return jnp.where(lanes_low(low.shape), low, high)


def shifted(value, by):
    row = lax.broadcasted_iota(jnp.int32, value.shape, 0) % 128
    inside = row >= by if by > 0 else row < 128 + by
    return jnp.where(inside, pltpu.roll(value, by % value.shape[0], 0), 0.0)


def build_conv(w_ref, out_ref):
    zero = jnp.zeros((64, 128), BF16)
    for e in range(3):
        for k in range(4):
            for slot, d in enumerate((0, 1, 2, -1)):
                for rx in range(2):
                    a = k - rx
                    halves = []
                    for ry in range(2):
                        b = d - ry + 1
                        live = 0 <= a < 3 and 0 <= b < 3
                        halves.append(w_ref[9 * a + 3 * b + e] if live else zero)
                    row = k * 256 + slot * 64
                    out_ref[e, row : row + 64, rx * 128 : rx * 128 + 128] = merge_half(*halves)


def conv_block(window_ref, slot, par, w_ref):
    lhs = jnp.concatenate([window_ref[slot, 2 * k + par] for k in range(4)], axis=1)
    below, level, above = [jnp.dot(lhs, w_ref[e], preferred_element_type=F32) for e in range(3)]
    return level + shifted(below, 2) + shifted(above, -2)


def gated(ref, plane, index, count):
    inside = (index >= 0) & (index < count)
    block = ref[plane, jnp.clip(index, 0, ref.shape[1] - 1)]
    return jnp.where(inside, block, jnp.zeros_like(block))


def fill_window(window_ref, slot, plane, src_ref, src_plane, index, count):
    window_ref[slot, plane, :, 0:128] = gated(src_ref, src_plane, index, count)
    window_ref[slot, plane, :, 128:256] = merge_half(
        gated(src_ref, src_plane, index + 1, count), gated(src_ref, src_plane, index - 1, count)
    )


def local_kernel(foot_ref, feat_ref, w1_ref, w2_ref, y1_ref, m1_ref, m2_ref, window):
    column = lax.axis_index("bricks") * lax.axis_size("rep") + lax.axis_index("rep")
    count = 2 * foot_ref[1, column]
    build_conv(w1_ref, m1_ref)
    build_conv(w2_ref, m2_ref)

    def fill(t, carry):
        for p in range(8):
            fill_window(window, t, p, feat_ref, p, t, count)
        return carry

    lax.fori_loop(0, count, fill, 0)

    def conv(t, carry):
        for par in range(2):
            out = jnp.maximum(conv_block(window, t, par, m1_ref), 0.0).astype(BF16)
            for rx in range(2):
                y1_ref[2 * rx + par, t] = out[:, 128 * rx : 128 * rx + 128]
        return carry

    lax.fori_loop(0, count, conv, 0)


def main_kernel(
    foot_ref,
    feat_ref,
    halo_ref,
    near_ref,
    m1_ref,
    m2_ref,
    wd_ref,
    wdt_ref,
    head_ref,
    headm_ref,
    label_ref,
    out_ref,
    window,
    hidden,
    hwin,
    down_mat,
    back_mat,
    y2_ref,
    delta_t,
    err_t,
    grad,
    grad_down,
    small,
):
    reps, chans = lax.axis_size("rep"), lax.axis_size("chan")
    columns = lax.axis_size("bricks") * reps
    column = lax.axis_index("bricks") * reps + lax.axis_index("rep")
    planes = BRICK // chans
    mine = lax.axis_index("chan") * planes
    side = mine // 4
    other = column + 2 * side - 1
    present = (other >= 0) & (other < columns)
    other = jnp.clip(other, 0, columns - 1)
    count = 2 * foot_ref[1, column]
    other_count = jnp.where(present, 2 * foot_ref[1, other], 0)
    offset = 2 * (foot_ref[0, other] - foot_ref[0, column])

    grad[...] = jnp.zeros_like(grad)
    grad_down[...] = jnp.zeros_like(grad_down)
    small[...] = jnp.zeros_like(small)
    low = lanes_low((64, 128))
    zero = jnp.zeros((64, 128), BF16)
    for t in range(8):
        ab, e = t // 2, t % 2
        for ry in range(2):
            keep = low if ry == 0 else ~low
            row = ab * 128 + ry * 64
            down_mat[row : row + 64, e * 128 : e * 128 + 128] = jnp.where(keep, wd_ref[t], zero)
            lane = ab * 256 + e * 128
            back_mat[ry * 64 : ry * 64 + 64, lane : lane + 128] = jnp.where(keep, wdt_ref[t], zero)

    def fill(slot, carry):
        t = slot - 1
        for p in range(4):
            fill_window(window, slot, (1 - side) * 4 + p, feat_ref, side * 4 + p, t, count)
            fill_window(window, slot, side * 4 + p, halo_ref, p, t - offset, other_count)
        return carry

    lax.fori_loop(0, count + 2, fill, 0)

    def first(slot, carry):
        t = slot - 1
        own = (t >= 0) & (t < count)
        next_to = (t - offset >= 0) & (t - offset < other_count)
        for par in range(2):
            out = jnp.maximum(conv_block(window, slot, par, m1_ref), 0.0).astype(BF16)
            for rx in range(2):
                live = jnp.where(side == rx, next_to, own)
                block = out[:, 128 * rx : 128 * rx + 128]
                hidden[slot, side * 4 + 2 * rx + par] = jnp.where(
                    live, block, jnp.zeros_like(block)
                )
        for p in range(4):
            hidden[slot, (1 - side) * 4 + p] = gated(near_ref, p, t, count)
        return carry

    lax.fori_loop(0, count + 2, first, 0)

    even = lax.broadcasted_iota(jnp.int32, (128, 128), 0) % 2 == 0
    head_row = head_ref[0:1, :]

    def second(t, carry):
        for p in range(8):
            hwin[p, :, 0:128] = hidden[t + 1, p]
            hwin[p, :, 128:256] = merge_half(hidden[t + 2, p], hidden[t, p])
        for par in range(2):
            lhs = jnp.concatenate([hwin[2 * k + par] for k in range(4)], axis=1)
            below, level, above = [
                jnp.dot(lhs, m2_ref[e], preferred_element_type=F32) for e in range(3)
            ]
            out = level + shifted(below, 2) + shifted(above, -2)
            out = jnp.maximum(out, 0.0).astype(BF16)
            for rx in range(2):
                y2_ref[rx, par] = out[:, 128 * rx : 128 * rx + 128]
        for rx in range(2):
            fine = jnp.concatenate(
                [y2_ref[rx, a, 128 * b : 128 * b + 128] for a in range(2) for b in range(2)], axis=1
            )
            both = jnp.dot(fine, down_mat[...], preferred_element_type=F32)
            coarse = both[:, 0:128] + shifted(both[:, 128:256], -1)
            rect = jnp.maximum(coarse, 0.0)
            logit = jnp.dot(
                rect, headm_ref[...], precision=lax.Precision.HIGHEST, preferred_element_type=F32
            )
            plane = 4 * side + 2 * rx
            keep = even & (plane >= mine) & (plane < mine + planes)
            label = label_ref[2 * side + rx, t].astype(F32)
            tail = jnp.exp(-jnp.abs(logit))
            soft = jnp.maximum(logit, 0.0) + jnp.log1p(tail)
            sigmoid = jnp.where(logit >= 0.0, 1.0, tail) / (1.0 + tail)
            loss = jnp.where(keep, soft - label * logit, 0.0)
            slope = jnp.where(keep, (sigmoid - label) * (1.0 / COARSE), 0.0)
            small[0:1] += jnp.sum(slope * rect, axis=0, keepdims=True)
            small[1:2] += jnp.sum(loss, axis=0, keepdims=True)
            delta = jnp.where(coarse > 0.0, slope * head_row, 0.0).astype(BF16).astype(F32)
            moved = shifted(delta, 1)
            delta_t[0:128, 128 * rx : 128 * rx + 128] = delta.T.astype(BF16)
            delta_t[128:256, 128 * rx : 128 * rx + 128] = moved.T.astype(BF16)
            spread = (delta + moved).astype(BF16)
            back = jnp.dot(spread, back_mat[...], preferred_element_type=F32)
            for a in range(2):
                for b in range(2):
                    lane = (2 * a + b) * 256
                    err = jnp.where(even, back[:, lane : lane + 128], back[:, lane + 128 : lane + 256])
                    live = y2_ref[rx, a, 128 * b : 128 * b + 128].astype(F32) > 0.0
                    err = jnp.where(live, err, 0.0)
                    col = (2 * rx + a) * 256 + b * 128
                    for e, by in enumerate((-2, 0, 2)):
                        value = shifted(err, by) if by else err
                        err_t[128 * e : 128 * e + 128, col : col + 128] = value.T.astype(BF16)
        fine = jnp.concatenate(
            [
                jnp.concatenate([y2_ref[rx, a, 128 * b : 128 * b + 128] for rx in range(2)], axis=0)
                for a in range(2)
                for b in range(2)
            ],
            axis=1,
        )
        grad_down[...] += jnp.dot(delta_t[...], fine, preferred_element_type=F32)
        for a in range(3):
            rows = hwin[2 * a : 2 * a + 4].reshape(4 * ROWS, 256)
            grad[a] += jnp.dot(err_t[...], rows, preferred_element_type=F32)
        return carry

    lax.fori_loop(0, count, second, 0)

    low = lanes_low((64, 128))
    firsts = []
    for a in range(3):
        for e in range(3):
            both = grad[a, 128 * e : 128 * e + 64] + pltpu.roll(
                grad[a, 128 * e + 64 : 128 * e + 128], 192, 1
            )
            out_ref[3 * a + e] = both[:, 0:128]
            firsts.append(both[:, 128:256])
    for m in range(5):
        right = firsts[2 * m + 1] if 2 * m + 1 < 9 else jnp.zeros_like(firsts[0])
        out_ref[9 + m] = jnp.where(low, pltpu.roll(firsts[2 * m], 64, 1), right)
    halves = [
        grad_down[128 * e : 128 * e + 64] + pltpu.roll(grad_down[128 * e + 64 : 128 * e + 128], 448, 1)
        for e in range(2)
    ]
    for ab in range(4):
        tile = jnp.concatenate([half[:, 128 * ab : 128 * ab + 128] for half in halves], axis=0)
        out_ref[14 + ab] = tile.T[0:64]
    sums = small[...]
    head = sums[0:1] + pltpu.roll(sums, 64, 1)[0:1]
    total = jnp.sum(sums[1:2], axis=1, keepdims=True) * (1.0 / 64)
    row = merge_half(head, jnp.broadcast_to(total, (1, 128)))
    out_ref[18] = jnp.broadcast_to(row, (64, 128))


def arrange(features):
    channels, width, rows, depth = features.shape
    split = features.reshape(channels, width, rows // 4, 2, 2, depth)
    return split.transpose(1, 2, 4, 5, 3, 0).reshape(width, rows // 4, 2 * depth, 2 * channels)


def gather_pieces(value, axis):
    peers = lax.axis_size(axis)
    pieces = [value]
    for step in range(1, peers):
        pieces.append(lax.ppermute(value, axis, [(i, (i + step) % peers) for i in range(peers)]))
    order = (lax.axis_index(axis) - jnp.arange(peers)) % peers
    return jnp.stack(pieces)[order]


def gather_weights(w_first, w_second):
    both = jnp.concatenate([w_first, w_second], axis=0)
    taps, channels, share = both.shape
    fold = 128 // share
    packed = both.reshape(taps, fold, channels // fold, share).transpose(0, 2, 1, 3)
    packed = packed.reshape(taps, channels // fold, 128)
    pieces = gather_pieces(packed, "chan")
    pieces = pieces.reshape(-1, taps, channels // fold, fold, share).transpose(1, 3, 2, 0, 4)
    whole = pieces.reshape(taps, channels, -1)
    return jnp.concatenate([whole, whole], axis=2)


def doubling(value, axis):
    peers = lax.axis_size(axis)
    step = 1
    while step < peers:
        value = value + lax.ppermute(value, axis, [(i, i ^ step) for i in range(peers)])
        step *= 2
    return value


def scatter_sum(value, axis, dim):
    peers, me = lax.axis_size(axis), lax.axis_index(axis)
    total = lax.dynamic_index_in_dim(value, me, dim, keepdims=False)
    for step in range(1, peers):
        part = lax.dynamic_index_in_dim(value, (me + step) % peers, dim, keepdims=False)
        total = total + lax.ppermute(part, axis, [(i, (i + step) % peers) for i in range(peers)])
    return total


def shards(features, w_first, w_second, w_down, w_head, footprint, labels):
    bricks, chans, reps = lax.axis_size("bricks"), lax.axis_size("chan"), lax.axis_size("rep")
    planes = BRICK // chans
    side = lax.axis_index("chan") * planes // 4
    features = features[0]
    pairs = []
    for col in range(bricks * reps):
        for c in range(chans):
            src = col + 2 * (c * planes // 4) - 1
            if 0 <= src < bricks * reps:
                ends = [(j // reps * chans + c) * reps + j % reps for j in (src, col)]
                pairs.append(tuple(ends))
    outward = lax.dynamic_slice_in_dim(features, (1 - side) * 4, 4, 1)
    halo = lax.ppermute(outward, ("bricks", "chan", "rep"), pairs)

    weights = gather_weights(w_first, w_second)
    fold = 128 // w_down.shape[2]
    down = gather_pieces(w_down, "chan").transpose(1, 0, 2, 3).reshape(8, -1, w_down.shape[2])
    down2 = jnp.concatenate([down] * fold, axis=2)
    down_t = down.transpose(0, 2, 1)
    down_t2 = jnp.concatenate([down_t] * fold, axis=2)
    head2 = jnp.broadcast_to(jnp.concatenate([w_head, w_head])[None], (8, 128))
    half = jnp.arange(128) // 64
    head_mat = jnp.where(half[:, None] == half[None, :], jnp.concatenate([w_head, w_head])[:, None], 0.0)
    target = labels[0].reshape(4, 6, 2, 64).transpose(0, 1, 3, 2).astype(BF16)
    target = jnp.broadcast_to(target[:, :, :, None, :, None], (4, 6, 64, 2, 2, 64))
    target = target.reshape(4, 6, 128, 128)

    feat = arrange(features)
    slabs = feat.shape[1]
    smem = pl.BlockSpec(memory_space=pltpu.SMEM)
    vmem = pl.BlockSpec(memory_space=pltpu.VMEM)
    near, mat1, mat2 = pl.pallas_call(
        local_kernel,
        out_shape=(
            jax.ShapeDtypeStruct((4, slabs, ROWS, 128), BF16),
            jax.ShapeDtypeStruct((3, 1024, 256), BF16),
            jax.ShapeDtypeStruct((3, 1024, 256), BF16),
        ),
        in_specs=[smem, vmem, vmem, vmem],
        out_specs=(vmem, vmem, vmem),
        scratch_shapes=[pltpu.VMEM((slabs, 8, ROWS, 256), BF16)],
        compiler_params=pltpu.CompilerParams(vmem_limit_bytes=40 << 20),
        cost_estimate=pl.CostEstimate(flops=6 * 6 * 512 * 1024 * 512, bytes_accessed=8 << 20, transcendentals=0),
        name="first_local",
    )(footprint, feat, weights[:27], weights[27:])
    halo = arrange(halo)
    sums = pl.pallas_call(
        main_kernel,
        out_shape=jax.ShapeDtypeStruct((19, 64, 128), F32),
        in_specs=[smem] + [vmem] * 10,
        out_specs=vmem,
        scratch_shapes=[
            pltpu.VMEM((slabs + 2, 8, ROWS, 256), BF16),
            pltpu.VMEM((slabs + 2, 8, ROWS, 128), BF16),
            pltpu.VMEM((8, ROWS, 256), BF16),
            pltpu.VMEM((512, 256), BF16),
            pltpu.VMEM((128, 1024), BF16),
            pltpu.VMEM((2, 2, ROWS, 128), BF16),
            pltpu.VMEM((256, 256), BF16),
            pltpu.VMEM((384, 1024), BF16),
            pltpu.VMEM((3, 384, 256), F32),
            pltpu.VMEM((256, 512), F32),
            pltpu.VMEM((8, 128), F32),
        ],
        compiler_params=pltpu.CompilerParams(vmem_limit_bytes=56 << 20),
        cost_estimate=pl.CostEstimate(flops=4 * 6 * 6 * 512 * 1024 * 512, bytes_accessed=16 << 20, transcendentals=0),
        name="head_and_grads",
    )(footprint, feat, halo, near, mat1, mat2, down2, down_t2, head2, head_mat, target)

    share = 64 // chans
    parts = sums.reshape(19, chans, reps, share // reps, 128)
    mine = scatter_sum(parts, "rep", 2)
    mine = scatter_sum(mine, "chan", 1)
    mine = doubling(mine, "bricks")
    whole = gather_pieces(mine, "rep").transpose(1, 0, 2, 3).reshape(19, share, 128)
    later = whole[:9].reshape(3, 3, share, 2, 64).transpose(0, 3, 1, 4, 2)
    first = whole[9:14].reshape(5, share, 2, 64).transpose(0, 2, 3, 1).reshape(10, 64, share)[:9]
    second = jnp.concatenate([first.reshape(3, 1, 3, 64, share), later], axis=1).reshape(27, 64, share)
    down_out = whole[14:18].reshape(4, share, 2, 64).transpose(0, 2, 1, 3).reshape(8, share, 64)
    live = jnp.sum(footprint[1]).astype(F32)
    loss = (whole[18, 0, 64] / (COARSE * live)).reshape(1)
    return second, down_out, whole[18, 0, :64], loss


def solution(mesh):
    return jax.shard_map(
        shards,
        mesh=mesh,
        in_specs=(
            P(("groups", "bricks", "rep"), None, None, None, None),
            P(None, None, "chan"),
            P(None, None, "chan"),
            P(None, "chan", None),
            P(),
            P(None, "groups"),
            P(("groups", "bricks", "rep"), None, None),
        ),
        out_specs=(P("groups", None, "chan"), P("groups", "chan", None), P("groups"), P("groups")),
        check_vma=False,
    )
```

```python
import jax
import jax.numpy as jnp
from jax import lax
from jax.experimental import pallas as pl
from jax.experimental.pallas import tpu as pltpu
from jax.sharding import PartitionSpec as P

BRICK = 8
COARSE = 1024
ROWS = 256
F32 = jnp.float32
BF16 = jnp.bfloat16


def lanes_low(shape):
    return lax.broadcasted_iota(jnp.int32, shape, len(shape) - 1) % 128 < 64


def merge_half(low, high):
    return jnp.where(lanes_low(low.shape), low, high)


def shifted(value, by):
    row = lax.broadcasted_iota(jnp.int32, value.shape, 0) % 128
    inside = row >= by if by > 0 else row < 128 + by
    return jnp.where(inside, pltpu.roll(value, by % value.shape[0], 0), 0.0)


def build_conv(w_ref, out_ref):
    zero = jnp.zeros((64, 128), BF16)
    for e in range(3):
        for k in range(4):
            for slot, d in enumerate((0, 1, 2, -1)):
                for rx in range(2):
                    a = k - rx
                    halves = []
                    for ry in range(2):
                        b = d - ry + 1
                        live = 0 <= a < 3 and 0 <= b < 3
                        halves.append(w_ref[9 * a + 3 * b + e] if live else zero)
                    row = k * 256 + slot * 64
                    out_ref[e, row : row + 64, rx * 128 : rx * 128 + 128] = merge_half(*halves)


def conv_block(window_ref, slot, par, w_ref):
    lhs = jnp.concatenate([window_ref[slot, 2 * k + par] for k in range(4)], axis=1)
    below, level, above = [jnp.dot(lhs, w_ref[e], preferred_element_type=F32) for e in range(3)]
    return level + shifted(below, 2) + shifted(above, -2)


def gated(ref, plane, index, count):
    inside = (index >= 0) & (index < count)
    block = ref[plane, jnp.clip(index, 0, ref.shape[1] - 1)]
    return jnp.where(inside, block, jnp.zeros_like(block))


def turn_block(src_ref, dst_ref, plane, t):
    for py in range(2):
        tall = jnp.concatenate([src_ref[plane, 4 * t + py], src_ref[plane, 4 * t + 2 + py]], axis=0)
        dst_ref[plane, t, 128 * py : 128 * py + 128] = tall.T


def fill_window(window_ref, slot, plane, src_ref, src_plane, index, count):
    window_ref[slot, plane, :, 0:128] = gated(src_ref, src_plane, index, count)
    window_ref[slot, plane, :, 128:256] = merge_half(
        gated(src_ref, src_plane, index + 1, count), gated(src_ref, src_plane, index - 1, count)
    )


def pack_kernel(w1_ref, w2_ref, wd_ref, out_ref):
    half = w1_ref.shape[1] // 2
    start = 0
    for ref in (w1_ref, w2_ref, wd_ref):
        stop = start + ref.shape[0]
        out_ref[start:stop] = jnp.concatenate([ref[:, :half], ref[:, half:]], axis=2)
        start = stop


def local_kernel(foot_ref, feat_ref, *refs):
    chans = lax.axis_size("chan")
    piece_refs = refs[:chans]
    edge_ref, y1_ref, m1_ref, m2_ref, down_ref, back_ref, whole, turned, arranged, window = refs[chans:]
    column = lax.axis_index("bricks") * lax.axis_size("rep") + lax.axis_index("rep")
    me = lax.axis_index("chan")
    side = me * (BRICK // chans) // 4
    count = 2 * foot_ref[1, column]

    half = piece_refs[0].shape[1]
    for step in range(chans):
        block = piece_refs[step][...]
        source = lax.rem(me - step + chans, chans)
        for h in range(2):
            part = block[:, :, 64 * h : 64 * h + 64]
            rows = pl.ds(pl.multiple_of((2 * source + h) * half, half), half)
            whole[:, rows, :] = jnp.concatenate([part, part], axis=2)
    for t in range(54):
        turned[t] = jnp.concatenate([whole[t], whole[t]], axis=0).T[0:64]
    build_conv(turned.at[0:27], m1_ref)
    build_conv(turned.at[27:54], m2_ref)
    low = lanes_low((64, 128))
    zero = jnp.zeros((64, 128), BF16)
    for t in range(8):
        ab, e = t // 2, t % 2
        block = whole[54 + t]
        tile = jnp.concatenate([jnp.where(low, block, zero), jnp.where(low, zero, block)], axis=0)
        down_ref[ab * 128 : ab * 128 + 128, e * 128 : e * 128 + 128] = tile
        back_ref[:, t * 128 : t * 128 + 128] = tile.T

    def turn(t, carry):
        for p in range(8):
            turn_block(feat_ref, arranged, p, t)
        for p in range(4):
            edge_ref[p, t] = arranged[4 * side + p, t]
        return carry

    lax.fori_loop(0, count, turn, 0)

    def fill(t, carry):
        for p in range(8):
            fill_window(window, t, p, arranged, p, t, count)
        return carry

    lax.fori_loop(0, count, fill, 0)

    def conv(t, carry):
        for par in range(2):
            out = jnp.maximum(conv_block(window, t, par, m1_ref), 0.0).astype(BF16)
            for rx in range(2):
                y1_ref[2 * rx + par, t] = out[:, 128 * rx : 128 * rx + 128]
        return carry

    lax.fori_loop(0, count, conv, 0)


def main_kernel(
    foot_ref,
    edge_ref,
    halo_ref,
    near_ref,
    m1_ref,
    m2_ref,
    down_mat,
    back_mat,
    head_ref,
    label_ref,
    keep_ref,
    send_ref,
    arranged,
    window,
    hidden,
    hwin,
    headm_ref,
    y2_ref,
    delta_t,
    err_t,
    grad,
    grad_down,
    small,
):
    reps, chans = lax.axis_size("rep"), lax.axis_size("chan")
    columns = lax.axis_size("bricks") * reps
    column = lax.axis_index("bricks") * reps + lax.axis_index("rep")
    planes = BRICK // chans
    mine = lax.axis_index("chan") * planes
    side = mine // 4
    other = column + 2 * side - 1
    present = (other >= 0) & (other < columns)
    other = jnp.clip(other, 0, columns - 1)
    count = 2 * foot_ref[1, column]
    other_count = jnp.where(present, 2 * foot_ref[1, other], 0)
    offset = 2 * (foot_ref[0, other] - foot_ref[0, column])

    grad[...] = jnp.zeros_like(grad)
    grad_down[...] = jnp.zeros_like(grad_down)
    small[...] = jnp.zeros_like(small)
    head_row = jnp.concatenate([head_ref[...], head_ref[...]], axis=1)
    square_row = lax.broadcasted_iota(jnp.int32, (128, 128), 0)
    square_lane = lax.broadcasted_iota(jnp.int32, (128, 128), 1)
    same_half = (square_row < 64) == (square_lane < 64)
    headm_ref[...] = jnp.where(same_half, jnp.broadcast_to(head_row, (128, 128)).T, 0.0)
    pick_depth = jnp.where(square_row // 2 == square_lane % 64, 1.0, 0.0).astype(BF16)

    def turn(t, carry):
        for p in range(4):
            turn_block(halo_ref, arranged, p, t)
        return carry

    lax.fori_loop(0, other_count, turn, 0)

    def fill(slot, carry):
        t = slot - 1
        for p in range(4):
            fill_window(window, slot, (1 - side) * 4 + p, edge_ref, p, t, count)
            fill_window(window, slot, side * 4 + p, arranged, p, t - offset, other_count)
        return carry

    lax.fori_loop(0, count + 2, fill, 0)

    def first(slot, carry):
        t = slot - 1
        own = (t >= 0) & (t < count)
        next_to = (t - offset >= 0) & (t - offset < other_count)
        for par in range(2):
            out = jnp.maximum(conv_block(window, slot, par, m1_ref), 0.0).astype(BF16)
            for rx in range(2):
                live = jnp.where(side == rx, next_to, own)
                block = out[:, 128 * rx : 128 * rx + 128]
                hidden[slot, side * 4 + 2 * rx + par] = jnp.where(
                    live, block, jnp.zeros_like(block)
                )
        for p in range(4):
            hidden[slot, (1 - side) * 4 + p] = gated(near_ref, p, t, count)
        return carry

    lax.fori_loop(0, count + 2, first, 0)

    even = square_row % 2 == 0

    def second(t, carry):
        for p in range(8):
            hwin[p, :, 0:128] = hidden[t + 1, p]
            hwin[p, :, 128:256] = merge_half(hidden[t + 2, p], hidden[t, p])
        for par in range(2):
            lhs = jnp.concatenate([hwin[2 * k + par] for k in range(4)], axis=1)
            below, level, above = [
                jnp.dot(lhs, m2_ref[e], preferred_element_type=F32) for e in range(3)
            ]
            out = level + shifted(below, 2) + shifted(above, -2)
            out = jnp.maximum(out, 0.0).astype(BF16)
            for rx in range(2):
                y2_ref[rx, par] = out[:, 128 * rx : 128 * rx + 128]
        for rx in range(2):
            fine = jnp.concatenate(
                [y2_ref[rx, a, 128 * b : 128 * b + 128] for a in range(2) for b in range(2)], axis=1
            )
            both = jnp.dot(fine, down_mat[...], preferred_element_type=F32)
            coarse = both[:, 0:128] + shifted(both[:, 128:256], -1)
            rect = jnp.maximum(coarse, 0.0)
            logit = jnp.dot(
                rect, headm_ref[...], precision=lax.Precision.HIGHEST, preferred_element_type=F32
            )
            plane = 4 * side + 2 * rx
            keep = even & (plane >= mine) & (plane < mine + planes)
            line = label_ref[:, pl.ds(pl.multiple_of(128 * t, 128), 128)].astype(F32)
            row = jnp.where(side == 1, line[2 + rx : 3 + rx], line[rx : rx + 1])
            row = jnp.broadcast_to(row, (128, 128))
            row = jnp.where(same_half, row, 0.0).astype(BF16)
            label = lax.dot_general(
                pick_depth, row, (((1,), (1,)), ((), ())), preferred_element_type=F32
            )
            tail = jnp.exp(-jnp.abs(logit))
            soft = jnp.maximum(logit, 0.0) + jnp.log1p(tail)
            sigmoid = jnp.where(logit >= 0.0, 1.0, tail) / (1.0 + tail)
            loss = jnp.where(keep, soft - label * logit, 0.0)
            slope = jnp.where(keep, (sigmoid - label) * (1.0 / COARSE), 0.0)
            small[0:1] += jnp.sum(slope * rect, axis=0, keepdims=True)
            small[1:2] += jnp.sum(loss, axis=0, keepdims=True)
            delta = jnp.where(coarse > 0.0, slope * head_row, 0.0).astype(BF16).astype(F32)
            moved = shifted(delta, 1)
            delta_t[0:128, 128 * rx : 128 * rx + 128] = delta.T.astype(BF16)
            delta_t[128:256, 128 * rx : 128 * rx + 128] = moved.T.astype(BF16)
            spread = (delta + moved).astype(BF16)
            back = jnp.dot(spread, back_mat[...], preferred_element_type=F32)
            for a in range(2):
                for b in range(2):
                    lane = (2 * a + b) * 256
                    err = jnp.where(even, back[:, lane : lane + 128], back[:, lane + 128 : lane + 256])
                    live = y2_ref[rx, a, 128 * b : 128 * b + 128].astype(F32) > 0.0
                    err = jnp.where(live, err, 0.0)
                    col = (2 * rx + a) * 256 + b * 128
                    turned = err.astype(BF16).T.astype(F32)
                    up = jnp.where(square_lane < 126, pltpu.roll(turned, 126, 1), 0.0)
                    down = jnp.where(square_lane >= 2, pltpu.roll(turned, 2, 1), 0.0)
                    for e, value in enumerate((up, turned, down)):
                        err_t[128 * e : 128 * e + 128, col : col + 128] = value.astype(BF16)
        fine = jnp.concatenate(
            [
                jnp.concatenate([y2_ref[rx, a, 128 * b : 128 * b + 128] for rx in range(2)], axis=0)
                for a in range(2)
                for b in range(2)
            ],
            axis=1,
        )
        grad_down[...] += jnp.dot(delta_t[...], fine, preferred_element_type=F32)
        for a in range(3):
            rows = hwin[2 * a : 2 * a + 4].reshape(4 * ROWS, 256)
            grad[a] += jnp.dot(err_t[...], rows, preferred_element_type=F32)
        return carry

    lax.fori_loop(0, count, second, 0)

    low = lanes_low((64, 128))
    rep, chan = lax.axis_index("rep"), lax.axis_index("chan")
    share = 64 // chans // reps

    def emit(slab, value):
        for c in range(chans):
            place = lax.rem(c - chan + chans, chans)
            for r in range(reps):
                rows = value[(c * reps + r) * share : (c * reps + r + 1) * share]

                @pl.when(rep == r)
                def _():
                    keep_ref[place, slab] = rows

                @pl.when(rep != r)
                def _():
                    send_ref[place, slab] = rows

    firsts = []
    for a in range(3):
        for e in range(3):
            both = grad[a, 128 * e : 128 * e + 64] + pltpu.roll(
                grad[a, 128 * e + 64 : 128 * e + 128], 192, 1
            )
            emit(3 * a + e, both[:, 0:128])
            firsts.append(both[:, 128:256])
    for m in range(5):
        right = firsts[2 * m + 1] if 2 * m + 1 < 9 else jnp.zeros_like(firsts[0])
        emit(9 + m, jnp.where(low, pltpu.roll(firsts[2 * m], 64, 1), right))
    halves = [
        grad_down[128 * e : 128 * e + 64] + pltpu.roll(grad_down[128 * e + 64 : 128 * e + 128], 448, 1)
        for e in range(2)
    ]
    for ab in range(4):
        tile = jnp.concatenate([half[:, 128 * ab : 128 * ab + 128] for half in halves], axis=0)
        emit(14 + ab, tile.T[0:64])
    sums = small[...]
    head = sums[0:1] + pltpu.roll(sums, 64, 1)[0:1]
    total = jnp.sum(sums[1:2], axis=1, keepdims=True) * (1.0 / 64)
    row = merge_half(head, jnp.broadcast_to(total, (1, 128)))
    emit(18, jnp.broadcast_to(row, (64, 128)))


def final_kernel(foot_ref, mine_ref, peer_ref, second_ref, down_ref, head_ref, loss_ref):
    rep = lax.axis_index("rep")
    share = mine_ref.shape[1]
    for ref, r in ((mine_ref, rep), (peer_ref, 1 - rep)):
        rows = pl.ds(pl.multiple_of(r * share, share), share)
        for a in range(3):
            for e in range(3):
                m = 3 * a + e
                later, first = ref[m], ref[9 + m // 2]
                second_ref[9 * a + e, rows] = first[:, 64 * (m % 2) : 64 * (m % 2) + 64]
                second_ref[9 * a + 3 + e, rows] = later[:, 0:64]
                second_ref[9 * a + 6 + e, rows] = later[:, 64:128]
        for ab in range(4):
            for e in range(2):
                down_ref[2 * ab + e, rows] = ref[14 + ab][:, 64 * e : 64 * e + 64]
    line = mine_ref[18][0:1]
    head_ref[...] = line[:, 0:64]
    live = foot_ref[1, 0]
    for c in range(1, foot_ref.shape[1]):
        live += foot_ref[1, c]
    scale = jnp.full((1, 1), COARSE * live, jnp.int32).astype(F32)
    loss_ref[...] = line[:, 64:65] / scale


def shards(features, w_first, w_second, w_down, w_head, footprint, labels):
    bricks, chans, reps = lax.axis_size("bricks"), lax.axis_size("chan"), lax.axis_size("rep")
    planes = BRICK // chans
    side = lax.axis_index("chan") * planes // 4
    smem = pl.BlockSpec(memory_space=pltpu.SMEM)
    vmem = pl.BlockSpec(memory_space=pltpu.VMEM)
    features = features[0]
    slabs = features.shape[2] // 4

    packed = pl.pallas_call(
        pack_kernel,
        out_shape=jax.ShapeDtypeStruct((62, 32 // chans, 128), BF16),
        in_specs=[vmem] * 3,
        out_specs=vmem,
        name="pack",
    )(w_first.transpose(0, 2, 1), w_second.transpose(0, 2, 1), w_down)
    pieces = [packed]
    for step in range(1, chans):
        ring = [(i, (i + step) % chans) for i in range(chans)]
        pieces.append(lax.ppermute(packed, "chan", ring))

    pairs = []
    for col in range(bricks * reps):
        for c in range(chans):
            src = col + 2 * (c * planes // 4) - 1
            if 0 <= src < bricks * reps:
                ends = [(j // reps * chans + c) * reps + j % reps for j in (src, col)]
                pairs.append(tuple(ends))
    outward = lax.dynamic_slice_in_dim(features, (1 - side) * 4, 4, 1).transpose(1, 2, 0, 3)
    halo = lax.ppermute(outward, ("bricks", "chan", "rep"), pairs)

    edge, near, mat1, mat2, down_mat, back_mat = pl.pallas_call(
        local_kernel,
        out_shape=(
            jax.ShapeDtypeStruct((4, slabs, ROWS, 128), BF16),
            jax.ShapeDtypeStruct((4, slabs, ROWS, 128), BF16),
            jax.ShapeDtypeStruct((3, 1024, 256), BF16),
            jax.ShapeDtypeStruct((3, 1024, 256), BF16),
            jax.ShapeDtypeStruct((512, 256), BF16),
            jax.ShapeDtypeStruct((128, 1024), BF16),
        ),
        in_specs=[smem] + [vmem] * (1 + chans),
        out_specs=(vmem,) * 6,
        scratch_shapes=[
            pltpu.VMEM((62, 64, 128), BF16),
            pltpu.VMEM((54, 64, 128), BF16),
            pltpu.VMEM((8, slabs, ROWS, 128), BF16),
            pltpu.VMEM((slabs, 8, ROWS, 256), BF16),
        ],
        compiler_params=pltpu.CompilerParams(vmem_limit_bytes=36 << 20),
        cost_estimate=pl.CostEstimate(flops=6 * 6 * 512 * 1024 * 512, bytes_accessed=8 << 20, transcendentals=0),
        name="first_local",
    )(footprint, features.transpose(1, 2, 0, 3), *pieces)
    parts = jax.ShapeDtypeStruct((chans, 19, 64 // chans // reps, 128), F32)
    keep, send = pl.pallas_call(
        main_kernel,
        out_shape=(parts, parts),
        in_specs=[smem] + [vmem] * 9,
        out_specs=(vmem, vmem),
        scratch_shapes=[
            pltpu.VMEM((4, slabs, ROWS, 128), BF16),
            pltpu.VMEM((slabs + 2, 8, ROWS, 256), BF16),
            pltpu.VMEM((slabs + 2, 8, ROWS, 128), BF16),
            pltpu.VMEM((8, ROWS, 256), BF16),
            pltpu.VMEM((128, 128), F32),
            pltpu.VMEM((2, 2, ROWS, 128), BF16),
            pltpu.VMEM((256, 256), BF16),
            pltpu.VMEM((384, 1024), BF16),
            pltpu.VMEM((3, 384, 256), F32),
            pltpu.VMEM((256, 512), F32),
            pltpu.VMEM((8, 128), F32),
        ],
        compiler_params=pltpu.CompilerParams(vmem_limit_bytes=40 << 20),
        cost_estimate=pl.CostEstimate(flops=4 * 6 * 6 * 512 * 1024 * 512, bytes_accessed=16 << 20, transcendentals=0),
        name="head_and_grads",
    )(footprint, edge, halo, near, mat1, mat2, down_mat, back_mat, w_head.reshape(1, 64), labels[0])

    swap = [(i, 1 - i) for i in range(reps)]
    got = lax.ppermute(send, "rep", swap)
    mine = keep[0] + got[0]
    for step in range(1, chans):
        ring = [(i, (i + step) % chans) for i in range(chans)]
        mine = mine + lax.ppermute(keep[step] + got[step], "chan", ring)
    step = 1
    while step < bricks:
        mine = mine + lax.ppermute(mine, "bricks", [(i, i ^ step) for i in range(bricks)])
        step *= 2
    peer = lax.ppermute(mine, "rep", swap)
    share = 64 // chans
    second, down, head, loss = pl.pallas_call(
        final_kernel,
        out_shape=(
            jax.ShapeDtypeStruct((27, share, 64), F32),
            jax.ShapeDtypeStruct((8, share, 64), F32),
            jax.ShapeDtypeStruct((1, 64), F32),
            jax.ShapeDtypeStruct((1, 1), F32),
        ),
        in_specs=[smem, vmem, vmem],
        out_specs=(vmem,) * 4,
        name="assemble",
    )(footprint, mine, peer)
    return second.transpose(0, 2, 1), down, head.reshape(64), loss.reshape(1)


def solution(mesh):
    return jax.shard_map(
        shards,
        mesh=mesh,
        in_specs=(
            P(("groups", "bricks", "rep"), None, None, None, None),
            P(None, None, "chan"),
            P(None, None, "chan"),
            P(None, "chan", None),
            P(),
            P(None, "groups"),
            P(("groups", "bricks", "rep"), None, None),
        ),
        out_specs=(P("groups", None, "chan"), P("groups", "chan", None), P("groups"), P("groups")),
        check_vma=False,
    )
```

```python
import jax
import jax.numpy as jnp
from jax import lax
from jax.experimental import pallas as pl
from jax.experimental.pallas import tpu as pltpu
from jax.sharding import PartitionSpec as P

BRICK = 8
COARSE = 1024
ROWS = 256
F32 = jnp.float32
BF16 = jnp.bfloat16


def lanes_low(shape):
    return lax.broadcasted_iota(jnp.int32, shape, len(shape) - 1) % 128 < 64


def merge_half(low, high):
    return jnp.where(lanes_low(low.shape), low, high)


def shifted(value, by):
    row = lax.broadcasted_iota(jnp.int32, value.shape, 0) % 128
    inside = row >= by if by > 0 else row < 128 + by
    return jnp.where(inside, pltpu.roll(value, by % value.shape[0], 0), 0.0)


def build_conv(w_ref, out_ref):
    zero = jnp.zeros((64, 128), BF16)
    for e in range(3):
        for k in range(4):
            for slot, d in enumerate((0, 1, 2, -1)):
                for rx in range(2):
                    a = k - rx
                    halves = []
                    for ry in range(2):
                        b = d - ry + 1
                        live = 0 <= a < 3 and 0 <= b < 3
                        halves.append(w_ref[9 * a + 3 * b + e] if live else zero)
                    row = k * 256 + slot * 64
                    out_ref[e, row : row + 64, rx * 128 : rx * 128 + 128] = merge_half(*halves)


def conv_rows(window_ref, w_ref, slot=()):
    lhs = jnp.concatenate(
        [window_ref[(*slot, pl.ds(2 * k, 2))].reshape(2 * ROWS, 256) for k in range(4)], axis=1
    )
    below, level, above = [jnp.dot(lhs, w_ref[e], preferred_element_type=F32) for e in range(3)]
    return level + shifted(below, 2) + shifted(above, -2)


def gated(ref, plane, index, count):
    inside = (index >= 0) & (index < count)
    block = ref[plane, jnp.clip(index, 0, ref.shape[1] - 1)]
    return jnp.where(inside, block, jnp.zeros_like(block))


def turn_block(src_ref, dst_ref, plane, t):
    for py in range(2):
        tall = jnp.concatenate([src_ref[plane, 4 * t + py], src_ref[plane, 4 * t + 2 + py]], axis=0)
        dst_ref[plane, t, 128 * py : 128 * py + 128] = tall.T


def fill_window(window_ref, plane, src_ref, src_plane, index, count):
    window_ref[plane, :, 0:128] = gated(src_ref, src_plane, index, count)
    window_ref[plane, :, 128:256] = merge_half(
        gated(src_ref, src_plane, index + 1, count), gated(src_ref, src_plane, index - 1, count)
    )


def pack_kernel(w1_ref, w2_ref, wd_ref, out_ref):
    half = w1_ref.shape[1] // 2
    start = 0
    for ref in (w1_ref, w2_ref, wd_ref):
        stop = start + ref.shape[0]
        out_ref[start:stop] = jnp.concatenate([ref[:, :half], ref[:, half:]], axis=2)
        start = stop


def local_kernel(foot_ref, feat_ref, *refs):
    chans = lax.axis_size("chan")
    piece_refs = refs[:chans]
    edge_ref, y1_ref, m1_ref, m2_ref, down_ref, back_ref, whole, turned, arranged = refs[chans:-2]
    even_window, odd_window = refs[-2:]
    column = lax.axis_index("bricks") * lax.axis_size("rep") + lax.axis_index("rep")
    me = lax.axis_index("chan")
    side = me * (BRICK // chans) // 4
    count = 2 * foot_ref[1, column]

    half = piece_refs[0].shape[1]
    for step in range(chans):
        block = piece_refs[step][...]
        source = lax.rem(me - step + chans, chans)
        for h in range(2):
            part = block[:, :, 64 * h : 64 * h + 64]
            rows = pl.ds(pl.multiple_of((2 * source + h) * half, half), half)
            whole[:, rows, :] = jnp.concatenate([part, part], axis=2)
    for t in range(54):
        turned[t] = jnp.concatenate([whole[t], whole[t]], axis=0).T[0:64]
    build_conv(turned.at[0:27], m1_ref)
    build_conv(turned.at[27:54], m2_ref)
    low = lanes_low((64, 128))
    zero = jnp.zeros((64, 128), BF16)
    for t in range(8):
        ab, e = t // 2, t % 2
        block = whole[54 + t]
        tile = jnp.concatenate([jnp.where(low, block, zero), jnp.where(low, zero, block)], axis=0)
        down_ref[ab * 128 : ab * 128 + 128, e * 128 : e * 128 + 128] = tile
        back_ref[:, t * 128 : t * 128 + 128] = tile.T

    def turn(t, carry):
        for p in range(8):
            turn_block(feat_ref, arranged, p, t)
        for p in range(4):
            edge_ref[p, t] = arranged[4 * side + p, t]
        return carry

    lax.fori_loop(0, count, turn, 0)

    def fill(window, t):
        for p in range(8):
            fill_window(window, p, arranged, p, t, count)

    def conv(window, t):
        out = jnp.maximum(conv_rows(window, m1_ref), 0.0).astype(BF16)
        for par in range(2):
            for rx in range(2):
                y1_ref[2 * rx + par, t] = out[ROWS * par : ROWS * par + ROWS, 128 * rx : 128 * rx + 128]

    def pair(j, carry):
        fill(odd_window, 2 * j + 1)
        conv(even_window, 2 * j)
        fill(even_window, 2 * j + 2)
        conv(odd_window, 2 * j + 1)
        return carry

    fill(even_window, 0)
    lax.fori_loop(0, count // 2, pair, 0)


def main_kernel(
    foot_ref,
    edge_ref,
    halo_ref,
    near_ref,
    m1_ref,
    m2_ref,
    down_mat,
    back_mat,
    head_ref,
    label_ref,
    keep_ref,
    send_ref,
    arranged,
    even_window,
    odd_window,
    hidden,
    hwin,
    headm_ref,
    y2_ref,
    delta_t,
    err_t,
    grad,
    grad_down,
    small,
):
    reps, chans = lax.axis_size("rep"), lax.axis_size("chan")
    columns = lax.axis_size("bricks") * reps
    column = lax.axis_index("bricks") * reps + lax.axis_index("rep")
    planes = BRICK // chans
    mine = lax.axis_index("chan") * planes
    side = mine // 4
    other = column + 2 * side - 1
    present = (other >= 0) & (other < columns)
    other = jnp.clip(other, 0, columns - 1)
    count = 2 * foot_ref[1, column]
    other_count = jnp.where(present, 2 * foot_ref[1, other], 0)
    offset = 2 * (foot_ref[0, other] - foot_ref[0, column])

    grad[...] = jnp.zeros_like(grad)
    grad_down[...] = jnp.zeros_like(grad_down)
    small[...] = jnp.zeros_like(small)
    head_row = jnp.concatenate([head_ref[...], head_ref[...]], axis=1)
    square_row = lax.broadcasted_iota(jnp.int32, (128, 128), 0)
    square_lane = lax.broadcasted_iota(jnp.int32, (128, 128), 1)
    same_half = (square_row < 64) == (square_lane < 64)
    head_mat = jnp.where(same_half, jnp.broadcast_to(head_row, (128, 128)).T, 0.0)
    head_high = head_mat.astype(BF16)
    headm_ref[0:128] = head_high
    headm_ref[128:256] = head_high
    headm_ref[256:384] = (head_mat - head_high.astype(F32)).astype(BF16)
    pick_depth = jnp.where(square_row // 2 == square_lane % 64, 1.0, 0.0).astype(BF16)

    def turn(t, carry):
        for p in range(4):
            turn_block(halo_ref, arranged, p, t)
        return carry

    lax.fori_loop(0, other_count, turn, 0)

    def fill(window, t):
        for p in range(4):
            fill_window(window, (1 - side) * 4 + p, edge_ref, p, t, count)
            fill_window(window, side * 4 + p, arranged, p, t - offset, other_count)

    def first(window, t):
        own = (t >= 0) & (t < count)
        next_to = (t - offset >= 0) & (t - offset < other_count)
        out = jnp.maximum(conv_rows(window, m1_ref), 0.0).astype(BF16)
        for rx in range(2):
            live = jnp.where(side == rx, next_to, own)
            for par in range(2):
                block = out[ROWS * par : ROWS * par + ROWS, 128 * rx : 128 * rx + 128]
                hidden[t + 1, side * 4 + 2 * rx + par] = jnp.where(live, block, jnp.zeros_like(block))

    def near(t):
        for p in range(4):
            hidden[t + 1, (1 - side) * 4 + p] = gated(near_ref, p, t, count)

    def rim(i, carry):
        t = jnp.where(i == 0, -1, count)
        beside = (t - offset >= 0) & (t - offset < other_count)
        hidden[t + 1] = jnp.zeros((8, ROWS, 128), BF16)

        @pl.when(beside)
        def _():
            fill(even_window, t)
            first(even_window, t)

        return carry

    def pair(j, carry):
        fill(odd_window, 2 * j + 1)
        near(2 * j)
        first(even_window, 2 * j)
        fill(even_window, 2 * j + 2)
        near(2 * j + 1)
        first(odd_window, 2 * j + 1)
        return carry

    lax.fori_loop(0, 2, rim, 0)
    fill(even_window, 0)
    lax.fori_loop(0, count // 2, pair, 0)

    row4 = lax.broadcasted_iota(jnp.int32, (512, 128), 0)
    even4 = row4 % 2 == 0
    plane4 = 4 * side + 2 * (row4 // 128 % 2)
    keep = even4 & (plane4 >= mine) & (plane4 < mine + planes)

    def second(j, carry):
        for u in range(2):
            t = 2 * j + u
            for p in range(8):
                hwin[u, p, :, 0:128] = hidden[t + 1, p]
                hwin[u, p, :, 128:256] = merge_half(hidden[t + 2, p], hidden[t, p])
            out = jnp.maximum(conv_rows(hwin, m2_ref, (u,)), 0.0).astype(BF16)
            for par in range(2):
                for rx in range(2):
                    y2_ref[u, rx, par] = out[ROWS * par : ROWS * par + ROWS, 128 * rx : 128 * rx + 128]
        fine = jnp.concatenate(
            [
                jnp.concatenate(
                    [y2_ref[u, rx, a, 128 * b : 128 * b + 128] for u in range(2) for rx in range(2)],
                    axis=0,
                )
                for a in range(2)
                for b in range(2)
            ],
            axis=1,
        )
        both = jnp.dot(fine, down_mat[...], preferred_element_type=F32)
        coarse = both[:, 0:128] + shifted(both[:, 128:256], -1)
        rect = jnp.maximum(coarse, 0.0)
        high = rect.astype(BF16)
        rest = (rect - high.astype(F32)).astype(BF16)
        logit = jnp.dot(
            jnp.concatenate([high, rest, high], axis=1), headm_ref[...], preferred_element_type=F32
        )
        labels = []
        for u in range(2):
            line = label_ref[:, pl.ds(pl.multiple_of(256 * j + 128 * u, 128), 128)].astype(F32)
            for rx in range(2):
                row = jnp.where(side == 1, line[2 + rx : 3 + rx], line[rx : rx + 1])
                row = jnp.where(same_half, jnp.broadcast_to(row, (128, 128)), 0.0).astype(BF16)
                labels.append(
                    lax.dot_general(
                        pick_depth, row, (((1,), (1,)), ((), ())), preferred_element_type=F32
                    )
                )
        label = jnp.concatenate(labels, axis=0)
        tail = jnp.exp(-jnp.abs(logit))
        soft = jnp.maximum(logit, 0.0) + jnp.log1p(tail)
        sigmoid = jnp.where(logit >= 0.0, 1.0, tail) / (1.0 + tail)
        loss = jnp.where(keep, soft - label * logit, 0.0)
        slope = jnp.where(keep, (sigmoid - label) * (1.0 / COARSE), 0.0)
        small[0:1] += jnp.sum(slope * rect, axis=0, keepdims=True)
        small[1:2] += jnp.sum(loss, axis=0, keepdims=True)
        delta = jnp.where(coarse > 0.0, slope * head_row, 0.0).astype(BF16).astype(F32)
        moved = shifted(delta, 1)
        delta_t[0:128] = delta.astype(BF16).T
        delta_t[128:256] = moved.astype(BF16).T
        back = jnp.dot((delta + moved).astype(BF16), back_mat[...], preferred_element_type=F32)
        for a in range(2):
            for b in range(2):
                lane = (2 * a + b) * 256
                err = jnp.where(even4, back[:, lane : lane + 128], back[:, lane + 128 : lane + 256])
                live = fine[:, lane // 2 : lane // 2 + 128].astype(F32) > 0.0
                err = jnp.where(live, err, 0.0)
                for n in range(4):
                    turned = err[128 * n : 128 * n + 128].astype(BF16).T
                    col = n * 512 + a * 256 + b * 128
                    err_t[128:256, col : col + 128] = turned
                    up = jnp.where(square_lane < 126, pltpu.roll(turned, 126, 1), jnp.zeros_like(turned))
                    down = jnp.where(square_lane >= 2, pltpu.roll(turned, 2, 1), jnp.zeros_like(turned))
                    err_t[0:128, col : col + 128] = up
                    err_t[256:384, col : col + 128] = down
        grad_down[...] += jnp.dot(delta_t[...], fine, preferred_element_type=F32)
        for a in range(3):
            rows = hwin[:, 2 * a : 2 * a + 4].reshape(8 * ROWS, 256)
            grad[a] += jnp.dot(err_t[...], rows, preferred_element_type=F32)
        return carry

    lax.fori_loop(0, count // 2, second, 0)

    low = lanes_low((64, 128))
    rep, chan = lax.axis_index("rep"), lax.axis_index("chan")
    share = 64 // chans // reps

    def emit(slab, value):
        for c in range(chans):
            place = lax.rem(c - chan + chans, chans)
            for r in range(reps):
                rows = value[(c * reps + r) * share : (c * reps + r + 1) * share]

                @pl.when(rep == r)
                def _():
                    keep_ref[place, slab] = rows

                @pl.when(rep != r)
                def _():
                    send_ref[place, slab] = rows

    firsts = []
    for a in range(3):
        for e in range(3):
            both = grad[a, 128 * e : 128 * e + 64] + pltpu.roll(
                grad[a, 128 * e + 64 : 128 * e + 128], 192, 1
            )
            emit(3 * a + e, both[:, 0:128])
            firsts.append(both[:, 128:256])
    for m in range(5):
        right = firsts[2 * m + 1] if 2 * m + 1 < 9 else jnp.zeros_like(firsts[0])
        emit(9 + m, jnp.where(low, pltpu.roll(firsts[2 * m], 64, 1), right))
    halves = [
        grad_down[128 * e : 128 * e + 64] + pltpu.roll(grad_down[128 * e + 64 : 128 * e + 128], 448, 1)
        for e in range(2)
    ]
    for ab in range(4):
        tile = jnp.concatenate([half[:, 128 * ab : 128 * ab + 128] for half in halves], axis=0)
        emit(14 + ab, tile.T[0:64])
    sums = small[...]
    head = sums[0:1] + pltpu.roll(sums, 64, 1)[0:1]
    total = jnp.sum(sums[1:2], axis=1, keepdims=True) * (1.0 / 64)
    row = merge_half(head, jnp.broadcast_to(total, (1, 128)))
    emit(18, jnp.broadcast_to(row, (64, 128)))


def final_kernel(foot_ref, mine_ref, peer_ref, second_ref, down_ref, head_ref, loss_ref):
    rep = lax.axis_index("rep")
    share = mine_ref.shape[1]
    for ref, r in ((mine_ref, rep), (peer_ref, 1 - rep)):
        rows = pl.ds(pl.multiple_of(r * share, share), share)
        for a in range(3):
            for e in range(3):
                m = 3 * a + e
                later, first = ref[m], ref[9 + m // 2]
                second_ref[9 * a + e, rows] = first[:, 64 * (m % 2) : 64 * (m % 2) + 64]
                second_ref[9 * a + 3 + e, rows] = later[:, 0:64]
                second_ref[9 * a + 6 + e, rows] = later[:, 64:128]
        for ab in range(4):
            for e in range(2):
                down_ref[2 * ab + e, rows] = ref[14 + ab][:, 64 * e : 64 * e + 64]
    line = mine_ref[18][0:1]
    head_ref[...] = line[:, 0:64]
    live = foot_ref[1, 0]
    for c in range(1, foot_ref.shape[1]):
        live += foot_ref[1, c]
    scale = jnp.full((1, 1), COARSE * live, jnp.int32).astype(F32)
    loss_ref[...] = line[:, 64:65] / scale


def shards(features, w_first, w_second, w_down, w_head, footprint, labels):
    bricks, chans, reps = lax.axis_size("bricks"), lax.axis_size("chan"), lax.axis_size("rep")
    planes = BRICK // chans
    side = lax.axis_index("chan") * planes // 4
    smem = pl.BlockSpec(memory_space=pltpu.SMEM)
    vmem = pl.BlockSpec(memory_space=pltpu.VMEM)
    features = features[0]
    slabs = features.shape[2] // 4

    packed = pl.pallas_call(
        pack_kernel,
        out_shape=jax.ShapeDtypeStruct((62, 32 // chans, 128), BF16),
        in_specs=[vmem] * 3,
        out_specs=vmem,
        name="pack",
    )(w_first.transpose(0, 2, 1), w_second.transpose(0, 2, 1), w_down)
    pieces = [packed]
    for step in range(1, chans):
        ring = [(i, (i + step) % chans) for i in range(chans)]
        pieces.append(lax.ppermute(packed, "chan", ring))

    pairs = []
    for col in range(bricks * reps):
        for c in range(chans):
            src = col + 2 * (c * planes // 4) - 1
            if 0 <= src < bricks * reps:
                ends = [(j // reps * chans + c) * reps + j % reps for j in (src, col)]
                pairs.append(tuple(ends))
    outward = lax.dynamic_slice_in_dim(features, (1 - side) * 4, 4, 1).transpose(1, 2, 0, 3)
    halo = lax.ppermute(outward, ("bricks", "chan", "rep"), pairs)

    edge, near, mat1, mat2, down_mat, back_mat = pl.pallas_call(
        local_kernel,
        out_shape=(
            jax.ShapeDtypeStruct((4, slabs, ROWS, 128), BF16),
            jax.ShapeDtypeStruct((4, slabs, ROWS, 128), BF16),
            jax.ShapeDtypeStruct((3, 1024, 256), BF16),
            jax.ShapeDtypeStruct((3, 1024, 256), BF16),
            jax.ShapeDtypeStruct((512, 256), BF16),
            jax.ShapeDtypeStruct((128, 1024), BF16),
        ),
        in_specs=[smem] + [vmem] * (1 + chans),
        out_specs=(vmem,) * 6,
        scratch_shapes=[
            pltpu.VMEM((62, 64, 128), BF16),
            pltpu.VMEM((54, 64, 128), BF16),
            pltpu.VMEM((8, slabs, ROWS, 128), BF16),
            pltpu.VMEM((8, ROWS, 256), BF16),
            pltpu.VMEM((8, ROWS, 256), BF16),
        ],
        compiler_params=pltpu.CompilerParams(vmem_limit_bytes=36 << 20),
        cost_estimate=pl.CostEstimate(flops=6 * 6 * 512 * 1024 * 512, bytes_accessed=8 << 20, transcendentals=0),
        name="first_local",
    )(footprint, features.transpose(1, 2, 0, 3), *pieces)
    parts = jax.ShapeDtypeStruct((chans, 19, 64 // chans // reps, 128), F32)
    keep, send = pl.pallas_call(
        main_kernel,
        out_shape=(parts, parts),
        in_specs=[smem] + [vmem] * 9,
        out_specs=(vmem, vmem),
        scratch_shapes=[
            pltpu.VMEM((4, slabs, ROWS, 128), BF16),
            pltpu.VMEM((8, ROWS, 256), BF16),
            pltpu.VMEM((8, ROWS, 256), BF16),
            pltpu.VMEM((slabs + 2, 8, ROWS, 128), BF16),
            pltpu.VMEM((2, 8, ROWS, 256), BF16),
            pltpu.VMEM((384, 128), BF16),
            pltpu.VMEM((2, 2, 2, ROWS, 128), BF16),
            pltpu.VMEM((256, 512), BF16),
            pltpu.VMEM((384, 2048), BF16),
            pltpu.VMEM((3, 384, 256), F32),
            pltpu.VMEM((256, 512), F32),
            pltpu.VMEM((8, 128), F32),
        ],
        compiler_params=pltpu.CompilerParams(vmem_limit_bytes=40 << 20),
        cost_estimate=pl.CostEstimate(flops=4 * 6 * 6 * 512 * 1024 * 512, bytes_accessed=16 << 20, transcendentals=0),
        name="head_and_grads",
    )(footprint, edge, halo, near, mat1, mat2, down_mat, back_mat, w_head.reshape(1, 64), labels[0])

    swap = [(i, 1 - i) for i in range(reps)]
    got = lax.ppermute(send, "rep", swap)
    mine = keep[0] + got[0]
    for step in range(1, chans):
        ring = [(i, (i + step) % chans) for i in range(chans)]
        mine = mine + lax.ppermute(keep[step] + got[step], "chan", ring)
    step = 1
    while step < bricks:
        mine = mine + lax.ppermute(mine, "bricks", [(i, i ^ step) for i in range(bricks)])
        step *= 2
    peer = lax.ppermute(mine, "rep", swap)
    share = 64 // chans
    second, down, head, loss = pl.pallas_call(
        final_kernel,
        out_shape=(
            jax.ShapeDtypeStruct((27, share, 64), F32),
            jax.ShapeDtypeStruct((8, share, 64), F32),
            jax.ShapeDtypeStruct((1, 64), F32),
            jax.ShapeDtypeStruct((1, 1), F32),
        ),
        in_specs=[smem, vmem, vmem],
        out_specs=(vmem,) * 4,
        name="assemble",
    )(footprint, mine, peer)
    return second.transpose(0, 2, 1), down, head.reshape(64), loss.reshape(1)


def solution(mesh):
    return jax.shard_map(
        shards,
        mesh=mesh,
        in_specs=(
            P(("groups", "bricks", "rep"), None, None, None, None),
            P(None, None, "chan"),
            P(None, None, "chan"),
            P(None, "chan", None),
            P(),
            P(None, "groups"),
            P(("groups", "bricks", "rep"), None, None),
        ),
        out_specs=(P("groups", None, "chan"), P("groups", "chan", None), P("groups"), P("groups")),
        check_vma=False,
    )
```

```python
import jax
import jax.numpy as jnp
from jax import lax
from jax.experimental import pallas as pl
from jax.experimental.pallas import tpu as pltpu
from jax.sharding import PartitionSpec as P

BRICK = 8
COARSE = 1024
ROWS = 256
F32 = jnp.float32
BF16 = jnp.bfloat16


def lanes_low(shape):
    return lax.broadcasted_iota(jnp.int32, shape, len(shape) - 1) % 128 < 64


def merge_half(low, high):
    return jnp.where(lanes_low(low.shape), low, high)


def shifted(value, by):
    row = lax.broadcasted_iota(jnp.int32, value.shape, 0) % 128
    inside = row >= by if by > 0 else row < 128 + by
    return jnp.where(inside, pltpu.roll(value, by % value.shape[0], 0), 0.0)


def build_conv(w_ref, out_ref):
    zero = jnp.zeros((64, 128), BF16)
    for e in range(3):
        for k in range(4):
            for slot, d in enumerate((0, 1, 2, -1)):
                for rx in range(2):
                    a = k - rx
                    halves = []
                    for ry in range(2):
                        b = d - ry + 1
                        live = 0 <= a < 3 and 0 <= b < 3
                        halves.append(w_ref[9 * a + 3 * b + e] if live else zero)
                    row = k * 256 + slot * 64
                    out_ref[e, row : row + 64, rx * 128 : rx * 128 + 128] = merge_half(*halves)


def conv_rows(window_ref, w_ref, slot=()):
    lhs = jnp.concatenate(
        [window_ref[(*slot, pl.ds(2 * k, 2))].reshape(2 * ROWS, 256) for k in range(4)], axis=1
    )
    below, level, above = [jnp.dot(lhs, w_ref[e], preferred_element_type=F32) for e in range(3)]
    return level + shifted(below, 2) + shifted(above, -2)


def gated(ref, plane, index, count):
    inside = (index >= 0) & (index < count)
    block = ref[plane, jnp.clip(index, 0, ref.shape[1] - 1)]
    return jnp.where(inside, block, jnp.zeros_like(block))


def turn_block(src_ref, dst_ref, plane, t):
    for py in range(2):
        tall = jnp.concatenate([src_ref[plane, 4 * t + py], src_ref[plane, 4 * t + 2 + py]], axis=0)
        dst_ref[plane, t, 128 * py : 128 * py + 128] = tall.T


def fill_window(window_ref, plane, src_ref, src_plane, index, count):
    window_ref[plane, :, 0:128] = gated(src_ref, src_plane, index, count)
    window_ref[plane, :, 128:256] = merge_half(
        gated(src_ref, src_plane, index + 1, count), gated(src_ref, src_plane, index - 1, count)
    )


def pack_kernel(w1_ref, w2_ref, wd_ref, out_ref):
    half = w1_ref.shape[1] // 2
    start = 0
    for ref in (w1_ref, w2_ref, wd_ref):
        stop = start + ref.shape[0]
        out_ref[start:stop] = jnp.concatenate([ref[:, :half], ref[:, half:]], axis=2)
        start = stop


def local_kernel(foot_ref, feat_ref, *refs):
    chans = lax.axis_size("chan")
    piece_refs = refs[:chans]
    edge_ref, y1_ref, m1_ref, m2_ref, down_ref, back_ref, whole, turned, arranged = refs[chans:-2]
    even_window, odd_window = refs[-2:]
    column = lax.axis_index("bricks") * lax.axis_size("rep") + lax.axis_index("rep")
    me = lax.axis_index("chan")
    side = me * (BRICK // chans) // 4
    count = 2 * foot_ref[1, column]

    half = piece_refs[0].shape[1]
    for step in range(chans):
        block = piece_refs[step][...]
        source = lax.rem(me - step + chans, chans)
        for h in range(2):
            part = block[:, :, 64 * h : 64 * h + 64]
            rows = pl.ds(pl.multiple_of((2 * source + h) * half, half), half)
            whole[:, rows, :] = jnp.concatenate([part, part], axis=2)
    for t in range(54):
        turned[t] = jnp.concatenate([whole[t], whole[t]], axis=0).T[0:64]
    build_conv(turned.at[0:27], m1_ref)
    build_conv(turned.at[27:54], m2_ref)
    low = lanes_low((64, 128))
    zero = jnp.zeros((64, 128), BF16)
    for t in range(8):
        ab, e = t // 2, t % 2
        block = whole[54 + t]
        tile = jnp.concatenate([jnp.where(low, block, zero), jnp.where(low, zero, block)], axis=0)
        down_ref[ab * 128 : ab * 128 + 128, e * 128 : e * 128 + 128] = tile
        back_ref[:, t * 128 : t * 128 + 128] = tile.T

    def turn(t, carry):
        for p in range(8):
            turn_block(feat_ref, arranged, p, t)
        for p in range(4):
            edge_ref[p, t] = arranged[4 * side + p, t]
        return carry

    lax.fori_loop(0, count, turn, 0)

    def fill(window, t):
        for p in range(8):
            fill_window(window, p, arranged, p, t, count)

    def conv(window, t):
        out = jnp.maximum(conv_rows(window, m1_ref), 0.0).astype(BF16)
        for par in range(2):
            for rx in range(2):
                y1_ref[2 * rx + par, t] = out[ROWS * par : ROWS * par + ROWS, 128 * rx : 128 * rx + 128]

    def pair(j, carry):
        fill(odd_window, 2 * j + 1)
        conv(even_window, 2 * j)
        fill(even_window, 2 * j + 2)
        conv(odd_window, 2 * j + 1)
        return carry

    fill(even_window, 0)
    lax.fori_loop(0, count // 2, pair, 0)


def main_kernel(
    foot_ref,
    edge_ref,
    halo_ref,
    near_ref,
    m1_ref,
    m2_ref,
    down_mat,
    back_mat,
    head_ref,
    label_ref,
    keep_ref,
    send_ref,
    arranged,
    even_window,
    odd_window,
    hidden,
    hwin,
    headm_ref,
    y2_ref,
    delta_t,
    err_t,
    grad,
    grad_down,
    small,
    whole,
):
    reps, chans = lax.axis_size("rep"), lax.axis_size("chan")
    columns = lax.axis_size("bricks") * reps
    column = lax.axis_index("bricks") * reps + lax.axis_index("rep")
    planes = BRICK // chans
    mine = lax.axis_index("chan") * planes
    side = mine // 4
    other = column + 2 * side - 1
    present = (other >= 0) & (other < columns)
    other = jnp.clip(other, 0, columns - 1)
    count = 2 * foot_ref[1, column]
    other_count = jnp.where(present, 2 * foot_ref[1, other], 0)
    offset = 2 * (foot_ref[0, other] - foot_ref[0, column])

    grad[...] = jnp.zeros_like(grad)
    grad_down[...] = jnp.zeros_like(grad_down)
    small[...] = jnp.zeros_like(small)
    head_row = jnp.concatenate([head_ref[...], head_ref[...]], axis=1)
    square_row = lax.broadcasted_iota(jnp.int32, (128, 128), 0)
    square_lane = lax.broadcasted_iota(jnp.int32, (128, 128), 1)
    same_half = (square_row < 64) == (square_lane < 64)
    head_mat = jnp.where(same_half, jnp.broadcast_to(head_row, (128, 128)).T, 0.0)
    head_high = head_mat.astype(BF16)
    headm_ref[0:128] = head_high
    headm_ref[128:256] = head_high
    headm_ref[256:384] = (head_mat - head_high.astype(F32)).astype(BF16)
    pick_depth = jnp.where(square_row // 2 == square_lane % 64, 1.0, 0.0).astype(BF16)

    def turn(t, carry):
        for p in range(4):
            turn_block(halo_ref, arranged, p, t)
        return carry

    lax.fori_loop(0, other_count, turn, 0)

    def fill(window, t):
        for p in range(4):
            fill_window(window, (1 - side) * 4 + p, edge_ref, p, t, count)
            fill_window(window, side * 4 + p, arranged, p, t - offset, other_count)

    def first(window, t):
        own = (t >= 0) & (t < count)
        next_to = (t - offset >= 0) & (t - offset < other_count)
        out = jnp.maximum(conv_rows(window, m1_ref), 0.0).astype(BF16)
        for rx in range(2):
            live = jnp.where(side == rx, next_to, own)
            for par in range(2):
                block = out[ROWS * par : ROWS * par + ROWS, 128 * rx : 128 * rx + 128]
                hidden[t + 1, side * 4 + 2 * rx + par] = jnp.where(live, block, jnp.zeros_like(block))

    def near(t):
        for p in range(4):
            hidden[t + 1, (1 - side) * 4 + p] = gated(near_ref, p, t, count)

    def rim(i, carry):
        t = jnp.where(i == 0, -1, count)
        beside = (t - offset >= 0) & (t - offset < other_count)
        hidden[t + 1] = jnp.zeros((8, ROWS, 128), BF16)

        @pl.when(beside)
        def _():
            fill(even_window, t)
            first(even_window, t)

        return carry

    def pair(j, carry):
        fill(odd_window, 2 * j + 1)
        near(2 * j)
        first(even_window, 2 * j)
        fill(even_window, 2 * j + 2)
        near(2 * j + 1)
        first(odd_window, 2 * j + 1)
        return carry

    lax.fori_loop(0, 2, rim, 0)
    fill(even_window, 0)
    lax.fori_loop(0, count // 2, pair, 0)

    row4 = lax.broadcasted_iota(jnp.int32, (512, 128), 0)
    even4 = row4 % 2 == 0
    plane4 = 4 * side + 2 * (row4 // 128 % 2)
    keep = even4 & (plane4 >= mine) & (plane4 < mine + planes)

    def second(j, carry):
        for u in range(2):
            t = 2 * j + u
            for p in range(8):
                hwin[u, p, :, 0:128] = hidden[t + 1, p]
                hwin[u, p, :, 128:256] = merge_half(hidden[t + 2, p], hidden[t, p])
            out = jnp.maximum(conv_rows(hwin, m2_ref, (u,)), 0.0).astype(BF16)
            for par in range(2):
                for rx in range(2):
                    y2_ref[u, rx, par] = out[ROWS * par : ROWS * par + ROWS, 128 * rx : 128 * rx + 128]
        fine = jnp.concatenate(
            [
                jnp.concatenate(
                    [y2_ref[u, rx, a, 128 * b : 128 * b + 128] for u in range(2) for rx in range(2)],
                    axis=0,
                )
                for a in range(2)
                for b in range(2)
            ],
            axis=1,
        )
        both = jnp.dot(fine, down_mat[...], preferred_element_type=F32)
        coarse = both[:, 0:128] + shifted(both[:, 128:256], -1)
        rect = jnp.maximum(coarse, 0.0)
        high = rect.astype(BF16)
        rest = (rect - high.astype(F32)).astype(BF16)
        logit = jnp.dot(
            jnp.concatenate([high, rest, high], axis=1), headm_ref[...], preferred_element_type=F32
        )
        labels = []
        for u in range(2):
            line = label_ref[:, pl.ds(pl.multiple_of(256 * j + 128 * u, 128), 128)].astype(F32)
            for rx in range(2):
                row = jnp.where(side == 1, line[2 + rx : 3 + rx], line[rx : rx + 1])
                row = jnp.where(same_half, jnp.broadcast_to(row, (128, 128)), 0.0).astype(BF16)
                labels.append(
                    lax.dot_general(
                        pick_depth, row, (((1,), (1,)), ((), ())), preferred_element_type=F32
                    )
                )
        label = jnp.concatenate(labels, axis=0)
        tail = jnp.exp(-jnp.abs(logit))
        soft = jnp.maximum(logit, 0.0) + jnp.log1p(tail)
        sigmoid = jnp.where(logit >= 0.0, 1.0, tail) / (1.0 + tail)
        loss = jnp.where(keep, soft - label * logit, 0.0)
        slope = jnp.where(keep, (sigmoid - label) * (1.0 / COARSE), 0.0)
        small[0:1] += jnp.sum(slope * rect, axis=0, keepdims=True)
        small[1:2] += jnp.sum(loss, axis=0, keepdims=True)
        delta = jnp.where(coarse > 0.0, slope * head_row, 0.0).astype(BF16).astype(F32)
        moved = shifted(delta, 1)
        delta_t[0:128] = delta.astype(BF16).T
        delta_t[128:256] = moved.astype(BF16).T
        back = jnp.dot((delta + moved).astype(BF16), back_mat[...], preferred_element_type=F32)
        for a in range(2):
            for b in range(2):
                lane = (2 * a + b) * 256
                err = jnp.where(even4, back[:, lane : lane + 128], back[:, lane + 128 : lane + 256])
                live = fine[:, lane // 2 : lane // 2 + 128].astype(F32) > 0.0
                err = jnp.where(live, err, 0.0)
                for n in range(4):
                    turned = err[128 * n : 128 * n + 128].astype(BF16).T
                    col = n * 512 + a * 256 + b * 128
                    err_t[128:256, col : col + 128] = turned
                    up = jnp.where(square_lane < 126, pltpu.roll(turned, 126, 1), jnp.zeros_like(turned))
                    down = jnp.where(square_lane >= 2, pltpu.roll(turned, 2, 1), jnp.zeros_like(turned))
                    err_t[0:128, col : col + 128] = up
                    err_t[256:384, col : col + 128] = down
        grad_down[...] += jnp.dot(delta_t[...], fine, preferred_element_type=F32)
        for a in range(3):
            rows = hwin[:, 2 * a : 2 * a + 4].reshape(8 * ROWS, 256)
            grad[a] += jnp.dot(err_t[...], rows, preferred_element_type=F32)
        return carry

    lax.fori_loop(0, count // 2, second, 0)

    low = lanes_low((64, 128))
    rep, chan = lax.axis_index("rep"), lax.axis_index("chan")
    share = 64 // chans // reps

    def emit(slab, value):
        whole[slab] = value

    firsts = []
    for a in range(3):
        for e in range(3):
            both = grad[a, 128 * e : 128 * e + 64] + pltpu.roll(
                grad[a, 128 * e + 64 : 128 * e + 128], 192, 1
            )
            emit(3 * a + e, both[:, 0:128])
            firsts.append(both[:, 128:256])
    for m in range(5):
        right = firsts[2 * m + 1] if 2 * m + 1 < 9 else jnp.zeros_like(firsts[0])
        emit(9 + m, jnp.where(low, pltpu.roll(firsts[2 * m], 64, 1), right))
    halves = [
        grad_down[128 * e : 128 * e + 64] + pltpu.roll(grad_down[128 * e + 64 : 128 * e + 128], 448, 1)
        for e in range(2)
    ]
    for ab in range(4):
        tile = jnp.concatenate([half[:, 128 * ab : 128 * ab + 128] for half in halves], axis=0)
        emit(14 + ab, tile.T[0:64])
    sums = small[...]
    head = sums[0:1] + pltpu.roll(sums, 64, 1)[0:1]
    total = jnp.sum(sums[1:2], axis=1, keepdims=True) * (1.0 / 64)
    row = merge_half(head, jnp.broadcast_to(total, (1, 128)))
    emit(18, jnp.broadcast_to(row, (64, 128)))
    for c in range(chans):
        place = lax.rem(c - chan + chans, chans)
        for ref, r in ((keep_ref, rep), (send_ref, 1 - rep)):
            rows = pl.ds(pl.multiple_of((c * reps + r) * share, share), share)
            ref[place] = whole[:, rows, :]


def final_kernel(foot_ref, mine_ref, peer_ref, second_ref, down_ref, head_ref, loss_ref):
    rep = lax.axis_index("rep")
    share = mine_ref.shape[1]
    for ref, r in ((mine_ref, rep), (peer_ref, 1 - rep)):
        rows = pl.ds(pl.multiple_of(r * share, share), share)
        for a in range(3):
            for e in range(3):
                m = 3 * a + e
                later, first = ref[m], ref[9 + m // 2]
                second_ref[9 * a + e, rows] = first[:, 64 * (m % 2) : 64 * (m % 2) + 64]
                second_ref[9 * a + 3 + e, rows] = later[:, 0:64]
                second_ref[9 * a + 6 + e, rows] = later[:, 64:128]
        for ab in range(4):
            for e in range(2):
                down_ref[2 * ab + e, rows] = ref[14 + ab][:, 64 * e : 64 * e + 64]
    line = mine_ref[18][0:1]
    head_ref[...] = line[:, 0:64]
    live = foot_ref[1, 0]
    for c in range(1, foot_ref.shape[1]):
        live += foot_ref[1, c]
    scale = jnp.full((1, 1), COARSE * live, jnp.int32).astype(F32)
    loss_ref[...] = line[:, 64:65] / scale


def sums_slab(shape):
    return lax.broadcasted_iota(jnp.int32, shape, 0) == 18


def to_wire(value):
    high = lax.reduce_precision(value, 8, 7)
    rest = lax.reduce_precision(value - high, 8, 7)
    lower = lax.broadcasted_iota(jnp.int32, value.shape, 1) >= value.shape[1] // 2
    return jnp.where(sums_slab(value.shape) & lower, rest, high)


def from_wire(value):
    half = value.shape[1] // 2
    other = jnp.concatenate([value[:, half:], value[:, :half]], axis=1)
    return value + jnp.where(sums_slab(value.shape), other, 0.0)


def send_sum(value, axis, pairs):
    wire = to_wire(value)
    return from_wire(wire), from_wire(lax.ppermute(wire.astype(BF16), axis, pairs).astype(F32))


def shards(features, w_first, w_second, w_down, w_head, footprint, labels):
    bricks, chans, reps = lax.axis_size("bricks"), lax.axis_size("chan"), lax.axis_size("rep")
    planes = BRICK // chans
    side = lax.axis_index("chan") * planes // 4
    smem = pl.BlockSpec(memory_space=pltpu.SMEM)
    vmem = pl.BlockSpec(memory_space=pltpu.VMEM)
    features = features[0]
    slabs = features.shape[2] // 4

    packed = pl.pallas_call(
        pack_kernel,
        out_shape=jax.ShapeDtypeStruct((62, 32 // chans, 128), BF16),
        in_specs=[vmem] * 3,
        out_specs=vmem,
        name="pack",
    )(w_first.transpose(0, 2, 1), w_second.transpose(0, 2, 1), w_down)
    pieces = [packed]
    for step in range(1, chans):
        ring = [(i, (i + step) % chans) for i in range(chans)]
        pieces.append(lax.ppermute(packed, "chan", ring))

    pairs = []
    for col in range(bricks * reps):
        for c in range(chans):
            src = col + 2 * (c * planes // 4) - 1
            if 0 <= src < bricks * reps:
                ends = [(j // reps * chans + c) * reps + j % reps for j in (src, col)]
                pairs.append(tuple(ends))
    outward = lax.dynamic_slice_in_dim(features, (1 - side) * 4, 4, 1).transpose(1, 2, 0, 3)
    halo = lax.ppermute(outward, ("bricks", "chan", "rep"), pairs)

    edge, near, mat1, mat2, down_mat, back_mat = pl.pallas_call(
        local_kernel,
        out_shape=(
            jax.ShapeDtypeStruct((4, slabs, ROWS, 128), BF16),
            jax.ShapeDtypeStruct((4, slabs, ROWS, 128), BF16),
            jax.ShapeDtypeStruct((3, 1024, 256), BF16),
            jax.ShapeDtypeStruct((3, 1024, 256), BF16),
            jax.ShapeDtypeStruct((512, 256), BF16),
            jax.ShapeDtypeStruct((128, 1024), BF16),
        ),
        in_specs=[smem] + [vmem] * (1 + chans),
        out_specs=(vmem,) * 6,
        scratch_shapes=[
            pltpu.VMEM((62, 64, 128), BF16),
            pltpu.VMEM((54, 64, 128), BF16),
            pltpu.VMEM((8, slabs, ROWS, 128), BF16),
            pltpu.VMEM((8, ROWS, 256), BF16),
            pltpu.VMEM((8, ROWS, 256), BF16),
        ],
        compiler_params=pltpu.CompilerParams(vmem_limit_bytes=36 << 20),
        cost_estimate=pl.CostEstimate(flops=6 * 6 * 512 * 1024 * 512, bytes_accessed=8 << 20, transcendentals=0),
        name="first_local",
    )(footprint, features.transpose(1, 2, 0, 3), *pieces)
    parts = jax.ShapeDtypeStruct((chans, 19, 64 // chans // reps, 128), F32)
    keep, send = pl.pallas_call(
        main_kernel,
        out_shape=(parts, parts),
        in_specs=[smem] + [vmem] * 9,
        out_specs=(vmem, vmem),
        scratch_shapes=[
            pltpu.VMEM((4, slabs, ROWS, 128), BF16),
            pltpu.VMEM((8, ROWS, 256), BF16),
            pltpu.VMEM((8, ROWS, 256), BF16),
            pltpu.VMEM((slabs + 2, 8, ROWS, 128), BF16),
            pltpu.VMEM((2, 8, ROWS, 256), BF16),
            pltpu.VMEM((384, 128), BF16),
            pltpu.VMEM((2, 2, 2, ROWS, 128), BF16),
            pltpu.VMEM((256, 512), BF16),
            pltpu.VMEM((384, 2048), BF16),
            pltpu.VMEM((3, 384, 256), F32),
            pltpu.VMEM((256, 512), F32),
            pltpu.VMEM((8, 128), F32),
            pltpu.VMEM((19, 64, 128), F32),
        ],
        compiler_params=pltpu.CompilerParams(vmem_limit_bytes=40 << 20),
        cost_estimate=pl.CostEstimate(flops=4 * 6 * 6 * 512 * 1024 * 512, bytes_accessed=16 << 20, transcendentals=0),
        name="head_and_grads",
    )(footprint, edge, halo, near, mat1, mat2, down_mat, back_mat, w_head.reshape(1, 64), labels[0])

    swap = [(i, 1 - i) for i in range(reps)]
    got = lax.ppermute(send, "rep", swap)
    mine = keep[0] + got[0]
    for step in range(1, chans):
        ring = [(i, (i + step) % chans) for i in range(chans)]
        mine = mine + send_sum(keep[step] + got[step], "chan", ring)[1]
    step = 1
    while step < bricks:
        mine = sum(send_sum(mine, "bricks", [(i, i ^ step) for i in range(bricks)]))
        step *= 2
    peer = lax.ppermute(mine, "rep", swap)
    share = 64 // chans
    second, down, head, loss = pl.pallas_call(
        final_kernel,
        out_shape=(
            jax.ShapeDtypeStruct((27, share, 64), F32),
            jax.ShapeDtypeStruct((8, share, 64), F32),
            jax.ShapeDtypeStruct((1, 64), F32),
            jax.ShapeDtypeStruct((1, 1), F32),
        ),
        in_specs=[smem, vmem, vmem],
        out_specs=(vmem,) * 4,
        name="assemble",
    )(footprint, mine, peer)
    return second.transpose(0, 2, 1), down, head.reshape(64), loss.reshape(1)


def solution(mesh):
    return jax.shard_map(
        shards,
        mesh=mesh,
        in_specs=(
            P(("groups", "bricks", "rep"), None, None, None, None),
            P(None, None, "chan"),
            P(None, None, "chan"),
            P(None, "chan", None),
            P(),
            P(None, "groups"),
            P(("groups", "bricks", "rep"), None, None),
        ),
        out_specs=(P("groups", None, "chan"), P("groups", "chan", None), P("groups"), P("groups")),
        check_vma=False,
    )
```

```python
import jax
import jax.numpy as jnp
from jax import lax
from jax.experimental import pallas as pl
from jax.experimental.pallas import tpu as pltpu
from jax.sharding import PartitionSpec as P

BRICK = 8
COARSE = 1024
ROWS = 256
F32 = jnp.float32
BF16 = jnp.bfloat16


def lanes_low(shape):
    return lax.broadcasted_iota(jnp.int32, shape, len(shape) - 1) % 128 < 64


def merge_half(low, high):
    return jnp.where(lanes_low(low.shape), low, high)


def shifted(value, by):
    row = lax.broadcasted_iota(jnp.int32, value.shape, 0) % 128
    inside = row >= by if by > 0 else row < 128 + by
    return jnp.where(inside, pltpu.roll(value, by % value.shape[0], 0), 0.0)


def build_conv(w_ref, out_ref):
    zero = jnp.zeros((64, 128), BF16)
    for e in range(3):
        for k in range(4):
            for slot, d in enumerate((0, 1, 2, -1)):
                for rx in range(2):
                    a = k - rx
                    halves = []
                    for ry in range(2):
                        b = d - ry + 1
                        live = 0 <= a < 3 and 0 <= b < 3
                        halves.append(w_ref[9 * a + 3 * b + e] if live else zero)
                    row = k * 256 + slot * 64
                    out_ref[e, row : row + 64, rx * 128 : rx * 128 + 128] = merge_half(*halves)


def conv_rows(window_ref, w_ref, slot=()):
    lhs = jnp.concatenate(
        [window_ref[(*slot, pl.ds(2 * k, 2))].reshape(2 * ROWS, 256) for k in range(4)], axis=1
    )
    below, level, above = [jnp.dot(lhs, w_ref[e], preferred_element_type=F32) for e in range(3)]
    return level + shifted(below, 2) + shifted(above, -2)


def gated(ref, plane, index, count):
    inside = (index >= 0) & (index < count)
    block = ref[plane, jnp.clip(index, 0, ref.shape[1] - 1)]
    return jnp.where(inside, block, jnp.zeros_like(block))


def turn_block(src_ref, dst_ref, plane, t):
    for py in range(2):
        tall = jnp.concatenate([src_ref[plane, 4 * t + py], src_ref[plane, 4 * t + 2 + py]], axis=0)
        dst_ref[plane, t, 128 * py : 128 * py + 128] = tall.T


def fill_window(window_ref, plane, src_ref, src_plane, index, count):
    window_ref[plane, :, 0:128] = gated(src_ref, src_plane, index, count)
    window_ref[plane, :, 128:256] = merge_half(
        gated(src_ref, src_plane, index + 1, count), gated(src_ref, src_plane, index - 1, count)
    )


def pack_kernel(w1_ref, w2_ref, wd_ref, out_ref):
    half = w1_ref.shape[1] // 2
    start = 0
    for ref in (w1_ref, w2_ref, wd_ref):
        stop = start + ref.shape[0]
        out_ref[start:stop] = jnp.concatenate([ref[:, :half], ref[:, half:]], axis=2)
        start = stop


def local_kernel(foot_ref, feat_ref, *refs):
    chans = lax.axis_size("chan")
    piece_refs = refs[:chans]
    edge_ref, y1_ref, m1_ref, m2_ref, down_ref, back_ref, whole, turned, arranged = refs[chans:-2]
    even_window, odd_window = refs[-2:]
    column = lax.axis_index("bricks") * lax.axis_size("rep") + lax.axis_index("rep")
    me = lax.axis_index("chan")
    side = me * (BRICK // chans) // 4
    count = 2 * foot_ref[1, column]

    half = piece_refs[0].shape[1]
    for step in range(chans):
        block = piece_refs[step][...]
        source = lax.rem(me - step + chans, chans)
        for h in range(2):
            part = block[:, :, 64 * h : 64 * h + 64]
            rows = pl.ds(pl.multiple_of((2 * source + h) * half, half), half)
            whole[:, rows, :] = jnp.concatenate([part, part], axis=2)
    for t in range(54):
        turned[t] = jnp.concatenate([whole[t], whole[t]], axis=0).T[0:64]
    build_conv(turned.at[0:27], m1_ref)
    build_conv(turned.at[27:54], m2_ref)
    low = lanes_low((64, 128))
    zero = jnp.zeros((64, 128), BF16)
    for t in range(8):
        ab, e = t // 2, t % 2
        block = whole[54 + t]
        tile = jnp.concatenate([jnp.where(low, block, zero), jnp.where(low, zero, block)], axis=0)
        down_ref[ab * 128 : ab * 128 + 128, e * 128 : e * 128 + 128] = tile
        back_ref[:, t * 128 : t * 128 + 128] = tile.T

    def turn(t, carry):
        for p in range(8):
            turn_block(feat_ref, arranged, p, t)
        for p in range(4):
            edge_ref[p, t] = arranged[4 * side + p, t]
        return carry

    lax.fori_loop(0, count, turn, 0)

    def fill(window, t):
        for p in range(8):
            fill_window(window, p, arranged, p, t, count)

    def conv(window, t):
        out = jnp.maximum(conv_rows(window, m1_ref), 0.0).astype(BF16)
        for par in range(2):
            for rx in range(2):
                y1_ref[2 * rx + par, t] = out[ROWS * par : ROWS * par + ROWS, 128 * rx : 128 * rx + 128]

    def pair(j, carry):
        fill(odd_window, 2 * j + 1)
        conv(even_window, 2 * j)
        fill(even_window, 2 * j + 2)
        conv(odd_window, 2 * j + 1)
        return carry

    fill(even_window, 0)
    lax.fori_loop(0, count // 2, pair, 0)


def main_kernel(
    foot_ref,
    edge_ref,
    halo_ref,
    near_ref,
    m1_ref,
    m2_ref,
    down_mat,
    back_mat,
    head_ref,
    label_ref,
    keep_ref,
    send_ref,
    arranged,
    even_window,
    odd_window,
    hidden,
    hwin,
    headm_ref,
    y2_ref,
    delta_t,
    err_t,
    grad,
    grad_down,
    small,
    whole,
):
    reps, chans = lax.axis_size("rep"), lax.axis_size("chan")
    columns = lax.axis_size("bricks") * reps
    column = lax.axis_index("bricks") * reps + lax.axis_index("rep")
    planes = BRICK // chans
    mine = lax.axis_index("chan") * planes
    side = mine // 4
    other = column + 2 * side - 1
    present = (other >= 0) & (other < columns)
    other = jnp.clip(other, 0, columns - 1)
    count = 2 * foot_ref[1, column]
    other_count = jnp.where(present, 2 * foot_ref[1, other], 0)
    offset = 2 * (foot_ref[0, other] - foot_ref[0, column])

    grad[...] = jnp.zeros_like(grad)
    grad_down[...] = jnp.zeros_like(grad_down)
    small[...] = jnp.zeros_like(small)
    head_row = jnp.concatenate([head_ref[...], head_ref[...]], axis=1)
    square_row = lax.broadcasted_iota(jnp.int32, (128, 128), 0)
    square_lane = lax.broadcasted_iota(jnp.int32, (128, 128), 1)
    same_half = (square_row < 64) == (square_lane < 64)
    head_mat = jnp.where(same_half, jnp.broadcast_to(head_row, (128, 128)).T, 0.0)
    head_high = head_mat.astype(BF16)
    headm_ref[0:128] = head_high
    headm_ref[128:256] = head_high
    headm_ref[256:384] = (head_mat - head_high.astype(F32)).astype(BF16)
    pick_depth = jnp.where(square_row // 2 == square_lane % 64, 1.0, 0.0).astype(BF16)

    def turn(t, carry):
        for p in range(4):
            turn_block(halo_ref, arranged, p, t)
        return carry

    lax.fori_loop(0, other_count, turn, 0)

    def fill(window, t):
        for p in range(4):
            fill_window(window, (1 - side) * 4 + p, edge_ref, p, t, count)
            fill_window(window, side * 4 + p, arranged, p, t - offset, other_count)

    def first(window, t):
        own = (t >= 0) & (t < count)
        next_to = (t - offset >= 0) & (t - offset < other_count)
        out = jnp.maximum(conv_rows(window, m1_ref), 0.0).astype(BF16)
        for rx in range(2):
            live = jnp.where(side == rx, next_to, own)
            for par in range(2):
                block = out[ROWS * par : ROWS * par + ROWS, 128 * rx : 128 * rx + 128]
                hidden[t + 1, side * 4 + 2 * rx + par] = jnp.where(live, block, jnp.zeros_like(block))

    def near(t):
        for p in range(4):
            hidden[t + 1, (1 - side) * 4 + p] = gated(near_ref, p, t, count)

    def rim(i, carry):
        t = jnp.where(i == 0, -1, count)
        beside = (t - offset >= 0) & (t - offset < other_count)
        hidden[t + 1] = jnp.zeros((8, ROWS, 128), BF16)

        @pl.when(beside)
        def _():
            fill(even_window, t)
            first(even_window, t)

        return carry

    def pair(j, carry):
        fill(odd_window, 2 * j + 1)
        near(2 * j)
        first(even_window, 2 * j)
        fill(even_window, 2 * j + 2)
        near(2 * j + 1)
        first(odd_window, 2 * j + 1)
        return carry

    lax.fori_loop(0, 2, rim, 0)
    fill(even_window, 0)
    lax.fori_loop(0, count // 2, pair, 0)

    row4 = lax.broadcasted_iota(jnp.int32, (512, 128), 0)
    even4 = row4 % 2 == 0
    plane4 = 4 * side + 2 * (row4 // 128 % 2)
    keep = even4 & (plane4 >= mine) & (plane4 < mine + planes)

    def second(j, carry):
        for u in range(2):
            t = 2 * j + u
            for p in range(8):
                hwin[u, p, :, 0:128] = hidden[t + 1, p]
                hwin[u, p, :, 128:256] = merge_half(hidden[t + 2, p], hidden[t, p])
            out = jnp.maximum(conv_rows(hwin, m2_ref, (u,)), 0.0).astype(BF16)
            for par in range(2):
                for rx in range(2):
                    y2_ref[u, rx, par] = out[ROWS * par : ROWS * par + ROWS, 128 * rx : 128 * rx + 128]
        fine = jnp.concatenate(
            [
                jnp.concatenate(
                    [y2_ref[u, rx, a, 128 * b : 128 * b + 128] for u in range(2) for rx in range(2)],
                    axis=0,
                )
                for a in range(2)
                for b in range(2)
            ],
            axis=1,
        )
        both = jnp.dot(fine, down_mat[...], preferred_element_type=F32)
        coarse = both[:, 0:128] + shifted(both[:, 128:256], -1)
        rect = jnp.maximum(coarse, 0.0)
        high = rect.astype(BF16)
        rest = (rect - high.astype(F32)).astype(BF16)
        logit = jnp.dot(
            jnp.concatenate([high, rest, high], axis=1), headm_ref[...], preferred_element_type=F32
        )
        labels = []
        for u in range(2):
            line = label_ref[:, pl.ds(pl.multiple_of(256 * j + 128 * u, 128), 128)].astype(F32)
            for rx in range(2):
                row = jnp.where(side == 1, line[2 + rx : 3 + rx], line[rx : rx + 1])
                row = jnp.where(same_half, jnp.broadcast_to(row, (128, 128)), 0.0).astype(BF16)
                labels.append(
                    lax.dot_general(
                        pick_depth, row, (((1,), (1,)), ((), ())), preferred_element_type=F32
                    )
                )
        label = jnp.concatenate(labels, axis=0)
        tail = jnp.exp(-jnp.abs(logit))
        soft = jnp.maximum(logit, 0.0) + jnp.log1p(tail)
        sigmoid = jnp.where(logit >= 0.0, 1.0, tail) / (1.0 + tail)
        loss = jnp.where(keep, soft - label * logit, 0.0)
        slope = jnp.where(keep, (sigmoid - label) * (1.0 / COARSE), 0.0)
        small[0:1] += jnp.sum(slope * rect, axis=0, keepdims=True)
        small[1:2] += jnp.sum(loss, axis=0, keepdims=True)
        delta = jnp.where(coarse > 0.0, slope * head_row, 0.0).astype(BF16).astype(F32)
        moved = shifted(delta, 1)
        delta_t[0:128] = delta.astype(BF16).T
        delta_t[128:256] = moved.astype(BF16).T
        back = jnp.dot((delta + moved).astype(BF16), back_mat[...], preferred_element_type=F32)
        for a in range(2):
            for b in range(2):
                lane = (2 * a + b) * 256
                err = jnp.where(even4, back[:, lane : lane + 128], back[:, lane + 128 : lane + 256])
                live = fine[:, lane // 2 : lane // 2 + 128].astype(F32) > 0.0
                err = jnp.where(live, err, 0.0)
                for n in range(4):
                    turned = err[128 * n : 128 * n + 128].astype(BF16).T
                    col = n * 512 + a * 256 + b * 128
                    err_t[128:256, col : col + 128] = turned
                    up = jnp.where(square_lane < 126, pltpu.roll(turned, 126, 1), jnp.zeros_like(turned))
                    down = jnp.where(square_lane >= 2, pltpu.roll(turned, 2, 1), jnp.zeros_like(turned))
                    err_t[0:128, col : col + 128] = up
                    err_t[256:384, col : col + 128] = down
        grad_down[...] += jnp.dot(delta_t[...], fine, preferred_element_type=F32)
        for a in range(3):
            rows = hwin[:, 2 * a : 2 * a + 4].reshape(8 * ROWS, 256)
            grad[a] += jnp.dot(err_t[...], rows, preferred_element_type=F32)
        return carry

    lax.fori_loop(0, count // 2, second, 0)

    low = lanes_low((64, 128))
    rep, chan = lax.axis_index("rep"), lax.axis_index("chan")
    share = 64 // chans // reps

    def emit(slab, value):
        whole[slab] = value

    firsts = []
    for a in range(3):
        for e in range(3):
            both = grad[a, 128 * e : 128 * e + 64] + pltpu.roll(
                grad[a, 128 * e + 64 : 128 * e + 128], 192, 1
            )
            emit(3 * a + e, both[:, 0:128])
            firsts.append(both[:, 128:256])
    for m in range(5):
        right = firsts[2 * m + 1] if 2 * m + 1 < 9 else jnp.zeros_like(firsts[0])
        emit(9 + m, jnp.where(low, pltpu.roll(firsts[2 * m], 64, 1), right))
    halves = [
        grad_down[128 * e : 128 * e + 64] + pltpu.roll(grad_down[128 * e + 64 : 128 * e + 128], 448, 1)
        for e in range(2)
    ]
    for ab in range(4):
        tile = jnp.concatenate([half[:, 128 * ab : 128 * ab + 128] for half in halves], axis=0)
        emit(14 + ab, tile.T[0:64])
    sums = small[...]
    head = sums[0:1] + pltpu.roll(sums, 64, 1)[0:1]
    total = jnp.sum(sums[1:2], axis=1, keepdims=True) * (1.0 / 64)
    row = merge_half(head, jnp.broadcast_to(total, (1, 128)))
    emit(18, jnp.broadcast_to(row, (64, 128)))
    for c in range(chans):
        place = lax.rem(c - chan + chans, chans)
        for ref, r in ((keep_ref, rep), (send_ref, 1 - rep)):
            rows = pl.ds(pl.multiple_of((c * reps + r) * share, share), share)
            ref[place] = whole[:, rows, :]


def final_kernel(foot_ref, mine_ref, peer_ref, second_ref, down_ref, head_ref, loss_ref):
    rep = lax.axis_index("rep")
    share = mine_ref.shape[1]
    for ref, r in ((mine_ref, rep), (peer_ref, 1 - rep)):
        rows = pl.ds(pl.multiple_of(r * share, share), share)
        for a in range(3):
            for e in range(3):
                m = 3 * a + e
                later, first = ref[m], ref[9 + m // 2]
                second_ref[9 * a + e, rows] = first[:, 64 * (m % 2) : 64 * (m % 2) + 64]
                second_ref[9 * a + 3 + e, rows] = later[:, 0:64]
                second_ref[9 * a + 6 + e, rows] = later[:, 64:128]
        for ab in range(4):
            for e in range(2):
                down_ref[2 * ab + e, rows] = ref[14 + ab][:, 64 * e : 64 * e + 64]
    line = mine_ref[18][0:1]
    head_ref[...] = line[:, 0:64]
    live = foot_ref[1, 0]
    for c in range(1, foot_ref.shape[1]):
        live += foot_ref[1, c]
    scale = jnp.full((1, 1), COARSE * live, jnp.int32).astype(F32)
    loss_ref[...] = line[:, 64:65] / scale


def sums_slab(shape):
    return lax.broadcasted_iota(jnp.int32, shape, 0) == 18


def to_wire(value):
    high = lax.reduce_precision(value, 8, 7)
    rest = lax.reduce_precision(value - high, 8, 7)
    lower = lax.broadcasted_iota(jnp.int32, value.shape, 1) >= value.shape[1] // 2
    return jnp.where(sums_slab(value.shape) & lower, rest, high)


def from_wire(value):
    half = value.shape[1] // 2
    other = jnp.concatenate([value[:, half:], value[:, :half]], axis=1)
    return value + jnp.where(sums_slab(value.shape), other, 0.0)


def shards(features, w_first, w_second, w_down, w_head, footprint, labels):
    bricks, chans, reps = lax.axis_size("bricks"), lax.axis_size("chan"), lax.axis_size("rep")
    planes = BRICK // chans
    side = lax.axis_index("chan") * planes // 4
    smem = pl.BlockSpec(memory_space=pltpu.SMEM)
    vmem = pl.BlockSpec(memory_space=pltpu.VMEM)
    features = features[0]
    slabs = features.shape[2] // 4

    packed = pl.pallas_call(
        pack_kernel,
        out_shape=jax.ShapeDtypeStruct((62, 32 // chans, 128), BF16),
        in_specs=[vmem] * 3,
        out_specs=vmem,
        compiler_params=pltpu.CompilerParams(vmem_limit_bytes=16 << 20),
        name="pack",
    )(w_first.transpose(0, 2, 1), w_second.transpose(0, 2, 1), w_down)
    pieces = [packed]
    for step in range(1, chans):
        ring = [(i, (i + step) % chans) for i in range(chans)]
        pieces.append(lax.ppermute(packed, "chan", ring))

    pairs = []
    for col in range(bricks * reps):
        for c in range(chans):
            src = col + 2 * (c * planes // 4) - 1
            if 0 <= src < bricks * reps:
                ends = [(j // reps * chans + c) * reps + j % reps for j in (src, col)]
                pairs.append(tuple(ends))
    outward = lax.dynamic_slice_in_dim(features, (1 - side) * 4, 4, 1).transpose(1, 2, 0, 3)
    halo = lax.ppermute(outward, ("bricks", "chan", "rep"), pairs)

    edge, near, mat1, mat2, down_mat, back_mat = pl.pallas_call(
        local_kernel,
        out_shape=(
            jax.ShapeDtypeStruct((4, slabs, ROWS, 128), BF16),
            jax.ShapeDtypeStruct((4, slabs, ROWS, 128), BF16),
            jax.ShapeDtypeStruct((3, 1024, 256), BF16),
            jax.ShapeDtypeStruct((3, 1024, 256), BF16),
            jax.ShapeDtypeStruct((512, 256), BF16),
            jax.ShapeDtypeStruct((128, 1024), BF16),
        ),
        in_specs=[smem] + [vmem] * (1 + chans),
        out_specs=(vmem,) * 6,
        scratch_shapes=[
            pltpu.VMEM((62, 64, 128), BF16),
            pltpu.VMEM((54, 64, 128), BF16),
            pltpu.VMEM((8, slabs, ROWS, 128), BF16),
            pltpu.VMEM((8, ROWS, 256), BF16),
            pltpu.VMEM((8, ROWS, 256), BF16),
        ],
        compiler_params=pltpu.CompilerParams(vmem_limit_bytes=36 << 20),
        cost_estimate=pl.CostEstimate(flops=6 * 6 * 512 * 1024 * 512, bytes_accessed=8 << 20, transcendentals=0),
        name="first_local",
    )(footprint, features.transpose(1, 2, 0, 3), *pieces)
    parts = jax.ShapeDtypeStruct((chans, 19, 64 // chans // reps, 128), F32)
    keep, send = pl.pallas_call(
        main_kernel,
        out_shape=(parts, parts),
        in_specs=[smem] + [vmem] * 9,
        out_specs=(vmem, vmem),
        scratch_shapes=[
            pltpu.VMEM((4, slabs, ROWS, 128), BF16),
            pltpu.VMEM((8, ROWS, 256), BF16),
            pltpu.VMEM((8, ROWS, 256), BF16),
            pltpu.VMEM((slabs + 2, 8, ROWS, 128), BF16),
            pltpu.VMEM((2, 8, ROWS, 256), BF16),
            pltpu.VMEM((384, 128), BF16),
            pltpu.VMEM((2, 2, 2, ROWS, 128), BF16),
            pltpu.VMEM((256, 512), BF16),
            pltpu.VMEM((384, 2048), BF16),
            pltpu.VMEM((3, 384, 256), F32),
            pltpu.VMEM((256, 512), F32),
            pltpu.VMEM((8, 128), F32),
            pltpu.VMEM((19, 64, 128), F32),
        ],
        compiler_params=pltpu.CompilerParams(vmem_limit_bytes=40 << 20),
        cost_estimate=pl.CostEstimate(flops=4 * 6 * 6 * 512 * 1024 * 512, bytes_accessed=16 << 20, transcendentals=0),
        name="head_and_grads",
    )(footprint, edge, halo, near, mat1, mat2, down_mat, back_mat, w_head.reshape(1, 64), labels[0])

    swap = [(i, 1 - i) for i in range(reps)]
    got = lax.ppermute(send, "rep", swap)
    wire = [to_wire(keep[step] + got[step]) for step in range(chans)]
    near_sums = []
    for flip in range(2):
        for step in range(chans):
            if flip == step == 0:
                near_sums.append(wire[0])
                continue
            routes = [
                (b * chans + c, (b ^ flip) * chans + (c + step) % chans)
                for b in range(bricks)
                for c in range(chans)
            ]
            sent = lax.ppermute(wire[step].astype(BF16), ("bricks", "chan"), routes)
            near_sums.append(sent.astype(F32))
    mine = from_wire(sum(near_sums[1:chans], near_sums[0]) + sum(near_sums[chans + 1 :], near_sums[chans]))
    step = 2
    while step < bricks:
        wire = to_wire(mine)
        sent = lax.ppermute(wire.astype(BF16), "bricks", [(i, i ^ step) for i in range(bricks)])
        mine = from_wire(wire + sent.astype(F32))
        step *= 2
    peer = lax.ppermute(mine, "rep", swap)
    share = 64 // chans
    second, down, head, loss = pl.pallas_call(
        final_kernel,
        out_shape=(
            jax.ShapeDtypeStruct((27, share, 64), F32),
            jax.ShapeDtypeStruct((8, share, 64), F32),
            jax.ShapeDtypeStruct((1, 64), F32),
            jax.ShapeDtypeStruct((1, 1), F32),
        ),
        in_specs=[smem, vmem, vmem],
        out_specs=(vmem,) * 4,
        compiler_params=pltpu.CompilerParams(vmem_limit_bytes=16 << 20),
        name="assemble",
    )(footprint, mine, peer)
    return second.transpose(0, 2, 1), down, head.reshape(64), loss.reshape(1)


def solution(mesh):
    return jax.shard_map(
        shards,
        mesh=mesh,
        in_specs=(
            P(("groups", "bricks", "rep"), None, None, None, None),
            P(None, None, "chan"),
            P(None, None, "chan"),
            P(None, "chan", None),
            P(),
            P(None, "groups"),
            P(("groups", "bricks", "rep"), None, None),
        ),
        out_specs=(P("groups", None, "chan"), P("groups", "chan", None), P("groups"), P("groups")),
        check_vma=False,
    )
```

```python
import jax
import jax.numpy as jnp
from jax import lax
from jax.experimental import pallas as pl
from jax.experimental.pallas import tpu as pltpu
from jax.sharding import PartitionSpec as P

BRICK = 8
COARSE = 1024
ROWS = 256
F32 = jnp.float32
BF16 = jnp.bfloat16


def lanes_low(shape):
    return lax.broadcasted_iota(jnp.int32, shape, len(shape) - 1) % 128 < 64


def merge_half(low, high):
    return jnp.where(lanes_low(low.shape), low, high)


def shifted(value, by):
    row = lax.broadcasted_iota(jnp.int32, value.shape, 0) % 128
    inside = row >= by if by > 0 else row < 128 + by
    return jnp.where(inside, pltpu.roll(value, by % value.shape[0], 0), 0.0)


def build_conv(w_ref, out_ref):
    zero = jnp.zeros((64, 128), BF16)
    for e in range(3):
        for k in range(4):
            for slot, d in enumerate((0, 1, 2, -1)):
                for rx in range(2):
                    a = k - rx
                    halves = []
                    for ry in range(2):
                        b = d - ry + 1
                        live = 0 <= a < 3 and 0 <= b < 3
                        halves.append(w_ref[9 * a + 3 * b + e] if live else zero)
                    row = k * 256 + slot * 64
                    out_ref[e, row : row + 64, rx * 128 : rx * 128 + 128] = merge_half(*halves)


def plane_pairs(window_ref, first, pairs, slot=()):
    blocks = [window_ref[(*slot, pl.ds(first + 2 * k, 2))].reshape(2 * ROWS, 256) for k in range(pairs)]
    return jnp.concatenate(blocks, axis=1)


def conv_rows(lhs, mats):
    below, level, above = [jnp.dot(lhs, mat, preferred_element_type=F32) for mat in mats]
    return level + shifted(below, 2) + shifted(above, -2)


def half_mats(mat_ref, half):
    rows = pl.ds(pl.multiple_of(512 * half, 512), 512)
    return [mat_ref[e, rows, :] for e in range(3)]


def neighbour(foot_ref, column, columns, side):
    other = column + 2 * side - 1
    present = (other >= 0) & (other < columns)
    other = jnp.clip(other, 0, columns - 1)
    count = jnp.where(present, 2 * foot_ref[1, other], 0)
    return count, 2 * (foot_ref[0, other] - foot_ref[0, column])


def rims(count, offset, other_count, work):
    def rim(i, carry):
        t = jnp.where(i == 0, -1, count)

        @pl.when((t - offset >= 0) & (t - offset < other_count))
        def _():
            work(t)

        return carry

    lax.fori_loop(0, 2, rim, 0)


def gated(ref, plane, index, count):
    inside = (index >= 0) & (index < count)
    block = ref[plane, jnp.clip(index, 0, ref.shape[1] - 1)]
    return jnp.where(inside, block, jnp.zeros_like(block))


def turn_block(src_ref, dst_ref, plane, t):
    for py in range(2):
        tall = jnp.concatenate([src_ref[plane, 4 * t + py], src_ref[plane, 4 * t + 2 + py]], axis=0)
        dst_ref[plane, t, 128 * py : 128 * py + 128] = tall.T


def fill_window(window_ref, plane, src_ref, src_plane, index, count):
    window_ref[plane, :, 0:128] = gated(src_ref, src_plane, index, count)
    window_ref[plane, :, 128:256] = merge_half(
        gated(src_ref, src_plane, index + 1, count), gated(src_ref, src_plane, index - 1, count)
    )


def pack_kernel(w1_ref, w2_ref, wd_ref, out_ref):
    half = w1_ref.shape[1] // 2
    start = 0
    for ref in (w1_ref, w2_ref, wd_ref):
        stop = start + ref.shape[0]
        out_ref[start:stop] = jnp.concatenate([ref[:, :half], ref[:, half:]], axis=2)
        start = stop


def local_kernel(foot_ref, feat_ref, *refs):
    chans = lax.axis_size("chan")
    piece_refs = refs[:chans]
    part_ref, y1_ref, m1_ref, m2_ref, down_ref, back_ref, whole, turned, arranged = refs[chans:-2]
    even_window, odd_window = refs[-2:]
    column = lax.axis_index("bricks") * lax.axis_size("rep") + lax.axis_index("rep")
    me = lax.axis_index("chan")
    side = me * (BRICK // chans) // 4
    count = 2 * foot_ref[1, column]
    columns = lax.axis_size("bricks") * lax.axis_size("rep")
    other_count, offset = neighbour(foot_ref, column, columns, side)

    half = piece_refs[0].shape[1]
    for step in range(chans):
        block = piece_refs[step][...]
        source = lax.rem(me - step + chans, chans)
        for h in range(2):
            part = block[:, :, 64 * h : 64 * h + 64]
            rows = pl.ds(pl.multiple_of((2 * source + h) * half, half), half)
            whole[:, rows, :] = jnp.concatenate([part, part], axis=2)
    for t in range(54):
        turned[t] = jnp.concatenate([whole[t], whole[t]], axis=0).T[0:64]
    build_conv(turned.at[0:27], m1_ref)
    build_conv(turned.at[27:54], m2_ref)
    low = lanes_low((64, 128))
    zero = jnp.zeros((64, 128), BF16)
    for t in range(8):
        ab, e = t // 2, t % 2
        block = whole[54 + t]
        tile = jnp.concatenate([jnp.where(low, block, zero), jnp.where(low, zero, block)], axis=0)
        down_ref[ab * 128 : ab * 128 + 128, e * 128 : e * 128 + 128] = tile
        back_ref[:, t * 128 : t * 128 + 128] = tile.T

    def turn(t, carry):
        for p in range(8):
            turn_block(feat_ref, arranged, p, t)
        return carry

    lax.fori_loop(0, count, turn, 0)

    def fill(window, t):
        for p in range(8):
            fill_window(window, p, arranged, p, t, count)

    def edge(window, t):
        lhs = plane_pairs(window, 4 * side, 2)
        part_ref[t + 1] = conv_rows(lhs, half_mats(m1_ref, 1 - side))

    def conv(window, t):
        edge(window, t)
        lhs = plane_pairs(window, 0, 4)
        out = jnp.maximum(conv_rows(lhs, [m1_ref[e] for e in range(3)]), 0.0).astype(BF16)
        for par in range(2):
            for rx in range(2):
                y1_ref[2 * rx + par, t] = out[ROWS * par : ROWS * par + ROWS, 128 * rx : 128 * rx + 128]

    def pair(j, carry):
        fill(odd_window, 2 * j + 1)
        conv(even_window, 2 * j)
        fill(even_window, 2 * j + 2)
        conv(odd_window, 2 * j + 1)
        return carry

    def beside(t):
        fill(even_window, t)
        edge(even_window, t)

    rims(count, offset, other_count, beside)
    fill(even_window, 0)
    lax.fori_loop(0, count // 2, pair, 0)


def main_kernel(
    foot_ref,
    part_ref,
    halo_ref,
    near_ref,
    m1_ref,
    m2_ref,
    down_mat,
    back_mat,
    head_ref,
    label_ref,
    keep_ref,
    send_ref,
    arranged,
    even_window,
    odd_window,
    hidden,
    hwin,
    headm_ref,
    y2_ref,
    delta_t,
    err_t,
    grad,
    grad_down,
    small,
    whole,
):
    reps, chans = lax.axis_size("rep"), lax.axis_size("chan")
    columns = lax.axis_size("bricks") * reps
    column = lax.axis_index("bricks") * reps + lax.axis_index("rep")
    planes = BRICK // chans
    mine = lax.axis_index("chan") * planes
    side = mine // 4
    count = 2 * foot_ref[1, column]
    other_count, offset = neighbour(foot_ref, column, columns, side)

    grad[...] = jnp.zeros_like(grad)
    grad_down[...] = jnp.zeros_like(grad_down)
    small[...] = jnp.zeros_like(small)
    head_row = jnp.concatenate([head_ref[...], head_ref[...]], axis=1)
    square_row = lax.broadcasted_iota(jnp.int32, (128, 128), 0)
    square_lane = lax.broadcasted_iota(jnp.int32, (128, 128), 1)
    same_half = (square_row < 64) == (square_lane < 64)
    head_mat = jnp.where(same_half, jnp.broadcast_to(head_row, (128, 128)).T, 0.0)
    head_high = head_mat.astype(BF16)
    headm_ref[0:128] = head_high
    headm_ref[128:256] = head_high
    headm_ref[256:384] = (head_mat - head_high.astype(F32)).astype(BF16)
    pick_depth = jnp.where(square_row // 2 == square_lane % 64, 1.0, 0.0).astype(BF16)

    def turn(t, carry):
        for p in range(4):
            turn_block(halo_ref, arranged, p, t)
        return carry

    lax.fori_loop(0, other_count, turn, 0)

    def fill(window, t):
        for p in range(4):
            fill_window(window, p, arranged, p, t - offset, other_count)

    def first(window, t):
        own = (t >= 0) & (t < count)
        next_to = (t - offset >= 0) & (t - offset < other_count)
        out = part_ref[t + 1] + conv_rows(plane_pairs(window, 0, 2), half_mats(m1_ref, side))
        out = jnp.maximum(out, 0.0).astype(BF16)
        for rx in range(2):
            live = jnp.where(side == rx, next_to, own)
            for par in range(2):
                block = out[ROWS * par : ROWS * par + ROWS, 128 * rx : 128 * rx + 128]
                hidden[t + 1, side * 4 + 2 * rx + par] = jnp.where(live, block, jnp.zeros_like(block))

    def near(t):
        for p in range(4):
            hidden[t + 1, (1 - side) * 4 + p] = gated(near_ref, p, t, count)

    def beside(t):
        fill(even_window, t)
        first(even_window, t)

    def pair(j, carry):
        fill(odd_window, 2 * j + 1)
        near(2 * j)
        first(even_window, 2 * j)
        fill(even_window, 2 * j + 2)
        near(2 * j + 1)
        first(odd_window, 2 * j + 1)
        return carry

    hidden[0] = jnp.zeros((8, ROWS, 128), BF16)
    hidden[count + 1] = jnp.zeros((8, ROWS, 128), BF16)
    rims(count, offset, other_count, beside)
    fill(even_window, 0)
    lax.fori_loop(0, count // 2, pair, 0)

    row4 = lax.broadcasted_iota(jnp.int32, (512, 128), 0)
    even4 = row4 % 2 == 0
    plane4 = 4 * side + 2 * (row4 // 128 % 2)
    keep = even4 & (plane4 >= mine) & (plane4 < mine + planes)

    def second(j, carry):
        for u in range(2):
            t = 2 * j + u
            for p in range(8):
                hwin[u, p, :, 0:128] = hidden[t + 1, p]
                hwin[u, p, :, 128:256] = merge_half(hidden[t + 2, p], hidden[t, p])
            out = conv_rows(plane_pairs(hwin, 0, 4, (u,)), [m2_ref[e] for e in range(3)])
            out = jnp.maximum(out, 0.0).astype(BF16)
            for par in range(2):
                for rx in range(2):
                    y2_ref[u, rx, par] = out[ROWS * par : ROWS * par + ROWS, 128 * rx : 128 * rx + 128]
        fine = jnp.concatenate(
            [
                jnp.concatenate(
                    [y2_ref[u, rx, a, 128 * b : 128 * b + 128] for u in range(2) for rx in range(2)],
                    axis=0,
                )
                for a in range(2)
                for b in range(2)
            ],
            axis=1,
        )
        both = jnp.dot(fine, down_mat[...], preferred_element_type=F32)
        coarse = both[:, 0:128] + shifted(both[:, 128:256], -1)
        rect = jnp.maximum(coarse, 0.0)
        high = rect.astype(BF16)
        rest = (rect - high.astype(F32)).astype(BF16)
        logit = jnp.dot(
            jnp.concatenate([high, rest, high], axis=1), headm_ref[...], preferred_element_type=F32
        )
        labels = []
        for u in range(2):
            line = label_ref[:, pl.ds(pl.multiple_of(256 * j + 128 * u, 128), 128)].astype(F32)
            for rx in range(2):
                row = jnp.where(side == 1, line[2 + rx : 3 + rx], line[rx : rx + 1])
                row = jnp.where(same_half, jnp.broadcast_to(row, (128, 128)), 0.0).astype(BF16)
                labels.append(
                    lax.dot_general(
                        pick_depth, row, (((1,), (1,)), ((), ())), preferred_element_type=F32
                    )
                )
        label = jnp.concatenate(labels, axis=0)
        tail = jnp.exp(-jnp.abs(logit))
        soft = jnp.maximum(logit, 0.0) + jnp.log1p(tail)
        sigmoid = jnp.where(logit >= 0.0, 1.0, tail) / (1.0 + tail)
        loss = jnp.where(keep, soft - label * logit, 0.0)
        slope = jnp.where(keep, (sigmoid - label) * (1.0 / COARSE), 0.0)
        small[0:1] += jnp.sum(slope * rect, axis=0, keepdims=True)
        small[1:2] += jnp.sum(loss, axis=0, keepdims=True)
        delta = jnp.where(coarse > 0.0, slope * head_row, 0.0).astype(BF16).astype(F32)
        moved = shifted(delta, 1)
        delta_t[0:128] = delta.astype(BF16).T
        delta_t[128:256] = moved.astype(BF16).T
        back = jnp.dot((delta + moved).astype(BF16), back_mat[...], preferred_element_type=F32)
        for a in range(2):
            for b in range(2):
                lane = (2 * a + b) * 256
                err = jnp.where(even4, back[:, lane : lane + 128], back[:, lane + 128 : lane + 256])
                live = fine[:, lane // 2 : lane // 2 + 128].astype(F32) > 0.0
                err = jnp.where(live, err, 0.0)
                for n in range(4):
                    turned = err[128 * n : 128 * n + 128].astype(BF16).T
                    col = n * 512 + a * 256 + b * 128
                    err_t[128:256, col : col + 128] = turned
                    up = jnp.where(square_lane < 126, pltpu.roll(turned, 126, 1), jnp.zeros_like(turned))
                    down = jnp.where(square_lane >= 2, pltpu.roll(turned, 2, 1), jnp.zeros_like(turned))
                    err_t[0:128, col : col + 128] = up
                    err_t[256:384, col : col + 128] = down
        grad_down[...] += jnp.dot(delta_t[...], fine, preferred_element_type=F32)
        for a in range(3):
            rows = hwin[:, 2 * a : 2 * a + 4].reshape(8 * ROWS, 256)
            grad[a] += jnp.dot(err_t[...], rows, preferred_element_type=F32)
        return carry

    lax.fori_loop(0, count // 2, second, 0)

    low = lanes_low((64, 128))
    rep, chan = lax.axis_index("rep"), lax.axis_index("chan")
    share = 64 // chans // reps

    def emit(slab, value):
        whole[slab] = value

    firsts = []
    for a in range(3):
        for e in range(3):
            both = grad[a, 128 * e : 128 * e + 64] + pltpu.roll(
                grad[a, 128 * e + 64 : 128 * e + 128], 192, 1
            )
            emit(3 * a + e, both[:, 0:128])
            firsts.append(both[:, 128:256])
    for m in range(5):
        right = firsts[2 * m + 1] if 2 * m + 1 < 9 else jnp.zeros_like(firsts[0])
        emit(9 + m, jnp.where(low, pltpu.roll(firsts[2 * m], 64, 1), right))
    halves = [
        grad_down[128 * e : 128 * e + 64] + pltpu.roll(grad_down[128 * e + 64 : 128 * e + 128], 448, 1)
        for e in range(2)
    ]
    for ab in range(4):
        tile = jnp.concatenate([half[:, 128 * ab : 128 * ab + 128] for half in halves], axis=0)
        emit(14 + ab, tile.T[0:64])
    sums = small[...]
    head = sums[0:1] + pltpu.roll(sums, 64, 1)[0:1]
    total = jnp.sum(sums[1:2], axis=1, keepdims=True) * (1.0 / 64)
    row = merge_half(head, jnp.broadcast_to(total, (1, 128)))
    emit(18, jnp.broadcast_to(row, (64, 128)))
    for c in range(chans):
        place = lax.rem(c - chan + chans, chans)
        for ref, r in ((keep_ref, rep), (send_ref, 1 - rep)):
            rows = pl.ds(pl.multiple_of((c * reps + r) * share, share), share)
            ref[place] = whole[:, rows, :]


def final_kernel(foot_ref, mine_ref, peer_ref, second_ref, down_ref, head_ref, loss_ref):
    rep = lax.axis_index("rep")
    share = mine_ref.shape[1]
    for ref, r in ((mine_ref, rep), (peer_ref, 1 - rep)):
        rows = pl.ds(pl.multiple_of(r * share, share), share)
        for a in range(3):
            for e in range(3):
                m = 3 * a + e
                later, first = ref[m], ref[9 + m // 2]
                second_ref[9 * a + e, rows] = first[:, 64 * (m % 2) : 64 * (m % 2) + 64]
                second_ref[9 * a + 3 + e, rows] = later[:, 0:64]
                second_ref[9 * a + 6 + e, rows] = later[:, 64:128]
        for ab in range(4):
            for e in range(2):
                down_ref[2 * ab + e, rows] = ref[14 + ab][:, 64 * e : 64 * e + 64]
    line = mine_ref[18][0:1]
    head_ref[...] = line[:, 0:64]
    live = foot_ref[1, 0]
    for c in range(1, foot_ref.shape[1]):
        live += foot_ref[1, c]
    scale = jnp.full((1, 1), COARSE * live, jnp.int32).astype(F32)
    loss_ref[...] = line[:, 64:65] / scale


def sums_slab(shape):
    return lax.broadcasted_iota(jnp.int32, shape, 0) == 18


def to_wire(value):
    high = lax.reduce_precision(value, 8, 7)
    rest = lax.reduce_precision(value - high, 8, 7)
    lower = lax.broadcasted_iota(jnp.int32, value.shape, 1) >= value.shape[1] // 2
    return jnp.where(sums_slab(value.shape) & lower, rest, high)


def from_wire(value):
    half = value.shape[1] // 2
    other = jnp.concatenate([value[:, half:], value[:, :half]], axis=1)
    return value + jnp.where(sums_slab(value.shape), other, 0.0)


def shards(features, w_first, w_second, w_down, w_head, footprint, labels):
    bricks, chans, reps = lax.axis_size("bricks"), lax.axis_size("chan"), lax.axis_size("rep")
    planes = BRICK // chans
    side = lax.axis_index("chan") * planes // 4
    smem = pl.BlockSpec(memory_space=pltpu.SMEM)
    vmem = pl.BlockSpec(memory_space=pltpu.VMEM)
    features = features[0]
    slabs = features.shape[2] // 4

    packed = pl.pallas_call(
        pack_kernel,
        out_shape=jax.ShapeDtypeStruct((62, 32 // chans, 128), BF16),
        in_specs=[vmem] * 3,
        out_specs=vmem,
        compiler_params=pltpu.CompilerParams(vmem_limit_bytes=16 << 20),
        name="pack",
    )(w_first.transpose(0, 2, 1), w_second.transpose(0, 2, 1), w_down)
    pieces = [packed]
    for step in range(1, chans):
        ring = [(i, (i + step) % chans) for i in range(chans)]
        pieces.append(lax.ppermute(packed, "chan", ring))

    pairs = []
    for col in range(bricks * reps):
        for c in range(chans):
            src = col + 2 * (c * planes // 4) - 1
            if 0 <= src < bricks * reps:
                ends = [(j // reps * chans + c) * reps + j % reps for j in (src, col)]
                pairs.append(tuple(ends))
    outward = lax.dynamic_slice_in_dim(features, (1 - side) * 4, 4, 1).transpose(1, 2, 0, 3)
    halo = lax.ppermute(outward, ("bricks", "chan", "rep"), pairs)

    part, near, mat1, mat2, down_mat, back_mat = pl.pallas_call(
        local_kernel,
        out_shape=(
            jax.ShapeDtypeStruct((slabs + 2, 2 * ROWS, 256), F32),
            jax.ShapeDtypeStruct((4, slabs, ROWS, 128), BF16),
            jax.ShapeDtypeStruct((3, 1024, 256), BF16),
            jax.ShapeDtypeStruct((3, 1024, 256), BF16),
            jax.ShapeDtypeStruct((512, 256), BF16),
            jax.ShapeDtypeStruct((128, 1024), BF16),
        ),
        in_specs=[smem] + [vmem] * (1 + chans),
        out_specs=(vmem,) * 6,
        scratch_shapes=[
            pltpu.VMEM((62, 64, 128), BF16),
            pltpu.VMEM((54, 64, 128), BF16),
            pltpu.VMEM((8, slabs, ROWS, 128), BF16),
            pltpu.VMEM((8, ROWS, 256), BF16),
            pltpu.VMEM((8, ROWS, 256), BF16),
        ],
        compiler_params=pltpu.CompilerParams(vmem_limit_bytes=36 << 20),
        cost_estimate=pl.CostEstimate(flops=6 * 6 * 512 * 1024 * 512, bytes_accessed=8 << 20, transcendentals=0),
        name="first_local",
    )(footprint, features.transpose(1, 2, 0, 3), *pieces)
    parts = jax.ShapeDtypeStruct((chans, 19, 64 // chans // reps, 128), F32)
    keep, send = pl.pallas_call(
        main_kernel,
        out_shape=(parts, parts),
        in_specs=[smem] + [vmem] * 9,
        out_specs=(vmem, vmem),
        scratch_shapes=[
            pltpu.VMEM((4, slabs, ROWS, 128), BF16),
            pltpu.VMEM((4, ROWS, 256), BF16),
            pltpu.VMEM((4, ROWS, 256), BF16),
            pltpu.VMEM((slabs + 2, 8, ROWS, 128), BF16),
            pltpu.VMEM((2, 8, ROWS, 256), BF16),
            pltpu.VMEM((384, 128), BF16),
            pltpu.VMEM((2, 2, 2, ROWS, 128), BF16),
            pltpu.VMEM((256, 512), BF16),
            pltpu.VMEM((384, 2048), BF16),
            pltpu.VMEM((3, 384, 256), F32),
            pltpu.VMEM((256, 512), F32),
            pltpu.VMEM((8, 128), F32),
            pltpu.VMEM((19, 64, 128), F32),
        ],
        compiler_params=pltpu.CompilerParams(vmem_limit_bytes=40 << 20),
        cost_estimate=pl.CostEstimate(flops=4 * 6 * 6 * 512 * 1024 * 512, bytes_accessed=16 << 20, transcendentals=0),
        name="head_and_grads",
    )(footprint, part, halo, near, mat1, mat2, down_mat, back_mat, w_head.reshape(1, 64), labels[0])

    swap = [(i, 1 - i) for i in range(reps)]
    got = lax.ppermute(send, "rep", swap)
    wire = [to_wire(keep[step] + got[step]) for step in range(chans)]
    near_sums = []
    for flip in range(2):
        for step in range(chans):
            if flip == step == 0:
                near_sums.append(wire[0])
                continue
            routes = [
                (b * chans + c, (b ^ flip) * chans + (c + step) % chans)
                for b in range(bricks)
                for c in range(chans)
            ]
            sent = lax.ppermute(wire[step].astype(BF16), ("bricks", "chan"), routes)
            near_sums.append(sent.astype(F32))
    mine = from_wire(sum(near_sums[1:chans], near_sums[0]) + sum(near_sums[chans + 1 :], near_sums[chans]))
    step = 2
    while step < bricks:
        wire = to_wire(mine)
        sent = lax.ppermute(wire.astype(BF16), "bricks", [(i, i ^ step) for i in range(bricks)])
        mine = from_wire(wire + sent.astype(F32))
        step *= 2
    peer = lax.ppermute(mine, "rep", swap)
    share = 64 // chans
    second, down, head, loss = pl.pallas_call(
        final_kernel,
        out_shape=(
            jax.ShapeDtypeStruct((27, share, 64), F32),
            jax.ShapeDtypeStruct((8, share, 64), F32),
            jax.ShapeDtypeStruct((1, 64), F32),
            jax.ShapeDtypeStruct((1, 1), F32),
        ),
        in_specs=[smem, vmem, vmem],
        out_specs=(vmem,) * 4,
        compiler_params=pltpu.CompilerParams(vmem_limit_bytes=16 << 20),
        name="assemble",
    )(footprint, mine, peer)
    return second.transpose(0, 2, 1), down, head.reshape(64), loss.reshape(1)


def solution(mesh):
    return jax.shard_map(
        shards,
        mesh=mesh,
        in_specs=(
            P(("groups", "bricks", "rep"), None, None, None, None),
            P(None, None, "chan"),
            P(None, None, "chan"),
            P(None, "chan", None),
            P(),
            P(None, "groups"),
            P(("groups", "bricks", "rep"), None, None),
        ),
        out_specs=(P("groups", None, "chan"), P("groups", "chan", None), P("groups"), P("groups")),
        check_vma=False,
    )
```

```python
import jax
import jax.numpy as jnp
from jax import lax
from jax.experimental import pallas as pl
from jax.experimental.pallas import tpu as pltpu
from jax.sharding import PartitionSpec as P

BRICK = 8
COARSE = 1024
ROWS = 256
F32 = jnp.float32
BF16 = jnp.bfloat16


def lanes_low(shape):
    return lax.broadcasted_iota(jnp.int32, shape, len(shape) - 1) % 128 < 64


def merge_half(low, high):
    return jnp.where(lanes_low(low.shape), low, high)


def shifted(value, by):
    row = lax.broadcasted_iota(jnp.int32, value.shape, 0) % 128
    inside = row >= by if by > 0 else row < 128 + by
    return jnp.where(inside, pltpu.roll(value, by % value.shape[0], 0), 0.0)


def build_conv(w_ref, out_ref):
    zero = jnp.zeros((64, 128), BF16)
    for e in range(3):
        for k in range(4):
            for slot, d in enumerate((0, 1, 2, -1)):
                for rx in range(2):
                    a = k - rx
                    halves = []
                    for ry in range(2):
                        b = d - ry + 1
                        live = 0 <= a < 3 and 0 <= b < 3
                        halves.append(w_ref[9 * a + 3 * b + e] if live else zero)
                    row = k * 256 + slot * 64
                    out_ref[e, row : row + 64, rx * 128 : rx * 128 + 128] = merge_half(*halves)


def plane_pairs(window_ref, first, pairs, slot=()):
    blocks = [window_ref[(*slot, pl.ds(first + 2 * k, 2))].reshape(2 * ROWS, 256) for k in range(pairs)]
    return jnp.concatenate(blocks, axis=1)


def conv_rows(lhs, mats):
    below, level, above = [jnp.dot(lhs, mat, preferred_element_type=F32) for mat in mats]
    return level + shifted(below, 2) + shifted(above, -2)


def half_mats(mat_ref, half):
    rows = pl.ds(pl.multiple_of(512 * half, 512), 512)
    return [mat_ref[e, rows, :] for e in range(3)]


def neighbour(foot_ref, column, columns, side):
    other = column + 2 * side - 1
    present = (other >= 0) & (other < columns)
    other = jnp.clip(other, 0, columns - 1)
    count = jnp.where(present, 2 * foot_ref[1, other], 0)
    return count, 2 * (foot_ref[0, other] - foot_ref[0, column])


def rims(count, offset, other_count, work):
    def rim(i, carry):
        t = jnp.where(i == 0, -1, count)

        @pl.when((t - offset >= 0) & (t - offset < other_count))
        def _():
            work(t)

        return carry

    lax.fori_loop(0, 2, rim, 0)


def gated(ref, plane, index, count):
    inside = (index >= 0) & (index < count)
    block = ref[plane, jnp.clip(index, 0, ref.shape[1] - 1)]
    return jnp.where(inside, block, jnp.zeros_like(block))


def turn_block(src_ref, dst_ref, plane, t):
    for py in range(2):
        tall = jnp.concatenate([src_ref[plane, 4 * t + py], src_ref[plane, 4 * t + 2 + py]], axis=0)
        dst_ref[plane, t, 128 * py : 128 * py + 128] = tall.T


def fill_window(window_ref, plane, src_ref, src_plane, index, count):
    window_ref[plane, :, 0:128] = gated(src_ref, src_plane, index, count)
    window_ref[plane, :, 128:256] = merge_half(
        gated(src_ref, src_plane, index + 1, count), gated(src_ref, src_plane, index - 1, count)
    )


def pack_kernel(w1_ref, w2_ref, wd_ref, first_ref, rest_ref):
    half = w1_ref.shape[1] // 2

    def dense(ref):
        return jnp.concatenate([ref[:, :half], ref[:, half:]], axis=2)

    first_ref[...] = dense(w1_ref)
    rest_ref[0 : w2_ref.shape[0]] = dense(w2_ref)
    rest_ref[w2_ref.shape[0] :] = dense(wd_ref)


def unpack(piece_refs, whole):
    chans = lax.axis_size("chan")
    me = lax.axis_index("chan")
    half = piece_refs[0].shape[1]
    for step in range(chans):
        block = piece_refs[step][...]
        source = lax.rem(me - step + chans, chans)
        for h in range(2):
            part = block[:, :, 64 * h : 64 * h + 64]
            rows = pl.ds(pl.multiple_of((2 * source + h) * half, half), half)
            whole[:, rows, :] = jnp.concatenate([part, part], axis=2)


def turn_taps(whole, turned):
    for t in range(27):
        turned[t] = jnp.concatenate([whole[t], whole[t]], axis=0).T[0:64]


def mats_kernel(after_ref, *refs):
    chans = lax.axis_size("chan")
    m2_ref, down_ref, back_ref, whole, turned = refs[chans:]
    unpack(refs[:chans], whole)
    turn_taps(whole, turned)
    build_conv(turned, m2_ref)
    low = lanes_low((64, 128))
    zero = jnp.zeros((64, 128), BF16)
    for t in range(8):
        ab, e = t // 2, t % 2
        block = whole[27 + t]
        tile = jnp.concatenate([jnp.where(low, block, zero), jnp.where(low, zero, block)], axis=0)
        down_ref[ab * 128 : ab * 128 + 128, e * 128 : e * 128 + 128] = tile
        back_ref[:, t * 128 : t * 128 + 128] = tile.T


def local_kernel(foot_ref, feat_ref, *refs):
    chans = lax.axis_size("chan")
    part_ref, y1_ref, m1_ref, whole, turned, arranged, even_window, odd_window = refs[chans:]
    column = lax.axis_index("bricks") * lax.axis_size("rep") + lax.axis_index("rep")
    side = lax.axis_index("chan") * (BRICK // chans) // 4
    count = 2 * foot_ref[1, column]
    columns = lax.axis_size("bricks") * lax.axis_size("rep")
    other_count, offset = neighbour(foot_ref, column, columns, side)

    unpack(refs[:chans], whole)
    turn_taps(whole, turned)
    build_conv(turned, m1_ref)

    def turn(t, carry):
        for p in range(8):
            turn_block(feat_ref, arranged, p, t)
        return carry

    lax.fori_loop(0, count, turn, 0)

    def fill(window, t):
        for p in range(8):
            fill_window(window, p, arranged, p, t, count)

    def edge(window, t):
        lhs = plane_pairs(window, 4 * side, 2)
        part_ref[t + 1] = conv_rows(lhs, half_mats(m1_ref, 1 - side))

    def conv(window, t):
        edge(window, t)
        lhs = plane_pairs(window, 0, 4)
        out = jnp.maximum(conv_rows(lhs, [m1_ref[e] for e in range(3)]), 0.0).astype(BF16)
        for par in range(2):
            for rx in range(2):
                y1_ref[2 * rx + par, t] = out[ROWS * par : ROWS * par + ROWS, 128 * rx : 128 * rx + 128]

    def pair(j, carry):
        fill(odd_window, 2 * j + 1)
        conv(even_window, 2 * j)
        fill(even_window, 2 * j + 2)
        conv(odd_window, 2 * j + 1)
        return carry

    def beside(t):
        fill(even_window, t)
        edge(even_window, t)

    rims(count, offset, other_count, beside)
    fill(even_window, 0)
    lax.fori_loop(0, count // 2, pair, 0)


def main_kernel(
    foot_ref,
    part_ref,
    halo_ref,
    near_ref,
    m1_ref,
    m2_ref,
    down_mat,
    back_mat,
    head_ref,
    label_ref,
    keep_ref,
    send_ref,
    arranged,
    even_window,
    odd_window,
    hidden,
    hwin,
    headm_ref,
    y2_ref,
    delta_t,
    err_t,
    grad,
    grad_down,
    small,
    whole,
):
    reps, chans = lax.axis_size("rep"), lax.axis_size("chan")
    columns = lax.axis_size("bricks") * reps
    column = lax.axis_index("bricks") * reps + lax.axis_index("rep")
    planes = BRICK // chans
    mine = lax.axis_index("chan") * planes
    side = mine // 4
    count = 2 * foot_ref[1, column]
    other_count, offset = neighbour(foot_ref, column, columns, side)

    grad[...] = jnp.zeros_like(grad)
    grad_down[...] = jnp.zeros_like(grad_down)
    small[...] = jnp.zeros_like(small)
    head_row = jnp.concatenate([head_ref[...], head_ref[...]], axis=1)
    square_row = lax.broadcasted_iota(jnp.int32, (128, 128), 0)
    square_lane = lax.broadcasted_iota(jnp.int32, (128, 128), 1)
    same_half = (square_row < 64) == (square_lane < 64)
    head_mat = jnp.where(same_half, jnp.broadcast_to(head_row, (128, 128)).T, 0.0)
    head_high = head_mat.astype(BF16)
    headm_ref[0:128] = head_high
    headm_ref[128:256] = head_high
    headm_ref[256:384] = (head_mat - head_high.astype(F32)).astype(BF16)
    pick_depth = jnp.where(square_row // 2 == square_lane % 64, 1.0, 0.0).astype(BF16)

    def turn(t, carry):
        for p in range(4):
            turn_block(halo_ref, arranged, p, t)
        return carry

    lax.fori_loop(0, other_count, turn, 0)

    def fill(window, t):
        for p in range(4):
            fill_window(window, p, arranged, p, t - offset, other_count)

    def first(window, t):
        own = (t >= 0) & (t < count)
        next_to = (t - offset >= 0) & (t - offset < other_count)
        out = part_ref[t + 1] + conv_rows(plane_pairs(window, 0, 2), half_mats(m1_ref, side))
        out = jnp.maximum(out, 0.0).astype(BF16)
        for rx in range(2):
            live = jnp.where(side == rx, next_to, own)
            for par in range(2):
                block = out[ROWS * par : ROWS * par + ROWS, 128 * rx : 128 * rx + 128]
                hidden[t + 1, side * 4 + 2 * rx + par] = jnp.where(live, block, jnp.zeros_like(block))

    def near(t):
        for p in range(4):
            hidden[t + 1, (1 - side) * 4 + p] = gated(near_ref, p, t, count)

    def beside(t):
        fill(even_window, t)
        first(even_window, t)

    def pair(j, carry):
        fill(odd_window, 2 * j + 1)
        near(2 * j)
        first(even_window, 2 * j)
        fill(even_window, 2 * j + 2)
        near(2 * j + 1)
        first(odd_window, 2 * j + 1)
        return carry

    hidden[0] = jnp.zeros((8, ROWS, 128), BF16)
    hidden[count + 1] = jnp.zeros((8, ROWS, 128), BF16)
    rims(count, offset, other_count, beside)
    fill(even_window, 0)
    lax.fori_loop(0, count // 2, pair, 0)

    row4 = lax.broadcasted_iota(jnp.int32, (512, 128), 0)
    even4 = row4 % 2 == 0
    plane4 = 4 * side + 2 * (row4 // 128 % 2)
    keep = even4 & (plane4 >= mine) & (plane4 < mine + planes)

    def second(j, carry):
        for u in range(2):
            t = 2 * j + u
            for p in range(8):
                hwin[u, p, :, 0:128] = hidden[t + 1, p]
                hwin[u, p, :, 128:256] = merge_half(hidden[t + 2, p], hidden[t, p])
            out = conv_rows(plane_pairs(hwin, 0, 4, (u,)), [m2_ref[e] for e in range(3)])
            out = jnp.maximum(out, 0.0).astype(BF16)
            for par in range(2):
                for rx in range(2):
                    y2_ref[u, rx, par] = out[ROWS * par : ROWS * par + ROWS, 128 * rx : 128 * rx + 128]
        fine = jnp.concatenate(
            [
                jnp.concatenate(
                    [y2_ref[u, rx, a, 128 * b : 128 * b + 128] for u in range(2) for rx in range(2)],
                    axis=0,
                )
                for a in range(2)
                for b in range(2)
            ],
            axis=1,
        )
        both = jnp.dot(fine, down_mat[...], preferred_element_type=F32)
        coarse = both[:, 0:128] + shifted(both[:, 128:256], -1)
        rect = jnp.maximum(coarse, 0.0)
        high = rect.astype(BF16)
        rest = (rect - high.astype(F32)).astype(BF16)
        logit = jnp.dot(
            jnp.concatenate([high, rest, high], axis=1), headm_ref[...], preferred_element_type=F32
        )
        labels = []
        for u in range(2):
            line = label_ref[:, pl.ds(pl.multiple_of(256 * j + 128 * u, 128), 128)].astype(F32)
            for rx in range(2):
                row = jnp.where(side == 1, line[2 + rx : 3 + rx], line[rx : rx + 1])
                row = jnp.where(same_half, jnp.broadcast_to(row, (128, 128)), 0.0).astype(BF16)
                labels.append(
                    lax.dot_general(
                        pick_depth, row, (((1,), (1,)), ((), ())), preferred_element_type=F32
                    )
                )
        label = jnp.concatenate(labels, axis=0)
        tail = jnp.exp(-jnp.abs(logit))
        soft = jnp.maximum(logit, 0.0) + jnp.log1p(tail)
        sigmoid = jnp.where(logit >= 0.0, 1.0, tail) / (1.0 + tail)
        loss = jnp.where(keep, soft - label * logit, 0.0)
        slope = jnp.where(keep, (sigmoid - label) * (1.0 / COARSE), 0.0)
        small[0:1] += jnp.sum(slope * rect, axis=0, keepdims=True)
        small[1:2] += jnp.sum(loss, axis=0, keepdims=True)
        delta = jnp.where(coarse > 0.0, slope * head_row, 0.0).astype(BF16).astype(F32)
        moved = shifted(delta, 1)
        delta_t[0:128] = delta.astype(BF16).T
        delta_t[128:256] = moved.astype(BF16).T
        back = jnp.dot((delta + moved).astype(BF16), back_mat[...], preferred_element_type=F32)
        for a in range(2):
            for b in range(2):
                lane = (2 * a + b) * 256
                err = jnp.where(even4, back[:, lane : lane + 128], back[:, lane + 128 : lane + 256])
                live = fine[:, lane // 2 : lane // 2 + 128].astype(F32) > 0.0
                err = jnp.where(live, err, 0.0)
                for n in range(4):
                    turned = err[128 * n : 128 * n + 128].astype(BF16).T
                    col = n * 512 + a * 256 + b * 128
                    err_t[128:256, col : col + 128] = turned
                    up = jnp.where(square_lane < 126, pltpu.roll(turned, 126, 1), jnp.zeros_like(turned))
                    down = jnp.where(square_lane >= 2, pltpu.roll(turned, 2, 1), jnp.zeros_like(turned))
                    err_t[0:128, col : col + 128] = up
                    err_t[256:384, col : col + 128] = down
        grad_down[...] += jnp.dot(delta_t[...], fine, preferred_element_type=F32)
        for a in range(3):
            rows = hwin[:, 2 * a : 2 * a + 4].reshape(8 * ROWS, 256)
            grad[a] += jnp.dot(err_t[...], rows, preferred_element_type=F32)
        return carry

    lax.fori_loop(0, count // 2, second, 0)

    low = lanes_low((64, 128))
    rep, chan = lax.axis_index("rep"), lax.axis_index("chan")
    share = 64 // chans // reps

    def emit(slab, value):
        whole[slab] = value

    firsts = []
    for a in range(3):
        for e in range(3):
            both = grad[a, 128 * e : 128 * e + 64] + pltpu.roll(
                grad[a, 128 * e + 64 : 128 * e + 128], 192, 1
            )
            emit(3 * a + e, both[:, 0:128])
            firsts.append(both[:, 128:256])
    for m in range(5):
        right = firsts[2 * m + 1] if 2 * m + 1 < 9 else jnp.zeros_like(firsts[0])
        emit(9 + m, jnp.where(low, pltpu.roll(firsts[2 * m], 64, 1), right))
    halves = [
        grad_down[128 * e : 128 * e + 64] + pltpu.roll(grad_down[128 * e + 64 : 128 * e + 128], 448, 1)
        for e in range(2)
    ]
    for ab in range(4):
        tile = jnp.concatenate([half[:, 128 * ab : 128 * ab + 128] for half in halves], axis=0)
        emit(14 + ab, tile.T[0:64])
    sums = small[...]
    head = sums[0:1] + pltpu.roll(sums, 64, 1)[0:1]
    total = jnp.sum(sums[1:2], axis=1, keepdims=True) * (1.0 / 64)
    row = merge_half(head, jnp.broadcast_to(total, (1, 128)))
    emit(18, jnp.broadcast_to(row, (64, 128)))
    for c in range(chans):
        place = lax.rem(c - chan + chans, chans)
        for ref, r in ((keep_ref, rep), (send_ref, 1 - rep)):
            rows = pl.ds(pl.multiple_of((c * reps + r) * share, share), share)
            ref[place] = whole[:, rows, :]


def final_kernel(foot_ref, mine_ref, peer_ref, second_ref, down_ref, head_ref, loss_ref):
    rep = lax.axis_index("rep")
    share = mine_ref.shape[1]
    for ref, r in ((mine_ref, rep), (peer_ref, 1 - rep)):
        rows = pl.ds(pl.multiple_of(r * share, share), share)
        for a in range(3):
            for e in range(3):
                m = 3 * a + e
                later, first = ref[m], ref[9 + m // 2]
                second_ref[9 * a + e, rows] = first[:, 64 * (m % 2) : 64 * (m % 2) + 64]
                second_ref[9 * a + 3 + e, rows] = later[:, 0:64]
                second_ref[9 * a + 6 + e, rows] = later[:, 64:128]
        for ab in range(4):
            for e in range(2):
                down_ref[2 * ab + e, rows] = ref[14 + ab][:, 64 * e : 64 * e + 64]
    line = mine_ref[18][0:1]
    head_ref[...] = line[:, 0:64]
    live = foot_ref[1, 0]
    for c in range(1, foot_ref.shape[1]):
        live += foot_ref[1, c]
    scale = jnp.full((1, 1), COARSE * live, jnp.int32).astype(F32)
    loss_ref[...] = line[:, 64:65] / scale


def sums_slab(shape):
    return lax.broadcasted_iota(jnp.int32, shape, 0) == 18


def to_wire(value):
    high = lax.reduce_precision(value, 8, 7)
    rest = lax.reduce_precision(value - high, 8, 7)
    lower = lax.broadcasted_iota(jnp.int32, value.shape, 1) >= value.shape[1] // 2
    return jnp.where(sums_slab(value.shape) & lower, rest, high)


def from_wire(value):
    half = value.shape[1] // 2
    other = jnp.concatenate([value[:, half:], value[:, :half]], axis=1)
    return value + jnp.where(sums_slab(value.shape), other, 0.0)


def shards(features, w_first, w_second, w_down, w_head, footprint, labels):
    bricks, chans, reps = lax.axis_size("bricks"), lax.axis_size("chan"), lax.axis_size("rep")
    planes = BRICK // chans
    side = lax.axis_index("chan") * planes // 4
    smem = pl.BlockSpec(memory_space=pltpu.SMEM)
    vmem = pl.BlockSpec(memory_space=pltpu.VMEM)
    features = features[0]
    slabs = features.shape[2] // 4

    packs = pl.pallas_call(
        pack_kernel,
        out_shape=(
            jax.ShapeDtypeStruct((27, 32 // chans, 128), BF16),
            jax.ShapeDtypeStruct((35, 32 // chans, 128), BF16),
        ),
        in_specs=[vmem] * 3,
        out_specs=(vmem, vmem),
        compiler_params=pltpu.CompilerParams(vmem_limit_bytes=16 << 20),
        name="pack",
    )(w_first.transpose(0, 2, 1), w_second.transpose(0, 2, 1), w_down)
    pieces = [[packed] for packed in packs]
    for packed, gathered in zip(packs, pieces):
        for step in range(1, chans):
            ring = [(i, (i + step) % chans) for i in range(chans)]
            gathered.append(lax.ppermute(packed, "chan", ring))

    pairs = []
    for col in range(bricks * reps):
        for c in range(chans):
            src = col + 2 * (c * planes // 4) - 1
            if 0 <= src < bricks * reps:
                ends = [(j // reps * chans + c) * reps + j % reps for j in (src, col)]
                pairs.append(tuple(ends))
    outward = lax.dynamic_slice_in_dim(features, (1 - side) * 4, 4, 1).transpose(1, 2, 0, 3)
    halo = lax.ppermute(outward, ("bricks", "chan", "rep"), pairs)

    part, near, mat1 = pl.pallas_call(
        local_kernel,
        out_shape=(
            jax.ShapeDtypeStruct((slabs + 2, 2 * ROWS, 256), F32),
            jax.ShapeDtypeStruct((4, slabs, ROWS, 128), BF16),
            jax.ShapeDtypeStruct((3, 1024, 256), BF16),
        ),
        in_specs=[smem] + [vmem] * (1 + chans),
        out_specs=(vmem,) * 3,
        scratch_shapes=[
            pltpu.VMEM((27, 64, 128), BF16),
            pltpu.VMEM((27, 64, 128), BF16),
            pltpu.VMEM((8, slabs, ROWS, 128), BF16),
            pltpu.VMEM((8, ROWS, 256), BF16),
            pltpu.VMEM((8, ROWS, 256), BF16),
        ],
        compiler_params=pltpu.CompilerParams(vmem_limit_bytes=36 << 20),
        cost_estimate=pl.CostEstimate(flops=6 * 6 * 512 * 1024 * 512, bytes_accessed=8 << 20, transcendentals=0),
        name="first_local",
    )(footprint, features.transpose(1, 2, 0, 3), *pieces[0])
    mat2, down_mat, back_mat = pl.pallas_call(
        mats_kernel,
        out_shape=(
            jax.ShapeDtypeStruct((3, 1024, 256), BF16),
            jax.ShapeDtypeStruct((512, 256), BF16),
            jax.ShapeDtypeStruct((128, 1024), BF16),
        ),
        in_specs=[pl.BlockSpec(memory_space=pl.ANY)] + [vmem] * chans,
        out_specs=(vmem,) * 3,
        scratch_shapes=[pltpu.VMEM((35, 64, 128), BF16), pltpu.VMEM((27, 64, 128), BF16)],
        compiler_params=pltpu.CompilerParams(vmem_limit_bytes=16 << 20),
        name="mats",
    )(near, *pieces[1])
    parts = jax.ShapeDtypeStruct((chans, 19, 64 // chans // reps, 128), F32)
    keep, send = pl.pallas_call(
        main_kernel,
        out_shape=(parts, parts),
        in_specs=[smem] + [vmem] * 9,
        out_specs=(vmem, vmem),
        scratch_shapes=[
            pltpu.VMEM((4, slabs, ROWS, 128), BF16),
            pltpu.VMEM((4, ROWS, 256), BF16),
            pltpu.VMEM((4, ROWS, 256), BF16),
            pltpu.VMEM((slabs + 2, 8, ROWS, 128), BF16),
            pltpu.VMEM((2, 8, ROWS, 256), BF16),
            pltpu.VMEM((384, 128), BF16),
            pltpu.VMEM((2, 2, 2, ROWS, 128), BF16),
            pltpu.VMEM((256, 512), BF16),
            pltpu.VMEM((384, 2048), BF16),
            pltpu.VMEM((3, 384, 256), F32),
            pltpu.VMEM((256, 512), F32),
            pltpu.VMEM((8, 128), F32),
            pltpu.VMEM((19, 64, 128), F32),
        ],
        compiler_params=pltpu.CompilerParams(vmem_limit_bytes=40 << 20),
        cost_estimate=pl.CostEstimate(flops=4 * 6 * 6 * 512 * 1024 * 512, bytes_accessed=16 << 20, transcendentals=0),
        name="head_and_grads",
    )(footprint, part, halo, near, mat1, mat2, down_mat, back_mat, w_head.reshape(1, 64), labels[0])

    swap = [(i, 1 - i) for i in range(reps)]
    got = lax.ppermute(send, "rep", swap)
    wire = [to_wire(keep[step] + got[step]) for step in range(chans)]
    near_sums = []
    for flip in range(2):
        for step in range(chans):
            if flip == step == 0:
                near_sums.append(wire[0])
                continue
            routes = [
                (b * chans + c, (b ^ flip) * chans + (c + step) % chans)
                for b in range(bricks)
                for c in range(chans)
            ]
            sent = lax.ppermute(wire[step].astype(BF16), ("bricks", "chan"), routes)
            near_sums.append(sent.astype(F32))
    mine = from_wire(sum(near_sums[1:chans], near_sums[0]) + sum(near_sums[chans + 1 :], near_sums[chans]))
    step = 2
    while step < bricks:
        wire = to_wire(mine)
        sent = lax.ppermute(wire.astype(BF16), "bricks", [(i, i ^ step) for i in range(bricks)])
        mine = from_wire(wire + sent.astype(F32))
        step *= 2
    peer = lax.ppermute(mine, "rep", swap)
    share = 64 // chans
    second, down, head, loss = pl.pallas_call(
        final_kernel,
        out_shape=(
            jax.ShapeDtypeStruct((27, share, 64), F32),
            jax.ShapeDtypeStruct((8, share, 64), F32),
            jax.ShapeDtypeStruct((1, 64), F32),
            jax.ShapeDtypeStruct((1, 1), F32),
        ),
        in_specs=[smem, vmem, vmem],
        out_specs=(vmem,) * 4,
        compiler_params=pltpu.CompilerParams(vmem_limit_bytes=16 << 20),
        name="assemble",
    )(footprint, mine, peer)
    return second.transpose(0, 2, 1), down, head.reshape(64), loss.reshape(1)


def solution(mesh):
    return jax.shard_map(
        shards,
        mesh=mesh,
        in_specs=(
            P(("groups", "bricks", "rep"), None, None, None, None),
            P(None, None, "chan"),
            P(None, None, "chan"),
            P(None, "chan", None),
            P(),
            P(None, "groups"),
            P(("groups", "bricks", "rep"), None, None),
        ),
        out_specs=(P("groups", None, "chan"), P("groups", "chan", None), P("groups"), P("groups")),
        check_vma=False,
    )
```

```python
import jax
import jax.numpy as jnp
from jax import lax
from jax.experimental import pallas as pl
from jax.experimental.pallas import tpu as pltpu
from jax.sharding import PartitionSpec as P

BRICK = 8
COARSE = 1024
ROWS = 256
F32 = jnp.float32
BF16 = jnp.bfloat16


def lanes_low(shape):
    return lax.broadcasted_iota(jnp.int32, shape, len(shape) - 1) % 128 < 64


def merge_half(low, high):
    return jnp.where(lanes_low(low.shape), low, high)


def shifted(value, by):
    row = lax.broadcasted_iota(jnp.int32, value.shape, 0) % 128
    inside = row >= by if by > 0 else row < 128 + by
    return jnp.where(inside, pltpu.roll(value, by % value.shape[0], 0), 0.0)


def build_conv(w_ref, out_ref):
    zero = jnp.zeros((64, 128), BF16)
    for e in range(3):
        for k in range(4):
            for slot, d in enumerate((0, 1, 2, -1)):
                for rx in range(2):
                    a = k - rx
                    halves = []
                    for ry in range(2):
                        b = d - ry + 1
                        live = 0 <= a < 3 and 0 <= b < 3
                        halves.append(w_ref[9 * a + 3 * b + e] if live else zero)
                    row = k * 256 + slot * 64
                    out_ref[e, row : row + 64, rx * 128 : rx * 128 + 128] = merge_half(*halves)


def plane_pairs(window_ref, first, pairs, slot=()):
    blocks = [window_ref[(*slot, pl.ds(first + 2 * k, 2))].reshape(2 * ROWS, 256) for k in range(pairs)]
    return jnp.concatenate(blocks, axis=1)


def conv_rows(lhs, mats):
    below, level, above = [jnp.dot(lhs, mat, preferred_element_type=F32) for mat in mats]
    return level + shifted(below, 2) + shifted(above, -2)


def half_mats(mat_ref, half):
    rows = pl.ds(pl.multiple_of(512 * half, 512), 512)
    return [mat_ref[e, rows, :] for e in range(3)]


def neighbour(foot_ref, column, columns, side):
    other = column + 2 * side - 1
    present = (other >= 0) & (other < columns)
    other = jnp.clip(other, 0, columns - 1)
    count = jnp.where(present, 2 * foot_ref[1, other], 0)
    return count, 2 * (foot_ref[0, other] - foot_ref[0, column])


def rims(count, offset, other_count, work):
    def rim(i, carry):
        t = jnp.where(i == 0, -1, count)

        @pl.when((t - offset >= 0) & (t - offset < other_count))
        def _():
            work(t)

        return carry

    lax.fori_loop(0, 2, rim, 0)


def gated(ref, plane, index, count):
    inside = (index >= 0) & (index < count)
    block = ref[plane, jnp.clip(index, 0, ref.shape[1] - 1)]
    return jnp.where(inside, block, jnp.zeros_like(block))


def turn_block(src_ref, dst_ref, plane, t):
    for py in range(2):
        tall = jnp.concatenate([src_ref[plane, 4 * t + py], src_ref[plane, 4 * t + 2 + py]], axis=0)
        dst_ref[plane, t, 128 * py : 128 * py + 128] = tall.T


def fill_window(window_ref, plane, src_ref, src_plane, index, count):
    window_ref[plane, :, 0:128] = gated(src_ref, src_plane, index, count)
    window_ref[plane, :, 128:256] = merge_half(
        gated(src_ref, src_plane, index + 1, count), gated(src_ref, src_plane, index - 1, count)
    )


def pack_kernel(w1_ref, w2_ref, wd_ref, first_ref, rest_ref):
    half = w1_ref.shape[1] // 2

    def dense(ref):
        return jnp.concatenate([ref[:, :half], ref[:, half:]], axis=2)

    first_ref[...] = dense(w1_ref)
    rest_ref[0 : w2_ref.shape[0]] = dense(w2_ref)
    rest_ref[w2_ref.shape[0] :] = dense(wd_ref)


def unpack(piece_refs, whole):
    chans = lax.axis_size("chan")
    me = lax.axis_index("chan")
    half = piece_refs[0].shape[1]
    for step in range(chans):
        block = piece_refs[step][...]
        source = lax.rem(me - step + chans, chans)
        for h in range(2):
            part = block[:, :, 64 * h : 64 * h + 64]
            rows = pl.ds(pl.multiple_of((2 * source + h) * half, half), half)
            whole[:, rows, :] = jnp.concatenate([part, part], axis=2)


def turn_taps(whole, turned):
    for t in range(27):
        turned[t] = jnp.concatenate([whole[t], whole[t]], axis=0).T[0:64]


def mats_kernel(after_ref, *refs):
    chans = lax.axis_size("chan")
    m2_ref, down_ref, back_ref, whole, turned = refs[chans:]
    unpack(refs[:chans], whole)
    turn_taps(whole, turned)
    build_conv(turned, m2_ref)
    low = lanes_low((64, 128))
    zero = jnp.zeros((64, 128), BF16)
    for t in range(8):
        ab, e = t // 2, t % 2
        block = whole[27 + t]
        tile = jnp.concatenate([jnp.where(low, block, zero), jnp.where(low, zero, block)], axis=0)
        down_ref[ab * 128 : ab * 128 + 128, e * 128 : e * 128 + 128] = tile
        back_ref[:, t * 128 : t * 128 + 128] = tile.T


def local_kernel(foot_ref, feat_ref, *refs):
    chans = lax.axis_size("chan")
    part_ref, y1_ref, m1_ref, whole, turned, arranged, even_window, odd_window = refs[chans:]
    column = lax.axis_index("bricks") * lax.axis_size("rep") + lax.axis_index("rep")
    side = lax.axis_index("chan") * (BRICK // chans) // 4
    count = 2 * foot_ref[1, column]
    columns = lax.axis_size("bricks") * lax.axis_size("rep")
    other_count, offset = neighbour(foot_ref, column, columns, side)

    unpack(refs[:chans], whole)
    turn_taps(whole, turned)
    build_conv(turned, m1_ref)

    def turn(t, carry):
        for p in range(8):
            turn_block(feat_ref, arranged, p, t)
        return carry

    lax.fori_loop(0, count, turn, 0)

    def fill(window, t):
        for p in range(8):
            fill_window(window, p, arranged, p, t, count)

    def edge(window, t):
        lhs = plane_pairs(window, 4 * side, 2)
        part_ref[t + 1] = conv_rows(lhs, half_mats(m1_ref, 1 - side))

    def conv(window, t):
        edge(window, t)
        lhs = plane_pairs(window, 0, 4)
        out = jnp.maximum(conv_rows(lhs, [m1_ref[e] for e in range(3)]), 0.0).astype(BF16)
        for par in range(2):
            for rx in range(2):
                y1_ref[2 * rx + par, t] = out[ROWS * par : ROWS * par + ROWS, 128 * rx : 128 * rx + 128]

    def pair(j, carry):
        fill(odd_window, 2 * j + 1)
        conv(even_window, 2 * j)
        fill(even_window, 2 * j + 2)
        conv(odd_window, 2 * j + 1)
        return carry

    def beside(t):
        fill(even_window, t)
        edge(even_window, t)

    rims(count, offset, other_count, beside)
    fill(even_window, 0)
    lax.fori_loop(0, count // 2, pair, 0)


def main_kernel(
    foot_ref,
    part_ref,
    halo_ref,
    near_ref,
    m1_ref,
    m2_ref,
    down_mat,
    back_mat,
    head_ref,
    label_ref,
    keep_ref,
    send_ref,
    arranged,
    even_window,
    odd_window,
    hidden,
    hwin,
    headm_ref,
    y2_ref,
    delta_t,
    err_t,
    grad,
    grad_down,
    small,
    whole,
):
    reps, chans = lax.axis_size("rep"), lax.axis_size("chan")
    columns = lax.axis_size("bricks") * reps
    column = lax.axis_index("bricks") * reps + lax.axis_index("rep")
    planes = BRICK // chans
    mine = lax.axis_index("chan") * planes
    side = mine // 4
    count = 2 * foot_ref[1, column]
    other_count, offset = neighbour(foot_ref, column, columns, side)

    grad[...] = jnp.zeros_like(grad)
    grad_down[...] = jnp.zeros_like(grad_down)
    small[...] = jnp.zeros_like(small)
    head_row = jnp.concatenate([head_ref[...], head_ref[...]], axis=1)
    square_row = lax.broadcasted_iota(jnp.int32, (128, 128), 0)
    square_lane = lax.broadcasted_iota(jnp.int32, (128, 128), 1)
    same_half = (square_row < 64) == (square_lane < 64)
    head_mat = jnp.where(same_half, jnp.broadcast_to(head_row, (128, 128)).T, 0.0)
    head_high = head_mat.astype(BF16)
    headm_ref[0:128] = head_high
    headm_ref[128:256] = head_high
    headm_ref[256:384] = (head_mat - head_high.astype(F32)).astype(BF16)
    pick_depth = jnp.where(square_row // 2 == square_lane % 64, 1.0, 0.0).astype(BF16)

    def turn(t, carry):
        for p in range(4):
            turn_block(halo_ref, arranged, p, t)
        return carry

    lax.fori_loop(0, other_count, turn, 0)

    def fill(window, t):
        for p in range(4):
            fill_window(window, p, arranged, p, t - offset, other_count)

    def first(window, t):
        own = (t >= 0) & (t < count)
        next_to = (t - offset >= 0) & (t - offset < other_count)
        out = part_ref[t + 1] + conv_rows(plane_pairs(window, 0, 2), half_mats(m1_ref, side))
        out = jnp.maximum(out, 0.0).astype(BF16)
        for rx in range(2):
            live = jnp.where(side == rx, next_to, own)
            for par in range(2):
                block = out[ROWS * par : ROWS * par + ROWS, 128 * rx : 128 * rx + 128]
                hidden[t + 1, side * 4 + 2 * rx + par] = jnp.where(live, block, jnp.zeros_like(block))

    def near(t):
        for p in range(4):
            hidden[t + 1, (1 - side) * 4 + p] = gated(near_ref, p, t, count)

    def beside(t):
        fill(even_window, t)
        first(even_window, t)

    def pair(j, carry):
        fill(odd_window, 2 * j + 1)
        near(2 * j)
        first(even_window, 2 * j)
        fill(even_window, 2 * j + 2)
        near(2 * j + 1)
        first(odd_window, 2 * j + 1)
        return carry

    hidden[0] = jnp.zeros((8, ROWS, 128), BF16)
    hidden[count + 1] = jnp.zeros((8, ROWS, 128), BF16)
    rims(count, offset, other_count, beside)
    fill(even_window, 0)
    lax.fori_loop(0, count // 2, pair, 0)

    row4 = lax.broadcasted_iota(jnp.int32, (512, 128), 0)
    even4 = row4 % 2 == 0
    plane4 = 4 * side + 2 * (row4 // 128 % 2)
    keep = even4 & (plane4 >= mine) & (plane4 < mine + planes)

    def second(j, carry):
        for u in range(2):
            t = 2 * j + u
            for p in range(8):
                hwin[u, p, :, 0:128] = hidden[t + 1, p]
                hwin[u, p, :, 128:256] = merge_half(hidden[t + 2, p], hidden[t, p])
            out = conv_rows(plane_pairs(hwin, 0, 4, (u,)), [m2_ref[e] for e in range(3)])
            out = jnp.maximum(out, 0.0).astype(BF16)
            for par in range(2):
                for rx in range(2):
                    y2_ref[u, rx, par] = out[ROWS * par : ROWS * par + ROWS, 128 * rx : 128 * rx + 128]
        fine = jnp.concatenate(
            [
                jnp.concatenate(
                    [y2_ref[u, rx, a, 128 * b : 128 * b + 128] for u in range(2) for rx in range(2)],
                    axis=0,
                )
                for a in range(2)
                for b in range(2)
            ],
            axis=1,
        )
        both = jnp.dot(fine, down_mat[...], preferred_element_type=F32)
        coarse = both[:, 0:128] + shifted(both[:, 128:256], -1)
        rect = jnp.maximum(coarse, 0.0)
        high = rect.astype(BF16)
        rest = (rect - high.astype(F32)).astype(BF16)
        logit = jnp.dot(
            jnp.concatenate([high, rest, high], axis=1), headm_ref[...], preferred_element_type=F32
        )
        labels = []
        for u in range(2):
            line = label_ref[:, pl.ds(pl.multiple_of(256 * j + 128 * u, 128), 128)].astype(F32)
            for rx in range(2):
                row = jnp.where(side == 1, line[2 + rx : 3 + rx], line[rx : rx + 1])
                row = jnp.where(same_half, jnp.broadcast_to(row, (128, 128)), 0.0).astype(BF16)
                labels.append(
                    lax.dot_general(
                        pick_depth, row, (((1,), (1,)), ((), ())), preferred_element_type=F32
                    )
                )
        label = jnp.concatenate(labels, axis=0)
        tail = jnp.exp(-jnp.abs(logit))
        soft = jnp.maximum(logit, 0.0) + jnp.log1p(tail)
        sigmoid = jnp.where(logit >= 0.0, 1.0, tail) / (1.0 + tail)
        loss = jnp.where(keep, soft - label * logit, 0.0)
        slope = jnp.where(keep, (sigmoid - label) * (1.0 / COARSE), 0.0)
        small[0:1] += jnp.sum(slope * rect, axis=0, keepdims=True)
        small[1:2] += jnp.sum(loss, axis=0, keepdims=True)
        delta = jnp.where(coarse > 0.0, slope * head_row, 0.0).astype(BF16).astype(F32)
        moved = shifted(delta, 1)
        delta_t[0:128] = delta.astype(BF16).T
        delta_t[128:256] = moved.astype(BF16).T
        back = jnp.dot((delta + moved).astype(BF16), back_mat[...], preferred_element_type=F32)
        for a in range(2):
            for b in range(2):
                lane = (2 * a + b) * 256
                err = jnp.where(even4, back[:, lane : lane + 128], back[:, lane + 128 : lane + 256])
                live = fine[:, lane // 2 : lane // 2 + 128].astype(F32) > 0.0
                err = jnp.where(live, err, 0.0)
                for n in range(4):
                    turned = err[128 * n : 128 * n + 128].astype(BF16).T
                    row = 384 * (1 - n % 2)
                    col = n // 2 * 512 + a * 256 + b * 128
                    err_t[row + 128 : row + 256, col : col + 128] = turned
                    up = jnp.where(square_lane < 126, pltpu.roll(turned, 126, 1), jnp.zeros_like(turned))
                    down = jnp.where(square_lane >= 2, pltpu.roll(turned, 2, 1), jnp.zeros_like(turned))
                    err_t[row : row + 128, col : col + 128] = up
                    err_t[row + 256 : row + 384, col : col + 128] = down
        grad_down[...] += jnp.dot(delta_t[...], fine, preferred_element_type=F32)
        for k in range(4):
            rows = hwin[:, 2 * k : 2 * k + 2].reshape(4 * ROWS, 256)
            lower, upper = (384, 768) if k == 0 else (0, 384) if k == 3 else (0, 768)
            part = jnp.dot(err_t[lower:upper], rows, preferred_element_type=F32)
            if k > 0:
                grad[k - 1] += part[0:384]
            if k < 3:
                grad[k] += part[upper - lower - 384 :]
        return carry

    lax.fori_loop(0, count // 2, second, 0)

    low = lanes_low((64, 128))
    rep, chan = lax.axis_index("rep"), lax.axis_index("chan")
    share = 64 // chans // reps

    def emit(slab, value):
        whole[slab] = value

    firsts = []
    for a in range(3):
        for e in range(3):
            both = grad[a, 128 * e : 128 * e + 64] + pltpu.roll(
                grad[a, 128 * e + 64 : 128 * e + 128], 192, 1
            )
            emit(3 * a + e, both[:, 0:128])
            firsts.append(both[:, 128:256])
    for m in range(5):
        right = firsts[2 * m + 1] if 2 * m + 1 < 9 else jnp.zeros_like(firsts[0])
        emit(9 + m, jnp.where(low, pltpu.roll(firsts[2 * m], 64, 1), right))
    halves = [
        grad_down[128 * e : 128 * e + 64] + pltpu.roll(grad_down[128 * e + 64 : 128 * e + 128], 448, 1)
        for e in range(2)
    ]
    for ab in range(4):
        tile = jnp.concatenate([half[:, 128 * ab : 128 * ab + 128] for half in halves], axis=0)
        emit(14 + ab, tile.T[0:64])
    sums = small[...]
    head = sums[0:1] + pltpu.roll(sums, 64, 1)[0:1]
    total = jnp.sum(sums[1:2], axis=1, keepdims=True) * (1.0 / 64)
    row = merge_half(head, jnp.broadcast_to(total, (1, 128)))
    emit(18, jnp.broadcast_to(row, (64, 128)))
    for c in range(chans):
        place = lax.rem(c - chan + chans, chans)
        for ref, r in ((keep_ref, rep), (send_ref, 1 - rep)):
            rows = pl.ds(pl.multiple_of((c * reps + r) * share, share), share)
            ref[place] = whole[:, rows, :]


def final_kernel(foot_ref, mine_ref, peer_ref, second_ref, down_ref, head_ref, loss_ref):
    rep = lax.axis_index("rep")
    share = mine_ref.shape[1]
    for ref, r in ((mine_ref, rep), (peer_ref, 1 - rep)):
        rows = pl.ds(pl.multiple_of(r * share, share), share)
        for a in range(3):
            for e in range(3):
                m = 3 * a + e
                later, first = ref[m], ref[9 + m // 2]
                second_ref[9 * a + e, rows] = first[:, 64 * (m % 2) : 64 * (m % 2) + 64]
                second_ref[9 * a + 3 + e, rows] = later[:, 0:64]
                second_ref[9 * a + 6 + e, rows] = later[:, 64:128]
        for ab in range(4):
            for e in range(2):
                down_ref[2 * ab + e, rows] = ref[14 + ab][:, 64 * e : 64 * e + 64]
    line = mine_ref[18][0:1]
    head_ref[...] = line[:, 0:64]
    live = foot_ref[1, 0]
    for c in range(1, foot_ref.shape[1]):
        live += foot_ref[1, c]
    scale = jnp.full((1, 1), COARSE * live, jnp.int32).astype(F32)
    loss_ref[...] = line[:, 64:65] / scale


def sums_slab(shape):
    return lax.broadcasted_iota(jnp.int32, shape, 0) == 18


def to_wire(value):
    high = lax.reduce_precision(value, 8, 7)
    rest = lax.reduce_precision(value - high, 8, 7)
    lower = lax.broadcasted_iota(jnp.int32, value.shape, 1) >= value.shape[1] // 2
    return jnp.where(sums_slab(value.shape) & lower, rest, high)


def from_wire(value):
    half = value.shape[1] // 2
    other = jnp.concatenate([value[:, half:], value[:, :half]], axis=1)
    return value + jnp.where(sums_slab(value.shape), other, 0.0)


def shards(features, w_first, w_second, w_down, w_head, footprint, labels):
    bricks, chans, reps = lax.axis_size("bricks"), lax.axis_size("chan"), lax.axis_size("rep")
    planes = BRICK // chans
    side = lax.axis_index("chan") * planes // 4
    smem = pl.BlockSpec(memory_space=pltpu.SMEM)
    vmem = pl.BlockSpec(memory_space=pltpu.VMEM)
    features = features[0]
    slabs = features.shape[2] // 4

    packs = pl.pallas_call(
        pack_kernel,
        out_shape=(
            jax.ShapeDtypeStruct((27, 32 // chans, 128), BF16),
            jax.ShapeDtypeStruct((35, 32 // chans, 128), BF16),
        ),
        in_specs=[vmem] * 3,
        out_specs=(vmem, vmem),
        compiler_params=pltpu.CompilerParams(vmem_limit_bytes=16 << 20),
        name="pack",
    )(w_first.transpose(0, 2, 1), w_second.transpose(0, 2, 1), w_down)
    pieces = [[packed] for packed in packs]
    for packed, gathered in zip(packs, pieces):
        for step in range(1, chans):
            ring = [(i, (i + step) % chans) for i in range(chans)]
            gathered.append(lax.ppermute(packed, "chan", ring))

    pairs = []
    for col in range(bricks * reps):
        for c in range(chans):
            src = col + 2 * (c * planes // 4) - 1
            if 0 <= src < bricks * reps:
                ends = [(j // reps * chans + c) * reps + j % reps for j in (src, col)]
                pairs.append(tuple(ends))
    outward = lax.dynamic_slice_in_dim(features, (1 - side) * 4, 4, 1).transpose(1, 2, 0, 3)
    halo = lax.ppermute(outward, ("bricks", "chan", "rep"), pairs)

    part, near, mat1 = pl.pallas_call(
        local_kernel,
        out_shape=(
            jax.ShapeDtypeStruct((slabs + 2, 2 * ROWS, 256), F32),
            jax.ShapeDtypeStruct((4, slabs, ROWS, 128), BF16),
            jax.ShapeDtypeStruct((3, 1024, 256), BF16),
        ),
        in_specs=[smem] + [vmem] * (1 + chans),
        out_specs=(vmem,) * 3,
        scratch_shapes=[
            pltpu.VMEM((27, 64, 128), BF16),
            pltpu.VMEM((27, 64, 128), BF16),
            pltpu.VMEM((8, slabs, ROWS, 128), BF16),
            pltpu.VMEM((8, ROWS, 256), BF16),
            pltpu.VMEM((8, ROWS, 256), BF16),
        ],
        compiler_params=pltpu.CompilerParams(vmem_limit_bytes=36 << 20),
        cost_estimate=pl.CostEstimate(flops=6 * 6 * 512 * 1024 * 512, bytes_accessed=8 << 20, transcendentals=0),
        name="first_local",
    )(footprint, features.transpose(1, 2, 0, 3), *pieces[0])
    mat2, down_mat, back_mat = pl.pallas_call(
        mats_kernel,
        out_shape=(
            jax.ShapeDtypeStruct((3, 1024, 256), BF16),
            jax.ShapeDtypeStruct((512, 256), BF16),
            jax.ShapeDtypeStruct((128, 1024), BF16),
        ),
        in_specs=[pl.BlockSpec(memory_space=pl.ANY)] + [vmem] * chans,
        out_specs=(vmem,) * 3,
        scratch_shapes=[pltpu.VMEM((35, 64, 128), BF16), pltpu.VMEM((27, 64, 128), BF16)],
        compiler_params=pltpu.CompilerParams(vmem_limit_bytes=16 << 20),
        name="mats",
    )(near, *pieces[1])
    parts = jax.ShapeDtypeStruct((chans, 19, 64 // chans // reps, 128), F32)
    keep, send = pl.pallas_call(
        main_kernel,
        out_shape=(parts, parts),
        in_specs=[smem] + [vmem] * 9,
        out_specs=(vmem, vmem),
        scratch_shapes=[
            pltpu.VMEM((4, slabs, ROWS, 128), BF16),
            pltpu.VMEM((4, ROWS, 256), BF16),
            pltpu.VMEM((4, ROWS, 256), BF16),
            pltpu.VMEM((slabs + 2, 8, ROWS, 128), BF16),
            pltpu.VMEM((2, 8, ROWS, 256), BF16),
            pltpu.VMEM((384, 128), BF16),
            pltpu.VMEM((2, 2, 2, ROWS, 128), BF16),
            pltpu.VMEM((256, 512), BF16),
            pltpu.VMEM((768, 1024), BF16),
            pltpu.VMEM((3, 384, 256), F32),
            pltpu.VMEM((256, 512), F32),
            pltpu.VMEM((8, 128), F32),
            pltpu.VMEM((19, 64, 128), F32),
        ],
        compiler_params=pltpu.CompilerParams(vmem_limit_bytes=40 << 20),
        cost_estimate=pl.CostEstimate(flops=4 * 6 * 6 * 512 * 1024 * 512, bytes_accessed=16 << 20, transcendentals=0),
        name="head_and_grads",
    )(footprint, part, halo, near, mat1, mat2, down_mat, back_mat, w_head.reshape(1, 64), labels[0])

    swap = [(i, 1 - i) for i in range(reps)]
    got = lax.ppermute(send, "rep", swap)
    wire = [to_wire(keep[step] + got[step]) for step in range(chans)]
    near_sums = []
    for flip in range(2):
        for step in range(chans):
            if flip == step == 0:
                near_sums.append(wire[0])
                continue
            routes = [
                (b * chans + c, (b ^ flip) * chans + (c + step) % chans)
                for b in range(bricks)
                for c in range(chans)
            ]
            sent = lax.ppermute(wire[step].astype(BF16), ("bricks", "chan"), routes)
            near_sums.append(sent.astype(F32))
    mine = from_wire(sum(near_sums[1:chans], near_sums[0]) + sum(near_sums[chans + 1 :], near_sums[chans]))
    step = 2
    while step < bricks:
        wire = to_wire(mine)
        sent = lax.ppermute(wire.astype(BF16), "bricks", [(i, i ^ step) for i in range(bricks)])
        mine = from_wire(wire + sent.astype(F32))
        step *= 2
    peer = lax.ppermute(mine, "rep", swap)
    share = 64 // chans
    second, down, head, loss = pl.pallas_call(
        final_kernel,
        out_shape=(
            jax.ShapeDtypeStruct((27, share, 64), F32),
            jax.ShapeDtypeStruct((8, share, 64), F32),
            jax.ShapeDtypeStruct((1, 64), F32),
            jax.ShapeDtypeStruct((1, 1), F32),
        ),
        in_specs=[smem, vmem, vmem],
        out_specs=(vmem,) * 4,
        compiler_params=pltpu.CompilerParams(vmem_limit_bytes=16 << 20),
        name="assemble",
    )(footprint, mine, peer)
    return second.transpose(0, 2, 1), down, head.reshape(64), loss.reshape(1)


def solution(mesh):
    return jax.shard_map(
        shards,
        mesh=mesh,
        in_specs=(
            P(("groups", "bricks", "rep"), None, None, None, None),
            P(None, None, "chan"),
            P(None, None, "chan"),
            P(None, "chan", None),
            P(),
            P(None, "groups"),
            P(("groups", "bricks", "rep"), None, None),
        ),
        out_specs=(P("groups", None, "chan"), P("groups", "chan", None), P("groups"), P("groups")),
        check_vma=False,
    )
```

```python
import jax
import jax.numpy as jnp
from jax import lax
from jax.experimental import pallas as pl
from jax.experimental.pallas import tpu as pltpu
from jax.sharding import PartitionSpec as P

BRICK = 8
COARSE = 1024
ROWS = 256
F32 = jnp.float32
BF16 = jnp.bfloat16


def lanes_low(shape):
    return lax.broadcasted_iota(jnp.int32, shape, len(shape) - 1) % 128 < 64


def merge_half(low, high):
    return jnp.where(lanes_low(low.shape), low, high)


def shifted(value, by):
    row = lax.broadcasted_iota(jnp.int32, value.shape, 0) % 128
    inside = row >= by if by > 0 else row < 128 + by
    return jnp.where(inside, pltpu.roll(value, by % value.shape[0], 0), 0.0)


def build_conv(w_ref, out_ref):
    zero = jnp.zeros((64, 128), BF16)
    for e in range(3):
        for k in range(4):
            for slot, d in enumerate((0, 1, 2, -1)):
                for rx in range(2):
                    a = k - rx
                    halves = []
                    for ry in range(2):
                        b = d - ry + 1
                        live = 0 <= a < 3 and 0 <= b < 3
                        halves.append(w_ref[9 * a + 3 * b + e] if live else zero)
                    row = k * 256 + slot * 64
                    out_ref[e, row : row + 64, rx * 128 : rx * 128 + 128] = merge_half(*halves)


def plane_pairs(window_ref, first, pairs, slot=()):
    blocks = [window_ref[(*slot, pl.ds(first + 2 * k, 2))].reshape(2 * ROWS, 256) for k in range(pairs)]
    return jnp.concatenate(blocks, axis=1)


def conv_rows(lhs, mats):
    below, level, above = [jnp.dot(lhs, mat, preferred_element_type=F32) for mat in mats]
    return level + shifted(below, 2) + shifted(above, -2)


def half_mats(mat_ref, half):
    rows = pl.ds(pl.multiple_of(512 * half, 512), 512)
    return [mat_ref[e, rows, :] for e in range(3)]


def neighbour(foot_ref, column, columns, side):
    other = column + 2 * side - 1
    present = (other >= 0) & (other < columns)
    other = jnp.clip(other, 0, columns - 1)
    count = jnp.where(present, 2 * foot_ref[1, other], 0)
    return count, 2 * (foot_ref[0, other] - foot_ref[0, column])


def rims(count, offset, other_count, work):
    def rim(i, carry):
        t = jnp.where(i == 0, -1, count)

        @pl.when((t - offset >= 0) & (t - offset < other_count))
        def _():
            work(t)

        return carry

    lax.fori_loop(0, 2, rim, 0)


def gated(ref, plane, index, count):
    inside = (index >= 0) & (index < count)
    block = ref[plane, jnp.clip(index, 0, ref.shape[1] - 1)]
    return jnp.where(inside, block, jnp.zeros_like(block))


def turn_block(src_ref, dst_ref, plane, t):
    for py in range(2):
        tall = jnp.concatenate([src_ref[plane, 4 * t + py], src_ref[plane, 4 * t + 2 + py]], axis=0)
        dst_ref[plane, t, 128 * py : 128 * py + 128] = tall.T


def fill_window(window_ref, plane, src_ref, src_plane, index, count):
    window_ref[plane, :, 0:128] = gated(src_ref, src_plane, index, count)
    window_ref[plane, :, 128:256] = merge_half(
        gated(src_ref, src_plane, index + 1, count), gated(src_ref, src_plane, index - 1, count)
    )


def pack_kernel(w1_ref, w2_ref, wd_ref, first_ref, rest_ref):
    half = w1_ref.shape[1] // 2

    def dense(ref):
        return jnp.concatenate([ref[:, :half], ref[:, half:]], axis=2)

    first_ref[...] = dense(w1_ref)
    rest_ref[0 : w2_ref.shape[0]] = dense(w2_ref)
    rest_ref[w2_ref.shape[0] :] = dense(wd_ref)


def unpack(piece_refs, whole):
    chans = lax.axis_size("chan")
    me = lax.axis_index("chan")
    half = piece_refs[0].shape[1]
    for step in range(chans):
        block = piece_refs[step][...]
        source = lax.rem(me - step + chans, chans)
        for h in range(2):
            part = block[:, :, 64 * h : 64 * h + 64]
            rows = pl.ds(pl.multiple_of((2 * source + h) * half, half), half)
            whole[:, rows, :] = jnp.concatenate([part, part], axis=2)


def turn_taps(whole, turned):
    for t in range(27):
        turned[t] = jnp.concatenate([whole[t], whole[t]], axis=0).T[0:64]


def mats_kernel(after_ref, *refs):
    chans = lax.axis_size("chan")
    m2_ref, down_ref, back_ref, whole, turned = refs[chans:]
    unpack(refs[:chans], whole)
    turn_taps(whole, turned)
    build_conv(turned, m2_ref)
    low = lanes_low((64, 128))
    zero = jnp.zeros((64, 128), BF16)
    for t in range(8):
        ab, e = t // 2, t % 2
        block = whole[27 + t]
        tile = jnp.concatenate([jnp.where(low, block, zero), jnp.where(low, zero, block)], axis=0)
        down_ref[ab * 128 : ab * 128 + 128, e * 128 : e * 128 + 128] = tile
        back_ref[:, t * 128 : t * 128 + 128] = tile.T


def local_kernel(foot_ref, feat_ref, *refs):
    chans = lax.axis_size("chan")
    part_ref, y1_ref, m1_ref, whole, turned, arranged, even_window, odd_window = refs[chans:]
    column = lax.axis_index("bricks") * lax.axis_size("rep") + lax.axis_index("rep")
    side = lax.axis_index("chan") * (BRICK // chans) // 4
    count = 2 * foot_ref[1, column]
    columns = lax.axis_size("bricks") * lax.axis_size("rep")
    other_count, offset = neighbour(foot_ref, column, columns, side)

    unpack(refs[:chans], whole)
    turn_taps(whole, turned)
    build_conv(turned, m1_ref)

    def turn(t, carry):
        for p in range(8):
            turn_block(feat_ref, arranged, p, t)
        return carry

    lax.fori_loop(0, count, turn, 0)

    def fill(window, t):
        for p in range(8):
            fill_window(window, p, arranged, p, t, count)

    def edge(window, t):
        lhs = plane_pairs(window, 4 * side, 2)
        part_ref[t + 1] = conv_rows(lhs, half_mats(m1_ref, 1 - side))

    def conv(window, t):
        edge(window, t)
        lhs = plane_pairs(window, 0, 4)
        out = jnp.maximum(conv_rows(lhs, [m1_ref[e] for e in range(3)]), 0.0).astype(BF16)
        for par in range(2):
            for rx in range(2):
                y1_ref[2 * rx + par, t] = out[ROWS * par : ROWS * par + ROWS, 128 * rx : 128 * rx + 128]

    def pair(j, carry):
        fill(odd_window, 2 * j + 1)
        conv(even_window, 2 * j)
        fill(even_window, 2 * j + 2)
        conv(odd_window, 2 * j + 1)
        return carry

    def beside(t):
        for p in range(4):
            fill_window(even_window, 4 * side + p, arranged, 4 * side + p, t, count)
        edge(even_window, t)

    rims(count, offset, other_count, beside)
    fill(even_window, 0)
    lax.fori_loop(0, count // 2, pair, 0)


def main_kernel(
    foot_ref,
    part_ref,
    halo_ref,
    near_ref,
    m1_ref,
    m2_ref,
    down_mat,
    back_mat,
    head_ref,
    label_ref,
    keep_ref,
    send_ref,
    arranged,
    even_window,
    odd_window,
    hidden,
    hwin,
    headm_ref,
    y2_ref,
    delta_t,
    err_t,
    grad,
    grad_down,
    small,
    whole,
):
    reps, chans = lax.axis_size("rep"), lax.axis_size("chan")
    columns = lax.axis_size("bricks") * reps
    column = lax.axis_index("bricks") * reps + lax.axis_index("rep")
    planes = BRICK // chans
    mine = lax.axis_index("chan") * planes
    side = mine // 4
    count = 2 * foot_ref[1, column]
    other_count, offset = neighbour(foot_ref, column, columns, side)

    grad[...] = jnp.zeros_like(grad)
    grad_down[...] = jnp.zeros_like(grad_down)
    small[...] = jnp.zeros_like(small)
    head_row = jnp.concatenate([head_ref[...], head_ref[...]], axis=1)
    square_row = lax.broadcasted_iota(jnp.int32, (128, 128), 0)
    square_lane = lax.broadcasted_iota(jnp.int32, (128, 128), 1)
    same_half = (square_row < 64) == (square_lane < 64)
    head_mat = jnp.where(same_half, jnp.broadcast_to(head_row, (128, 128)).T, 0.0)
    head_high = head_mat.astype(BF16)
    headm_ref[0:128] = head_high
    headm_ref[128:256] = head_high
    headm_ref[256:384] = (head_mat - head_high.astype(F32)).astype(BF16)
    pick_depth = jnp.where(square_row // 2 == square_lane % 64, 1.0, 0.0).astype(BF16)

    def turn(t, carry):
        for p in range(4):
            turn_block(halo_ref, arranged, p, t)
        return carry

    lax.fori_loop(0, other_count, turn, 0)

    def fill(window, t):
        for p in range(4):
            fill_window(window, p, arranged, p, t - offset, other_count)

    def first(window, t):
        own = (t >= 0) & (t < count)
        next_to = (t - offset >= 0) & (t - offset < other_count)
        out = part_ref[t + 1] + conv_rows(plane_pairs(window, 0, 2), half_mats(m1_ref, side))
        out = jnp.maximum(out, 0.0).astype(BF16)
        for rx in range(2):
            live = jnp.where(side == rx, next_to, own)
            for par in range(2):
                block = out[ROWS * par : ROWS * par + ROWS, 128 * rx : 128 * rx + 128]
                hidden[t + 1, side * 4 + 2 * rx + par] = jnp.where(live, block, jnp.zeros_like(block))

    def near(t):
        for p in range(4):
            hidden[t + 1, (1 - side) * 4 + p] = gated(near_ref, p, t, count)

    def beside(t):
        fill(even_window, t)
        first(even_window, t)

    def pair(j, carry):
        fill(odd_window, 2 * j + 1)
        near(2 * j)
        first(even_window, 2 * j)
        fill(even_window, 2 * j + 2)
        near(2 * j + 1)
        first(odd_window, 2 * j + 1)
        return carry

    hidden[0] = jnp.zeros((8, ROWS, 128), BF16)
    hidden[count + 1] = jnp.zeros((8, ROWS, 128), BF16)
    rims(count, offset, other_count, beside)
    fill(even_window, 0)
    lax.fori_loop(0, count // 2, pair, 0)

    row4 = lax.broadcasted_iota(jnp.int32, (512, 128), 0)
    even4 = row4 % 2 == 0
    plane4 = 4 * side + 2 * (row4 // 128 % 2)
    keep = even4 & (plane4 >= mine) & (plane4 < mine + planes)

    def second(j, carry):
        for u in range(2):
            t = 2 * j + u
            for p in range(8):
                hwin[u, p, :, 0:128] = hidden[t + 1, p]
                hwin[u, p, :, 128:256] = merge_half(hidden[t + 2, p], hidden[t, p])
            out = conv_rows(plane_pairs(hwin, 0, 4, (u,)), [m2_ref[e] for e in range(3)])
            out = jnp.maximum(out, 0.0).astype(BF16)
            for par in range(2):
                for rx in range(2):
                    y2_ref[u, rx, par] = out[ROWS * par : ROWS * par + ROWS, 128 * rx : 128 * rx + 128]
        fine = jnp.concatenate(
            [
                jnp.concatenate(
                    [y2_ref[u, rx, a, 128 * b : 128 * b + 128] for u in range(2) for rx in range(2)],
                    axis=0,
                )
                for a in range(2)
                for b in range(2)
            ],
            axis=1,
        )
        both = jnp.dot(fine, down_mat[...], preferred_element_type=F32)
        coarse = both[:, 0:128] + shifted(both[:, 128:256], -1)
        rect = jnp.maximum(coarse, 0.0)
        high = rect.astype(BF16)
        rest = (rect - high.astype(F32)).astype(BF16)
        logit = jnp.dot(
            jnp.concatenate([high, rest, high], axis=1), headm_ref[...], preferred_element_type=F32
        )
        labels = []
        for u in range(2):
            line = label_ref[:, pl.ds(pl.multiple_of(256 * j + 128 * u, 128), 128)].astype(F32)
            for rx in range(2):
                row = jnp.where(side == 1, line[2 + rx : 3 + rx], line[rx : rx + 1])
                row = jnp.where(same_half, jnp.broadcast_to(row, (128, 128)), 0.0).astype(BF16)
                labels.append(
                    lax.dot_general(
                        pick_depth, row, (((1,), (1,)), ((), ())), preferred_element_type=F32
                    )
                )
        label = jnp.concatenate(labels, axis=0)
        tail = jnp.exp(-jnp.abs(logit))
        soft = jnp.maximum(logit, 0.0) + jnp.log1p(tail)
        sigmoid = jnp.where(logit >= 0.0, 1.0, tail) / (1.0 + tail)
        loss = jnp.where(keep, soft - label * logit, 0.0)
        slope = jnp.where(keep, (sigmoid - label) * (1.0 / COARSE), 0.0)
        small[0:1] += jnp.sum(slope * rect, axis=0, keepdims=True)
        small[1:2] += jnp.sum(loss, axis=0, keepdims=True)
        delta = jnp.where(coarse > 0.0, slope * head_row, 0.0).astype(BF16).astype(F32)
        moved = shifted(delta, 1)
        delta_t[0:128] = delta.astype(BF16).T
        delta_t[128:256] = moved.astype(BF16).T
        back = jnp.dot((delta + moved).astype(BF16), back_mat[...], preferred_element_type=F32)
        for a in range(2):
            for b in range(2):
                lane = (2 * a + b) * 256
                err = jnp.where(even4, back[:, lane : lane + 128], back[:, lane + 128 : lane + 256])
                live = fine[:, lane // 2 : lane // 2 + 128].astype(F32) > 0.0
                err = jnp.where(live, err, 0.0)
                for n in range(4):
                    turned = err[128 * n : 128 * n + 128].astype(BF16).T
                    row = 384 * (1 - n % 2)
                    col = n // 2 * 512 + a * 256 + b * 128
                    err_t[row + 128 : row + 256, col : col + 128] = turned
                    up = jnp.where(square_lane < 126, pltpu.roll(turned, 126, 1), jnp.zeros_like(turned))
                    down = jnp.where(square_lane >= 2, pltpu.roll(turned, 2, 1), jnp.zeros_like(turned))
                    err_t[row : row + 128, col : col + 128] = up
                    err_t[row + 256 : row + 384, col : col + 128] = down
        grad_down[...] += jnp.dot(delta_t[...], fine, preferred_element_type=F32)
        for k in range(4):
            rows = hwin[:, 2 * k : 2 * k + 2].reshape(4 * ROWS, 256)
            lower, upper = (384, 768) if k == 0 else (0, 384) if k == 3 else (0, 768)
            part = jnp.dot(err_t[lower:upper], rows, preferred_element_type=F32)
            if k > 0:
                grad[k - 1] += part[0:384]
            if k < 3:
                grad[k] += part[upper - lower - 384 :]
        return carry

    lax.fori_loop(0, count // 2, second, 0)

    low = lanes_low((64, 128))
    rep, chan = lax.axis_index("rep"), lax.axis_index("chan")
    share = 64 // chans // reps

    def emit(slab, value):
        whole[slab] = value

    firsts = []
    for a in range(3):
        for e in range(3):
            both = grad[a, 128 * e : 128 * e + 64] + pltpu.roll(
                grad[a, 128 * e + 64 : 128 * e + 128], 192, 1
            )
            emit(3 * a + e, both[:, 0:128])
            firsts.append(both[:, 128:256])
    for m in range(5):
        right = firsts[2 * m + 1] if 2 * m + 1 < 9 else jnp.zeros_like(firsts[0])
        emit(9 + m, jnp.where(low, pltpu.roll(firsts[2 * m], 64, 1), right))
    halves = [
        grad_down[128 * e : 128 * e + 64] + pltpu.roll(grad_down[128 * e + 64 : 128 * e + 128], 448, 1)
        for e in range(2)
    ]
    for ab in range(4):
        tile = jnp.concatenate([half[:, 128 * ab : 128 * ab + 128] for half in halves], axis=0)
        emit(14 + ab, tile.T[0:64])
    sums = small[...]
    head = sums[0:1] + pltpu.roll(sums, 64, 1)[0:1]
    total = jnp.sum(sums[1:2], axis=1, keepdims=True) * (1.0 / 64)
    row = merge_half(head, jnp.broadcast_to(total, (1, 128)))
    emit(18, jnp.broadcast_to(row, (64, 128)))
    for c in range(chans):
        place = lax.rem(c - chan + chans, chans)
        for ref, r in ((keep_ref, rep), (send_ref, 1 - rep)):
            rows = pl.ds(pl.multiple_of((c * reps + r) * share, share), share)
            ref[place] = whole[:, rows, :]


def final_kernel(foot_ref, mine_ref, peer_ref, second_ref, down_ref, head_ref, loss_ref):
    rep = lax.axis_index("rep")
    share = mine_ref.shape[1]
    for ref, r in ((mine_ref, rep), (peer_ref, 1 - rep)):
        rows = pl.ds(pl.multiple_of(r * share, share), share)
        for a in range(3):
            for e in range(3):
                m = 3 * a + e
                later, first = ref[m], ref[9 + m // 2]
                second_ref[9 * a + e, rows] = first[:, 64 * (m % 2) : 64 * (m % 2) + 64]
                second_ref[9 * a + 3 + e, rows] = later[:, 0:64]
                second_ref[9 * a + 6 + e, rows] = later[:, 64:128]
        for ab in range(4):
            for e in range(2):
                down_ref[2 * ab + e, rows] = ref[14 + ab][:, 64 * e : 64 * e + 64]
    line = mine_ref[18][0:1]
    head_ref[...] = line[:, 0:64]
    live = foot_ref[1, 0]
    for c in range(1, foot_ref.shape[1]):
        live += foot_ref[1, c]
    scale = jnp.full((1, 1), COARSE * live, jnp.int32).astype(F32)
    loss_ref[...] = line[:, 64:65] / scale


def sums_slab(shape):
    return lax.broadcasted_iota(jnp.int32, shape, 0) == 18


def to_wire(value):
    high = lax.reduce_precision(value, 8, 7)
    rest = lax.reduce_precision(value - high, 8, 7)
    lower = lax.broadcasted_iota(jnp.int32, value.shape, 1) >= value.shape[1] // 2
    return jnp.where(sums_slab(value.shape) & lower, rest, high)


def from_wire(value):
    half = value.shape[1] // 2
    other = jnp.concatenate([value[:, half:], value[:, :half]], axis=1)
    return value + jnp.where(sums_slab(value.shape), other, 0.0)


def shards(features, w_first, w_second, w_down, w_head, footprint, labels):
    bricks, chans, reps = lax.axis_size("bricks"), lax.axis_size("chan"), lax.axis_size("rep")
    planes = BRICK // chans
    side = lax.axis_index("chan") * planes // 4
    smem = pl.BlockSpec(memory_space=pltpu.SMEM)
    vmem = pl.BlockSpec(memory_space=pltpu.VMEM)
    features = features[0]
    slabs = features.shape[2] // 4

    packs = pl.pallas_call(
        pack_kernel,
        out_shape=(
            jax.ShapeDtypeStruct((27, 32 // chans, 128), BF16),
            jax.ShapeDtypeStruct((35, 32 // chans, 128), BF16),
        ),
        in_specs=[vmem] * 3,
        out_specs=(vmem, vmem),
        compiler_params=pltpu.CompilerParams(vmem_limit_bytes=16 << 20),
        name="pack",
    )(w_first.transpose(0, 2, 1), w_second.transpose(0, 2, 1), w_down)
    pieces = [[packed] for packed in packs]
    for packed, gathered in zip(packs, pieces):
        for step in range(1, chans):
            ring = [(i, (i + step) % chans) for i in range(chans)]
            gathered.append(lax.ppermute(packed, "chan", ring))

    pairs = []
    for col in range(bricks * reps):
        for c in range(chans):
            src = col + 2 * (c * planes // 4) - 1
            if 0 <= src < bricks * reps:
                ends = [(j // reps * chans + c) * reps + j % reps for j in (src, col)]
                pairs.append(tuple(ends))
    outward = lax.dynamic_slice_in_dim(features, (1 - side) * 4, 4, 1).transpose(1, 2, 0, 3)
    halo = lax.ppermute(outward, ("bricks", "chan", "rep"), pairs)

    part, near, mat1 = pl.pallas_call(
        local_kernel,
        out_shape=(
            jax.ShapeDtypeStruct((slabs + 2, 2 * ROWS, 256), F32),
            jax.ShapeDtypeStruct((4, slabs, ROWS, 128), BF16),
            jax.ShapeDtypeStruct((3, 1024, 256), BF16),
        ),
        in_specs=[smem] + [vmem] * (1 + chans),
        out_specs=(vmem,) * 3,
        scratch_shapes=[
            pltpu.VMEM((27, 64, 128), BF16),
            pltpu.VMEM((27, 64, 128), BF16),
            pltpu.VMEM((8, slabs, ROWS, 128), BF16),
            pltpu.VMEM((8, ROWS, 256), BF16),
            pltpu.VMEM((8, ROWS, 256), BF16),
        ],
        compiler_params=pltpu.CompilerParams(vmem_limit_bytes=36 << 20),
        cost_estimate=pl.CostEstimate(flops=6 * 6 * 512 * 1024 * 512, bytes_accessed=8 << 20, transcendentals=0),
        name="first_local",
    )(footprint, features.transpose(1, 2, 0, 3), *pieces[0])
    mat2, down_mat, back_mat = pl.pallas_call(
        mats_kernel,
        out_shape=(
            jax.ShapeDtypeStruct((3, 1024, 256), BF16),
            jax.ShapeDtypeStruct((512, 256), BF16),
            jax.ShapeDtypeStruct((128, 1024), BF16),
        ),
        in_specs=[pl.BlockSpec(memory_space=pl.ANY)] + [vmem] * chans,
        out_specs=(vmem,) * 3,
        scratch_shapes=[pltpu.VMEM((35, 64, 128), BF16), pltpu.VMEM((27, 64, 128), BF16)],
        compiler_params=pltpu.CompilerParams(vmem_limit_bytes=16 << 20),
        name="mats",
    )(near, *pieces[1])
    parts = jax.ShapeDtypeStruct((chans, 19, 64 // chans // reps, 128), F32)
    keep, send = pl.pallas_call(
        main_kernel,
        out_shape=(parts, parts),
        in_specs=[smem] + [vmem] * 9,
        out_specs=(vmem, vmem),
        scratch_shapes=[
            pltpu.VMEM((4, slabs, ROWS, 128), BF16),
            pltpu.VMEM((4, ROWS, 256), BF16),
            pltpu.VMEM((4, ROWS, 256), BF16),
            pltpu.VMEM((slabs + 2, 8, ROWS, 128), BF16),
            pltpu.VMEM((2, 8, ROWS, 256), BF16),
            pltpu.VMEM((384, 128), BF16),
            pltpu.VMEM((2, 2, 2, ROWS, 128), BF16),
            pltpu.VMEM((256, 512), BF16),
            pltpu.VMEM((768, 1024), BF16),
            pltpu.VMEM((3, 384, 256), F32),
            pltpu.VMEM((256, 512), F32),
            pltpu.VMEM((8, 128), F32),
            pltpu.VMEM((19, 64, 128), F32),
        ],
        compiler_params=pltpu.CompilerParams(vmem_limit_bytes=40 << 20),
        cost_estimate=pl.CostEstimate(flops=4 * 6 * 6 * 512 * 1024 * 512, bytes_accessed=16 << 20, transcendentals=0),
        name="head_and_grads",
    )(footprint, part, halo, near, mat1, mat2, down_mat, back_mat, w_head.reshape(1, 64), labels[0])

    swap = [(i, 1 - i) for i in range(reps)]
    got = lax.ppermute(send, "rep", swap)
    wire = [to_wire(keep[step] + got[step]) for step in range(chans)]
    near_sums = []
    for flip in range(2):
        for step in range(chans):
            if flip == step == 0:
                near_sums.append(wire[0])
                continue
            routes = [
                (b * chans + c, (b ^ flip) * chans + (c + step) % chans)
                for b in range(bricks)
                for c in range(chans)
            ]
            sent = lax.ppermute(wire[step].astype(BF16), ("bricks", "chan"), routes)
            near_sums.append(sent.astype(F32))
    mine = from_wire(sum(near_sums[1:chans], near_sums[0]) + sum(near_sums[chans + 1 :], near_sums[chans]))
    step = 2
    while step < bricks:
        wire = to_wire(mine)
        sent = lax.ppermute(wire.astype(BF16), "bricks", [(i, i ^ step) for i in range(bricks)])
        mine = from_wire(wire + sent.astype(F32))
        step *= 2
    peer = lax.ppermute(mine, "rep", swap)
    share = 64 // chans
    second, down, head, loss = pl.pallas_call(
        final_kernel,
        out_shape=(
            jax.ShapeDtypeStruct((27, share, 64), F32),
            jax.ShapeDtypeStruct((8, share, 64), F32),
            jax.ShapeDtypeStruct((1, 64), F32),
            jax.ShapeDtypeStruct((1, 1), F32),
        ),
        in_specs=[smem, vmem, vmem],
        out_specs=(vmem,) * 4,
        compiler_params=pltpu.CompilerParams(vmem_limit_bytes=16 << 20),
        name="assemble",
    )(footprint, mine, peer)
    return second.transpose(0, 2, 1), down, head.reshape(64), loss.reshape(1)


def solution(mesh):
    return jax.shard_map(
        shards,
        mesh=mesh,
        in_specs=(
            P(("groups", "bricks", "rep"), None, None, None, None),
            P(None, None, "chan"),
            P(None, None, "chan"),
            P(None, "chan", None),
            P(),
            P(None, "groups"),
            P(("groups", "bricks", "rep"), None, None),
        ),
        out_specs=(P("groups", None, "chan"), P("groups", "chan", None), P("groups"), P("groups")),
        check_vma=False,
    )
```
